32 devices in a mesh: dp: 16 (over z, y, core), tensor: 2 (over x).
Axes of the slice: x: 2, y: 2, z: 4, core: 2. Of those that a mesh axis runs over, the one named last changes fastest.
Arguments:
- x_in: bfloat16 [32768, 768], P(('dp', 'tensor')), may hold values from -6 to 6
- lengths: int32 [32], P('dp'), may hold values from 256 to 1024, as said below
- cotangent: bfloat16 [32768, 768], P(('dp', 'tensor')), may hold values from -6 to 6
- w_query: bfloat16 [768, 768], P('dp', 'tensor'), may hold values from -0.5 to 0.5
- w_key: bfloat16 [768, 768], P('dp', 'tensor'), may hold values from -0.5 to 0.5
- w_value: bfloat16 [768, 768], P('dp', 'tensor'), may hold values from -0.21875 to 0.21875
- w_out: bfloat16 [768, 768], P('tensor', 'dp'), may hold values from -0.21875 to 0.21875
- w_in: bfloat16 [768, 3072], P('dp', 'tensor'), may hold values from -0.21875 to 0.21875
- w_down: bfloat16 [3072, 768], P('tensor', 'dp'), may hold values from -0.109375 to 0.109375
- conv_weight: float32 [12, 33], P('tensor'), may hold values from -1 to 1
- ln1_gain: float32 [768], P(('dp', 'tensor')), may hold values from 0.5 to 1.5
- ln1_bias: float32 [768], P(('dp', 'tensor')), may hold values from -1.8 to 1.8
- ln2_gain: float32 [768], P(('dp', 'tensor')), may hold values from 0.5 to 1.5
- ln2_bias: float32 [768], P(('dp', 'tensor')), may hold values from -1.8 to 1.8
Outputs:
- output: bfloat16 [32768, 768], P(('dp', 'tensor'))
- input_grad: bfloat16 [32768, 768], P(('dp', 'tensor'))
- grad_query: float32 [768, 768], P('dp', 'tensor')
- grad_key: float32 [768, 768], P('dp', 'tensor')
- grad_value: float32 [768, 768], P('dp', 'tensor')
- grad_out: float32 [768, 768], P('tensor', 'dp')
- grad_in: float32 [768, 3072], P('dp', 'tensor')
- grad_down: float32 [3072, 768], P('tensor', 'dp')
- grad_conv: float32 [12, 33], P('tensor')
- grad_ln1_gain: float32 [768], P(('dp', 'tensor'))
- grad_ln1_bias: float32 [768], P(('dp', 'tensor'))
- grad_ln2_gain: float32 [768], P(('dp', 'tensor'))
- grad_ln2_bias: float32 [768], P(('dp', 'tensor'))
- stats: float32 [3], replicated
The draws below stay inside these ranges and needn't reach their ends.
Inputs may be any that keep to these rules, and one draw needn't show every extreme that they name: `lengths`: the valid tokens of a sequence are its first ones; in every draw some sequence fills all 1024 slots.
All inputs are finite; a program needn't handle non-finite values.
Results may differ from the reference program's by a relative error of at most 0.017.
Values may be sent and summed in bfloat16 or wider, within the bound.
A program may use at most 320 MiB of HBM per device.

```python
import jax
import jax.numpy as jnp
from jax import lax

D = 768
HEADS = 12
FF = 3072
LANDMARKS = 64
CONV = 33
PINV_STEPS = 6
SLOT = 1024
SEQS = 32
TOKENS = 32768
MIN_LEN = 256


def draw_lengths(key, part):
    first_key = jax.random.fold_in(key, 11)
    second_key = jax.random.fold_in(key, 23)
    drawn = jax.random.randint(first_key, (SEQS,), MIN_LEN, SLOT + 1)
    chosen = jax.random.randint(second_key, (), 0, SEQS)
    drawn = jnp.where(jnp.arange(SEQS) == chosen, SLOT, drawn)
    return drawn.astype(jnp.int32)


def levels(stream_key, extent, shards, least, high):
    def one(dim, blocks):
        heights = jax.random.uniform(jax.random.fold_in(jax.random.fold_in(stream_key, 6), dim), (blocks,), jnp.float32, least / len(shards), high / len(shards))
        return jnp.repeat(jnp.exp(heights), extent[dim] // blocks).reshape((-1,) + (1,) * (len(extent) - dim - 1))

    factor_of = one(*shards[0])
    for cut in shards[1:]:
        factor_of = factor_of * one(*cut)
    return factor_of


def scatter_about(key, dims, width, limit, cuts=(), kind=jnp.bfloat16):
    gain = levels(key, dims, cuts, -0.22, 0.18) if cuts else 1.0
    array = jax.random.normal(key, dims, jnp.float32) * width * gain
    return jnp.minimum(jnp.maximum(array, -limit), limit).astype(kind)


def setup_inputs(seed: int = 0) -> dict:
    key_of = jax.random.split(jax.random.key(seed), 15)
    x_in = scatter_about(key_of[0], (TOKENS, D), 1.0, 6.0, ((0, 32),))
    lengths = draw_lengths(jax.random.fold_in(key_of[14], 71), 0)
    cotangent = scatter_about(key_of[2], (TOKENS, D), 1.0, 6.0, ((0, 32),))
    w_query = scatter_about(key_of[3], (D, D), (D // 6) ** -0.5, 0.5, ((0, 16), (1, 2)))
    w_key = scatter_about(key_of[4], (D, D), (D // 6) ** -0.5, 0.5, ((0, 16), (1, 2)))
    w_value = scatter_about(key_of[5], (D, D), D ** -0.5, 0.21875, ((0, 16), (1, 2)))
    w_out = scatter_about(key_of[6], (D, D), D ** -0.5, 0.21875, ((0, 2), (1, 16)))
    w_in = scatter_about(key_of[7], (D, FF), D ** -0.5, 0.21875, ((0, 16), (1, 2)))
    w_down = scatter_about(key_of[8], (FF, D), FF ** -0.5, 0.109375, ((0, 2), (1, 16)))
    conv_weight = scatter_about(key_of[9], (HEADS, CONV), CONV ** -0.5, 1.0, ((0, 2),), jnp.float32)
    ln1_gain = jnp.clip(1.0 + 0.1 * jax.random.normal(key_of[10], (D,), jnp.float32), 0.5, 1.5)
    ln1_bias = scatter_about(key_of[11], (D,), 0.3, 1.8, ((0, 32),), jnp.float32)
    ln2_gain = jnp.clip(1.0 + 0.1 * jax.random.normal(key_of[12], (D,), jnp.float32), 0.5, 1.5)
    ln2_bias = scatter_about(key_of[13], (D,), 0.3, 1.8, ((0, 32),), jnp.float32)
    return dict(x_in=x_in, lengths=lengths, cotangent=cotangent, w_query=w_query, w_key=w_key, w_value=w_value, w_out=w_out, w_in=w_in, w_down=w_down, conv_weight=conv_weight, ln1_gain=ln1_gain, ln1_bias=ln1_bias, ln2_gain=ln2_gain, ln2_bias=ln2_bias)


@jax.custom_vjp
def low(v):
    return lax.optimization_barrier(v.astype(jnp.bfloat16)).astype(jnp.float32)

@jax.custom_vjp
def low_back(v):
    return v

def low_keep(v):
    return (low(v), None)

def low_pass(kept, grad):
    return (grad,)

def back_keep(v):
    return (v, None)

def back_low(kept, grad):
    return (low(grad),)
low.defvjp(low_keep, low_pass)
low_back.defvjp(back_keep, back_low)

def matmul_hi(left_op, right_op):
    return jnp.dot(left_op, right_op, precision=lax.Precision.HIGHEST, preferred_element_type=jnp.float32)

def exact_einsum_product(formula, left_op, right_op):
    return jnp.einsum(formula, left_op, right_op, precision=lax.Precision.HIGHEST)

def layer_norm(values, gain_vec, shift_vec):
    centre = values - lax.optimization_barrier(jnp.mean(values, axis=-1, keepdims=True))
    spread = lax.optimization_barrier(jnp.mean(centre * centre, axis=-1, keepdims=True))
    return centre * lax.rsqrt(spread + 1e-05) * gain_vec + shift_vec

def iterative_pseudo_inverse(matrix):
    identity_mat = jnp.eye(matrix.shape[-1], dtype=matrix.dtype)
    column_sums = lax.optimization_barrier(jnp.sum(matrix, axis=-2))
    largest = lax.optimization_barrier(jnp.max(column_sums, axis=-1))
    inverse = jnp.swapaxes(matrix, -1, -2) / largest[:, None, None]
    for sweep_no in range(PINV_STEPS):
        product = exact_einsum_product('hij,hjk->hik', matrix, inverse)
        inner_term = 7.0 * identity_mat - product
        inner_term = 15.0 * identity_mat - exact_einsum_product('hij,hjk->hik', product, inner_term)
        inner_term = 13.0 * identity_mat - exact_einsum_product('hij,hjk->hik', product, inner_term)
        inverse = exact_einsum_product('hij,hjk->hik', 0.25 * inverse, inner_term)
    return inverse

def nystrom(queries, keys_in, values_in, valid_mask, conv_taps):
    length = queries.shape[0]
    head_count = conv_taps.shape[0]
    head_width = queries.shape[1] // head_count
    scale_factor = head_width ** (-0.25)

    def split_heads(tensor):
        return tensor.reshape(length, head_count, head_width).transpose(1, 0, 2)
    query_heads = split_heads(queries * valid_mask[:, None] * scale_factor)
    key_heads = split_heads(keys_in * valid_mask[:, None] * scale_factor)
    value_heads = split_heads(values_in * valid_mask[:, None])
    query_landmark_rows = lax.optimization_barrier(jnp.mean(query_heads.reshape(head_count, LANDMARKS, length // LANDMARKS, head_width), axis=2))
    key_landmark_rows = lax.optimization_barrier(jnp.mean(key_heads.reshape(head_count, LANDMARKS, length // LANDMARKS, head_width), axis=2))
    kernel_one = jax.nn.softmax(exact_einsum_product('hsd,hld->hsl', query_heads, key_landmark_rows), axis=-1)
    landmark_kernel_matrix = jax.nn.softmax(exact_einsum_product('sux,sgx->sug', query_landmark_rows, key_landmark_rows), axis=-1)
    scores = exact_einsum_product('hld,hsd->hls', query_landmark_rows, key_heads)
    scores = jnp.where(valid_mask[None, None, :] > 0.5, scores, -1000000000.0)
    kernel_three = jax.nn.softmax(scores, axis=-1)
    result_overview = exact_einsum_product('hls,hsd->hld', kernel_three, value_heads)
    result_overview = exact_einsum_product('fba,fau->fbu', iterative_pseudo_inverse(landmark_kernel_matrix), result_overview)
    mixture = exact_einsum_product('hsl,hld->hsd', kernel_one, result_overview)
    half_taps = conv_taps.shape[1] // 2
    padded = jnp.pad(value_heads, ((0, 0), (half_taps, half_taps), (0, 0)))
    for offset in range(conv_taps.shape[1]):
        mixture = mixture + conv_taps[:, offset, None, None] * padded[:, offset:offset + length, :]
    return mixture.transpose(1, 0, 2).reshape(length, head_count * head_width)

def reference(x_in, lengths, cotangent, w_query, w_key, w_value, w_out, w_in, w_down, conv_weight, ln1_gain, ln1_bias, ln2_gain, ln2_bias):
    positions = jnp.arange(SLOT, dtype=jnp.int32)
    seq_mask = (positions[None, :] < lengths[:, None].astype(jnp.int32)).astype(jnp.float32)
    flat_mask = seq_mask.reshape(-1)

    def forward(tokens, query_weight, key_weight, value_weight, out_weight, in_weight, down_weight, conv_taps, gain_one, bias_one, gain_two, bias_two):
        queries = low_back(matmul_hi(tokens, query_weight))
        keys_all = low_back(matmul_hi(tokens, key_weight))
        values_all = low_back(matmul_hi(tokens, value_weight))

        def one_sequence(pieces):
            return nystrom(pieces[0], pieces[1], pieces[2], pieces[3], conv_taps)
        context = lax.map(jax.checkpoint(one_sequence), (queries.reshape(SEQS, SLOT, D), keys_all.reshape(SEQS, SLOT, D), values_all.reshape(SEQS, SLOT, D), seq_mask))
        context = low(context.reshape(SEQS * SLOT, D))
        attn_branch = low_back(matmul_hi(context, out_weight))
        hidden = low(layer_norm(tokens + attn_branch, gain_one, bias_one))
        pre_act = low_back(matmul_hi(hidden, in_weight))
        act_val = low(jax.nn.gelu(pre_act, approximate=False))
        ffn_branch = low_back(matmul_hi(act_val, down_weight))
        result = layer_norm(hidden + ffn_branch, gain_two, bias_two)
        return (result, (attn_branch, ffn_branch))
    tokens = x_in.astype(jnp.float32)
    inputs = (tokens, w_query.astype(jnp.float32), w_key.astype(jnp.float32), w_value.astype(jnp.float32), w_out.astype(jnp.float32), w_in.astype(jnp.float32), w_down.astype(jnp.float32), conv_weight.astype(jnp.float32), ln1_gain.astype(jnp.float32), ln1_bias.astype(jnp.float32), ln2_gain.astype(jnp.float32), ln2_bias.astype(jnp.float32))
    result, pullback, branches = jax.vjp(forward, *inputs, has_aux=True)
    grads = pullback(cotangent.astype(jnp.float32) * flat_mask[:, None])
    count = jnp.sum(flat_mask)

    def root_mean(data):
        return jnp.sqrt(jnp.sum(flat_mask[:, None] * data * data) / (count * D))
    stats = jnp.stack([root_mean(tokens), root_mean(branches[0]), root_mean(branches[1])])
    return (result.astype(jnp.bfloat16), grads[0].astype(jnp.bfloat16), grads[1], grads[2], grads[3], grads[4], grads[5], grads[6], grads[7], grads[8], grads[9], grads[10], grads[11], stats)
```

```python
from functools import partial

import jax
import jax.numpy as jnp
from jax import lax
from jax.experimental import pallas as pl
from jax.experimental.pallas import tpu as pltpu
from jax.sharding import PartitionSpec as P

F32, BF = jnp.float32, jnp.bfloat16
NN, NT, TN = ((1,), (0,)), ((1,), (1,)), ((0,), (0,))
MARKS = 64
HEAD = 64
PACK = 4
WIDE = PACK * HEAD
TAPS = 33
EDGE = TAPS // 2
ROWS = 128
WINDOW = ROWS + 2 * EDGE
STEPS = 6
KEPT = 4


def mm(a, b, dims=NN):
    return lax.dot_general(a, b, (dims, ((), ())), preferred_element_type=F32)


def halves(a):
    high = a.astype(BF)
    return high, (a - high.astype(F32)).astype(BF)


def mm3(a, b, dims=NN):
    (ah, al), (bh, bl) = a, b
    return mm(ah, bh, dims) + (mm(ah, bl, dims) + mm(al, bh, dims))


def mm3f(a, b, dims=NN):
    return mm3(halves(a), halves(b), dims)


def grid_of(shape):
    return (
        lax.broadcasted_iota(jnp.int32, shape, 0),
        lax.broadcasted_iota(jnp.int32, shape, 1),
    )


def block_mask():
    row, col = grid_of((WIDE, WIDE))
    return row // HEAD == col // HEAD


def eye():
    row, col = grid_of((WIDE, WIDE))
    return (row == col).astype(F32)


def spread(packed, mask):
    full = jnp.concatenate([packed] * PACK, axis=0)
    return jnp.where(mask, full, jnp.zeros_like(full))


def gather_up(full):
    return sum(full[i * MARKS : (i + 1) * MARKS] for i in range(PACK))


def segment_reduce(a, fill, op):
    lane = lax.broadcasted_iota(jnp.int32, (a.shape[0], 128), 1) < HEAD
    parts = []
    for tile in range(a.shape[1] // 128):
        piece = a[:, tile * 128 : (tile + 1) * 128]
        low = op(jnp.where(lane, piece, fill), axis=1, keepdims=True)
        high = op(jnp.where(lane, fill, piece), axis=1, keepdims=True)
        parts.append(jnp.where(lane, low, high))
    return jnp.concatenate(parts, axis=1)


def average_matrix():
    row, col = grid_of((ROWS * MARKS // 1024, ROWS))
    return jnp.where(row == col // 16, 1.0 / 16, 0.0).astype(BF)


def average_back():
    row, col = grid_of((ROWS, ROWS * MARKS // 1024))
    return jnp.where(row // 16 == col, 1.0 / 16, 0.0).astype(BF)


def lanes_of(group):
    return slice(group * WIDE, (group + 1) * WIDE)


def toeplitz(taps_ref, group):
    parts = []
    for i in range(PACK):
        head = group * PACK + i
        line = jnp.broadcast_to(taps_ref[head : head + 1, :], (ROWS, 256))
        parts.append(pltpu.roll(line, 0, 1, stride=1, stride_axis=0)[:, :WINDOW])
    return jnp.concatenate(parts, axis=0).astype(BF)


def diagonal_lanes(stacked):
    col = lax.broadcasted_iota(jnp.int32, (ROWS, WIDE), 1) // HEAD
    out = stacked[:ROWS]
    for i in range(1, PACK):
        out = jnp.where(col == i, stacked[i * ROWS : (i + 1) * ROWS], out)
    return out


def attn_fwd_kernel(slot, groups, len_ref, q_ref, k_ref, v_ref, taps_ref,
                    ctx_ref, qh_ref, kh_ref, vp_ref, k1_ref, k3_ref,
                    small_ref, chain_ref,
                    z_ref, k2_ref, s_ref, top_ref, t_ref):
    count = slot // ROWS
    marks = ROWS // 16
    scale = HEAD ** -0.25
    length = len_ref[0]
    avg = average_matrix()
    wide = groups * WIDE
    vp_ref[0:EDGE, :] = jnp.zeros((EDGE, wide), BF)
    vp_ref[slot + EDGE : slot + 2 * EDGE, :] = jnp.zeros((EDGE, wide), BF)

    def load(i, carry):
        rows = pl.ds(pl.multiple_of(i * ROWS, ROWS), ROWS)
        row = lax.broadcasted_iota(jnp.int32, (ROWS, 1), 0) + i * ROWS
        valid = (row < length).astype(F32)
        few = pl.ds(pl.multiple_of(i * marks, marks), marks)
        q = q_ref[rows, :] * (valid * scale)
        high, low = halves(q)
        qh_ref[rows, :] = high
        small_ref[0, few, :] = mm(avg, high) + mm(avg, low)
        k = k_ref[rows, :] * (valid * scale)
        high, low = halves(k)
        kh_ref[rows, :] = high
        small_ref[1, few, :] = mm(avg, high) + mm(avg, low)
        vp_ref[pl.ds(pl.multiple_of(i * ROWS + EDGE, EDGE), ROWS), :] = (
            v_ref[rows, :] * valid
        ).astype(BF)
        return carry

    lax.fori_loop(0, count, load, 0)
    mask = block_mask()
    one = eye()

    for g in range(groups):
        at = lanes_of(g)
        ql, kl = spread(small_ref[0, :, at], mask), spread(small_ref[1, :, at], mask)
        a2 = jnp.where(mask, mm3f(ql, kl, NT), -1e30)
        e2 = jnp.where(mask, jnp.exp(a2 - jnp.max(a2, axis=1, keepdims=True)), 0.0)
        k2 = e2 / jnp.sum(e2, axis=1, keepdims=True)
        top = segment_reduce(jnp.sum(k2, axis=0, keepdims=True), -1e30, jnp.max)
        k2_ref[g] = k2
        small_ref[2, :, at] = gather_up(k2)
        z_ref[g] = jnp.transpose(k2) / top

    def newton(step, carry):
        for g in range(groups):
            at = lanes_of(g)
            z = z_ref[g]
            zs = halves(z)
            p = mm3(halves(k2_ref[g]), zs)
            ps = halves(p)
            t2 = 15.0 * one - mm3(ps, halves(7.0 * one - p))
            t3 = 13.0 * one - mm3(ps, halves(t2))
            chain_ref[step, 0, :, at] = gather_up(z)
            chain_ref[step, 1, :, at] = gather_up(p)
            chain_ref[step, 2, :, at] = gather_up(t2)
            chain_ref[step, 3, :, at] = gather_up(t3)
            z_ref[g] = 0.25 * mm3(zs, halves(t3))
        return carry

    lax.fori_loop(0, STEPS, newton, 0)

    for g in range(groups):
        at = lanes_of(g)
        ql = spread(small_ref[0, :, at], mask).astype(BF)
        top_ref[...] = jnp.full(top_ref.shape, -jnp.inf, F32)

        def scores(i, carry):
            rows = pl.ds(pl.multiple_of(i * ROWS, ROWS), ROWS)
            row = lax.broadcasted_iota(jnp.int32, (ROWS, 1), 0) + i * ROWS
            a3 = jnp.where(row < length, mm(kh_ref[rows, at], ql, NT), -1e9)
            s_ref[rows, :] = a3
            top_ref[0:1, :] = jnp.maximum(top_ref[0:1, :], jnp.max(a3, axis=0, keepdims=True))
            return carry

        lax.fori_loop(0, count, scores, 0)
        peak = top_ref[0:1, :]
        top_ref[0:1, :] = jnp.zeros((1, WIDE), F32)

        def powers(i, carry):
            rows = pl.ds(pl.multiple_of(i * ROWS, ROWS), ROWS)
            e3 = jnp.exp(s_ref[rows, :] - peak)
            s_ref[rows, :] = e3
            top_ref[0:1, :] += jnp.sum(e3, axis=0, keepdims=True)
            return carry

        lax.fori_loop(0, count, powers, 0)
        inverse = 1.0 / top_ref[0:1, :]

        def weigh(i, carry):
            rows = pl.ds(pl.multiple_of(i * ROWS, ROWS), ROWS)
            k3_ref[rows, at] = (s_ref[rows, :] * inverse).astype(BF)
            return carry

        lax.fori_loop(0, count, weigh, 0)
        b = mm(k3_ref[:, at], vp_ref[EDGE : slot + EDGE, at], TN)
        b = jnp.where(mask, b, 0.0)
        z = z_ref[g]
        c = mm3f(z, b)
        small_ref[3, :, at] = gather_up(b)
        small_ref[4, :, at] = gather_up(c)
        small_ref[5, :, at] = gather_up(z)
        t_ref[...] = toeplitz(taps_ref, g)
        cb = c.astype(BF)
        kl = spread(small_ref[1, :, at], mask).astype(BF)
        ones = mask.astype(F32).astype(BF)

        def mix(i, carry):
            rows = pl.ds(pl.multiple_of(i * ROWS, ROWS), ROWS)
            a1 = mm(qh_ref[rows, at], kl, NT)
            e1 = jnp.exp(a1 - segment_reduce(a1, -jnp.inf, jnp.max)).astype(BF)
            k1 = (e1.astype(F32) / mm(e1, ones)).astype(BF)
            k1_ref[rows, at] = k1
            window = vp_ref[pl.ds(pl.multiple_of(i * ROWS, ROWS), WINDOW), at]
            ctx_ref[rows, at] = (
                mm(k1, cb) + diagonal_lanes(mm(t_ref[...], window))
            ).astype(BF)
            return carry

        lax.fori_loop(0, count, mix, 0)


def attn_bwd_kernel(slot, groups, len_ref, g_ref, qh_ref, kh_ref, vp_ref, k1_ref, k3_ref,
                    small_ref, chain_ref, flip_ref,
                    dqkv_ref, conv_ref,
                    gp_ref, da1_ref, da3_ref, dk_ref, dz_ref, k2_ref,
                    dql_ref, dkl_ref, t_ref, acc_ref):
    count = slot // ROWS
    marks = ROWS // 16
    scale = HEAD ** -0.25
    length = len_ref[0]
    wide = groups * WIDE
    mask = block_mask()
    one = eye()
    ones = mask.astype(F32).astype(BF)
    gp_ref[0:EDGE, :] = jnp.zeros((EDGE, wide), BF)
    gp_ref[slot + EDGE : slot + 2 * EDGE, :] = jnp.zeros((EDGE, wide), BF)
    gp_ref[EDGE : slot + EDGE, :] = g_ref[...]
    col = lax.broadcasted_iota(jnp.int32, (ROWS, WIDE), 1) // HEAD
    up, across = grid_of((ROWS, ROWS))
    flip = jnp.where(up + across == ROWS - 1, 1.0, 0.0).astype(BF)

    for g in range(groups):
        at = lanes_of(g)
        c = spread(small_ref[4, :, at], mask)
        cb = c.astype(BF)

        def first(i, carry):
            rows = pl.ds(pl.multiple_of(i * ROWS, ROWS), ROWS)
            k1 = k1_ref[rows, at].astype(F32)
            dk1 = mm(g_ref[rows, at], cb, NT)
            high, low = halves(dk1 * k1)
            da1_ref[rows, at] = (k1 * (dk1 - (mm(high, ones) + mm(low, ones)))).astype(BF)
            return carry

        lax.fori_loop(0, count, first, 0)
        dc = jnp.where(mask, mm(k1_ref[:, at], g_ref[:, at], TN), 0.0)
        dkl_ref[g] = jnp.where(mask, mm(da1_ref[:, at], qh_ref[:, at], TN), 0.0)
        b = spread(small_ref[3, :, at], mask)
        z = spread(small_ref[5, :, at], mask)
        dcs = halves(dc)
        dz_ref[g] = mm3(halves(b), dcs, NT)
        db = mm3(halves(z), dcs, TN)
        dbb = db.astype(BF)
        high, low = halves(db * b)
        many = jnp.ones((8, WIDE), BF)
        total = (mm(many, high, NT) + mm(many, low, NT))[0:1, :]
        t_ref[...] = toeplitz(flip_ref, g)
        acc_ref[...] = jnp.zeros(acc_ref.shape, F32)

        def second(i, carry):
            rows = pl.ds(pl.multiple_of(i * ROWS, ROWS), ROWS)
            row = lax.broadcasted_iota(jnp.int32, (ROWS, 1), 0) + i * ROWS
            valid = (row < length).astype(F32)
            k3 = k3_ref[rows, at]
            vh = vp_ref[pl.ds(pl.multiple_of(i * ROWS + EDGE, EDGE), ROWS), at]
            dk3 = mm(vh, dbb, NT)
            da3_ref[rows, at] = (k3.astype(F32) * (dk3 - total)).astype(BF)
            window = pl.ds(pl.multiple_of(i * ROWS, ROWS), WINDOW)
            dv = mm(k3, dbb) + diagonal_lanes(mm(t_ref[...], gp_ref[window, at]))
            dqkv_ref[rows, 2 * wide + g * WIDE : 2 * wide + (g + 1) * WIDE] = (dv * valid).astype(BF)
            grad = g_ref[rows, at]
            split = jnp.concatenate(
                [jnp.where(col == h, grad, jnp.zeros_like(grad)) for h in range(PACK)], axis=0
            )
            acc_ref[:, :WINDOW] += mm(split, vp_ref[window, at], NT)
            return carry

        lax.fori_loop(0, count, second, 0)
        for h in range(PACK):
            high, low = halves(acc_ref[h * ROWS : (h + 1) * ROWS, :])
            turned = pltpu.roll(mm(flip, high) + mm(flip, low), 0, 1, stride=1, stride_axis=0)
            conv_ref[g * PACK + h : g * PACK + h + 1, :] = jnp.sum(turned, axis=0, keepdims=True)
        dql_ref[g] = jnp.where(mask, mm(da3_ref[:, at], kh_ref[:, at], TN), 0.0)
        dk_ref[g] = jnp.zeros((WIDE, WIDE), F32)
        k2_ref[g] = spread(small_ref[2, :, at], mask)

    def newton(back, carry):
        step = STEPS - 1 - back
        for g in range(groups):
            at = lanes_of(g)
            zs = halves(spread(chain_ref[step, 0, :, at], mask))
            p = spread(chain_ref[step, 1, :, at], mask)
            t2s = halves(spread(chain_ref[step, 2, :, at], mask))
            t3s = halves(spread(chain_ref[step, 3, :, at], mask))
            ps = halves(p)
            t1s = halves(7.0 * one - p)
            dzs = halves(0.25 * dz_ref[g])
            dt3 = halves(mm3(dzs, zs))
            dp = -mm3(t2s, dt3)
            dt2f = -mm3(dt3, ps)
            dt2 = halves(dt2f)
            dp = dp - mm3(t1s, dt2) + mm3(dt2, ps)
            dps = halves(dp)
            dk_ref[g] += mm3(zs, dps)
            dz_ref[g] = mm3(t3s, dzs) + mm3(dps, halves(k2_ref[g]))
        return carry

    lax.fori_loop(0, STEPS, newton, 0)

    for g in range(groups):
        at = lanes_of(g)
        k2 = k2_ref[g]
        sums = jnp.sum(k2, axis=0, keepdims=True)
        top = segment_reduce(sums, -1e30, jnp.max)
        hit = (sums == top).astype(F32)
        ties = segment_reduce(hit, 0.0, jnp.sum)
        dz0 = dz_ref[g]
        dtop = -segment_reduce(jnp.sum(dz0 * k2, axis=0, keepdims=True), 0.0, jnp.sum) / (top * top)
        dk2 = jnp.transpose(dk_ref[g]) + dz0 / top + hit * (dtop / ties)
        dk2 = jnp.where(mask, dk2, 0.0)
        da2 = k2 * (dk2 - jnp.sum(dk2 * k2, axis=1, keepdims=True))
        da2s = halves(da2)
        ql, kl = spread(small_ref[0, :, at], mask), spread(small_ref[1, :, at], mask)
        qls, kls = halves(ql), halves(kl)
        dql = gather_up(dql_ref[g] + mm3(da2s, kls))
        dkl = gather_up(dkl_ref[g] + mm3(da2s, qls, TN))
        dql_ref[g, 0:MARKS, :] = dql
        dkl_ref[g, 0:MARKS, :] = dkl
        qlb, klb = qls[0], kls[0]
        back = average_back()

        def third(i, carry):
            rows = pl.ds(pl.multiple_of(i * ROWS, ROWS), ROWS)
            few = pl.ds(pl.multiple_of(i * marks, marks), marks)
            row = lax.broadcasted_iota(jnp.int32, (ROWS, 1), 0) + i * ROWS
            valid = jnp.where(row < length, scale, 0.0)
            dq = mm(da1_ref[rows, at], klb) + mm(back, dql_ref[g, few, :].astype(BF))
            dk = mm(da3_ref[rows, at], qlb) + mm(back, dkl_ref[g, few, :].astype(BF))
            dqkv_ref[rows, g * WIDE : (g + 1) * WIDE] = (dq * valid).astype(BF)
            dqkv_ref[rows, wide + g * WIDE : wide + (g + 1) * WIDE] = (dk * valid).astype(BF)
            return carry

        lax.fori_loop(0, count, third, 0)


VM = pl.BlockSpec(memory_space=pltpu.VMEM)
SM = pl.BlockSpec(memory_space=pltpu.SMEM)
LIMIT = 60 * 1024 * 1024


def attn_fwd(length, q, k, v, taps):
    slot, wide = q.shape
    groups = wide // WIDE
    shape = jax.ShapeDtypeStruct
    return pl.pallas_call(
        partial(attn_fwd_kernel, slot, groups),
        out_shape=(
            shape((slot, wide), BF),
            shape((slot, wide), BF),
            shape((slot, wide), BF),
            shape((slot + 2 * EDGE, wide), BF),
            shape((slot, wide), BF),
            shape((slot, wide), BF),
            shape((6, MARKS, wide), F32),
            shape((STEPS, KEPT, MARKS, wide), F32),
        ),
        in_specs=[SM, VM, VM, VM, VM],
        out_specs=[VM] * 8,
        scratch_shapes=[
            pltpu.VMEM((groups, WIDE, WIDE), F32),
            pltpu.VMEM((groups, WIDE, WIDE), F32),
            pltpu.VMEM((slot, WIDE), F32),
            pltpu.VMEM((8, WIDE), F32),
            pltpu.VMEM((PACK * ROWS, WINDOW), BF),
        ],
        compiler_params=pltpu.CompilerParams(vmem_limit_bytes=LIMIT),
        name="attn_fwd",
    )(length, q, k, v, taps)


def attn_bwd(length, g, qh, kh, vp, k1, k3, small, chain, flip):
    slot, wide = g.shape
    groups = wide // WIDE
    shape = jax.ShapeDtypeStruct
    return pl.pallas_call(
        partial(attn_bwd_kernel, slot, groups),
        out_shape=(shape((slot, 3 * wide), BF), shape((16, 256), F32)),
        in_specs=[SM] + [VM] * 9,
        out_specs=[VM] * 2,
        scratch_shapes=[
            pltpu.VMEM((slot + 2 * EDGE, wide), BF),
            pltpu.VMEM((slot, wide), BF),
            pltpu.VMEM((slot, wide), BF),
            pltpu.VMEM((groups, WIDE, WIDE), F32),
            pltpu.VMEM((groups, WIDE, WIDE), F32),
            pltpu.VMEM((groups, WIDE, WIDE), F32),
            pltpu.VMEM((groups, WIDE, WIDE), F32),
            pltpu.VMEM((groups, WIDE, WIDE), F32),
            pltpu.VMEM((PACK * ROWS, WINDOW), BF),
            pltpu.VMEM((PACK * ROWS, 256), F32),
        ],
        compiler_params=pltpu.CompilerParams(vmem_limit_bytes=LIMIT),
        name="attn_bwd",
    )(length, g, qh, kh, vp, k1, k3, small, chain, flip)


D = 768
BOTH = ("tensor", "dp")


def rows_sum(left_op, right_op):
    return lax.dot_general(left_op, right_op, (TN, ((), ())), preferred_element_type=F32)


def cols_sum(left_op, right_op):
    return lax.dot_general(left_op, right_op, (NT, ((), ())), preferred_element_type=F32)


def dense(left_op, right_op):
    return jnp.dot(left_op, right_op, preferred_element_type=F32)


def norm_parts(values):
    centre = values - jnp.mean(values, axis=-1, keepdims=True)
    spread_of = jnp.mean(centre * centre, axis=-1, keepdims=True)
    inverse = lax.rsqrt(spread_of + 1e-05)
    return centre * inverse, inverse


def norm_back(grad, gain, normal, inverse):
    scaled = grad * gain
    lean = jnp.mean(scaled, axis=-1, keepdims=True)
    along = jnp.mean(scaled * normal, axis=-1, keepdims=True)
    return (
        inverse * (scaled - lean - normal * along),
        jnp.sum(grad * normal, axis=0),
        jnp.sum(grad, axis=0),
    )


def gather_weights(pieces):
    joined = lax.all_gather(jnp.concatenate(pieces, axis=1), BOTH, axis=0, tiled=True)
    halves_of = lax.axis_size("tensor")
    joined = joined.reshape(halves_of, D, -1)
    whole, start = [], 0
    for piece in pieces:
        width = piece.shape[1]
        part = joined[:, :, start : start + width]
        whole.append(part.transpose(1, 0, 2).reshape(D, halves_of * width))
        start += width
    return whole


def scatter_grads(fulls):
    halves_of = lax.axis_size("tensor")
    stacked = jnp.concatenate(
        [
            jnp.concatenate(
                [
                    full[:, t * full.shape[1] // halves_of : (t + 1) * full.shape[1] // halves_of]
                    for t in range(halves_of)
                ],
                axis=0,
            )
            for full in fulls
        ],
        axis=1,
    )
    mine = lax.psum_scatter(stacked, BOTH, scatter_dimension=0, tiled=True)
    out, start = [], 0
    for full in fulls:
        width = full.shape[1] // halves_of
        out.append(mine[:, start : start + width].astype(F32))
        start += width
    return out


def per_device(x_in, lengths, cotangent, w_query, w_key, w_value, w_out, w_in, w_down,
               conv_weight, ln1_gain, ln1_bias, ln2_gain, ln2_bias):
    tensor_index = lax.axis_index("tensor")
    slot = x_in.shape[0]
    halves_of = lax.axis_size("tensor")
    length = lax.dynamic_slice_in_dim(lengths, tensor_index, 1)
    valid = (jnp.arange(slot, dtype=jnp.int32) < length[0]).astype(F32)[:, None]

    query_w, key_w, value_w = gather_weights((w_query, w_key, w_value))
    out_w, in_w, down_w = gather_weights((w_out.T, w_in, w_down.T))
    gains = lax.all_gather(
        jnp.stack([ln1_gain, ln1_bias, ln2_gain, ln2_bias]), ("dp", "tensor"), axis=1, tiled=True
    )
    gain_one, bias_one, gain_two, bias_two = gains[0], gains[1], gains[2], gains[3]
    taps = lax.all_gather(conv_weight, "tensor", axis=0, tiled=True)
    heads, count = taps.shape
    room = ((0, 16 - heads), (0, 256 - count))

    tokens = x_in.astype(F32)
    queries, keys_all, values_all = dense(x_in, query_w), dense(x_in, key_w), dense(x_in, value_w)
    ctx, qh, kh, vp, k1, k3, small, chain = attn_fwd(
        length, queries, keys_all, values_all, jnp.pad(taps, room)
    )
    attn_branch = cols_sum(ctx, out_w)
    normal_one, inverse_one = norm_parts(tokens + attn_branch)
    hidden = (normal_one * gain_one + bias_one).astype(BF)
    pre = dense(hidden, in_w)
    below = 0.5 * (1.0 + lax.erf(pre * 0.5**0.5))
    act = (pre * below).astype(BF)
    slope = (below + pre * jnp.exp(-0.5 * pre * pre) * (2.0 * jnp.pi) ** -0.5).astype(BF)
    ffn_branch = cols_sum(act, down_w)
    normal_two, inverse_two = norm_parts(hidden.astype(F32) + ffn_branch)
    output = (normal_two * gain_two + bias_two).astype(BF)
    grad_result = cotangent.astype(F32) * valid
    d_res2, grad_gain_two, grad_bias_two = norm_back(grad_result, gain_two, normal_two, inverse_two)
    d_ffn = d_res2.astype(BF)
    grad_down = rows_sum(d_ffn, act)
    d_pre = (dense(d_ffn, down_w) * slope.astype(F32)).astype(BF)
    grad_in = rows_sum(hidden, d_pre)
    d_hidden = cols_sum(d_pre, in_w) + d_res2
    d_res1, grad_gain_one, grad_bias_one = norm_back(d_hidden, gain_one, normal_one, inverse_one)
    d_attn = d_res1.astype(BF)
    grad_out = rows_sum(d_attn, ctx)
    d_ctx = dense(d_attn, out_w).astype(BF)
    early = scatter_grads([grad_out.astype(BF), grad_in.astype(BF), grad_down.astype(BF)])
    d_qkv, conv_rows = attn_bwd(
        length, d_ctx, qh, kh, vp, k1, k3, small, chain, jnp.pad(taps[:, ::-1], room)
    )
    qkv_w = jnp.concatenate([query_w, key_w, value_w], axis=1)
    input_grad = (d_res1 + cols_sum(d_qkv, qkv_w)).astype(BF)
    grad_qkv = rows_sum(x_in, d_qkv).astype(BF)
    late = scatter_grads([grad_qkv[:, :D], grad_qkv[:, D : 2 * D], grad_qkv[:, 2 * D :]])

    def total(branch):
        return jnp.sum(valid * branch * branch)

    summed = lax.psum(
        jnp.concatenate(
            [
                grad_gain_one, grad_bias_one, grad_gain_two, grad_bias_two,
                conv_rows[:heads, ROWS - 1 : ROWS - 1 + count].reshape(-1),
                jnp.stack([total(tokens), total(attn_branch), total(ffn_branch), jnp.sum(valid)]),
            ]
        ),
        ("dp", "tensor"),
    )
    share = D // lax.axis_size(("dp", "tensor"))
    start_at = lax.axis_index(("dp", "tensor")) * share
    vectors = lax.dynamic_slice_in_dim(summed[: 4 * D].reshape(4, D), start_at, share, 1)
    conv_all = summed[4 * D : 4 * D + heads * count].reshape(heads, count)
    own_heads = heads // halves_of
    conv_grad = lax.dynamic_slice_in_dim(conv_all, tensor_index * own_heads, own_heads, 0)
    sums = summed[4 * D + heads * count :]
    stats = jnp.sqrt(sums[:3] / (sums[3] * D))
    return (
        output, input_grad, late[0], late[1], late[2], early[0].T, early[1], early[2].T,
        conv_grad, vectors[0], vectors[1], vectors[2], vectors[3], stats,
    )


def solution(mesh):
    rows, both = P(("dp", "tensor"), None), P(("dp", "tensor"))
    split, crossed = P("dp", "tensor"), P("tensor", "dp")
    return jax.shard_map(
        per_device,
        mesh=mesh,
        in_specs=(rows, P("dp"), rows, split, split, split, crossed, split, crossed,
                  P("tensor", None), both, both, both, both),
        out_specs=(rows, rows, split, split, split, crossed, split, crossed,
                   P("tensor", None), both, both, both, both, P()),
        check_vma=False,
    )
```

```python
from functools import partial

import jax
import jax.numpy as jnp
from jax import lax
from jax.experimental import pallas as pl
from jax.experimental.pallas import tpu as pltpu
from jax.sharding import PartitionSpec as P

ANY = pl.BlockSpec(memory_space=pl.ANY)
F32, BF = jnp.float32, jnp.bfloat16
NN, NT, TN = ((1,), (0,)), ((1,), (1,)), ((0,), (0,))
MARKS = 64
HEAD = 64
PACK = 4
WIDE = PACK * HEAD
TAPS = 33
EDGE = TAPS // 2
ROWS = 128
WINDOW = ROWS + 2 * EDGE
STEPS = 6
KEPT = 4


def mm(a, b, dims=NN):
    return lax.dot_general(a, b, (dims, ((), ())), preferred_element_type=F32)


def halves(a):
    high = a.astype(BF)
    return high, (a - high.astype(F32)).astype(BF)


def mm3(a, b, dims=NN):
    (ah, al), (bh, bl) = a, b
    return mm(ah, bh, dims) + (mm(ah, bl, dims) + mm(al, bh, dims))


def mm3f(a, b, dims=NN):
    return mm3(halves(a), halves(b), dims)


def grid_of(shape):
    return (
        lax.broadcasted_iota(jnp.int32, shape, 0),
        lax.broadcasted_iota(jnp.int32, shape, 1),
    )


def block_mask():
    row, col = grid_of((WIDE, WIDE))
    return row // HEAD == col // HEAD


def eye():
    row, col = grid_of((WIDE, WIDE))
    return (row == col).astype(F32)


def spread(packed, mask):
    full = jnp.concatenate([packed] * PACK, axis=0)
    return jnp.where(mask, full, jnp.zeros_like(full))


def gather_up(full):
    return sum(full[i * MARKS : (i + 1) * MARKS] for i in range(PACK))


def segment_reduce(a, fill, op):
    lane = lax.broadcasted_iota(jnp.int32, (a.shape[0], 128), 1) < HEAD
    parts = []
    for tile in range(a.shape[1] // 128):
        piece = a[:, tile * 128 : (tile + 1) * 128]
        low = op(jnp.where(lane, piece, fill), axis=1, keepdims=True)
        high = op(jnp.where(lane, fill, piece), axis=1, keepdims=True)
        parts.append(jnp.where(lane, low, high))
    return jnp.concatenate(parts, axis=1)


def average_matrix():
    row, col = grid_of((ROWS * MARKS // 1024, ROWS))
    return jnp.where(row == col // 16, 1.0 / 16, 0.0).astype(BF)


def average_back():
    row, col = grid_of((ROWS, ROWS * MARKS // 1024))
    return jnp.where(row // 16 == col, 1.0 / 16, 0.0).astype(BF)


def lanes_of(group):
    return slice(group * WIDE, (group + 1) * WIDE)


def picked(ref, rows, which, wide, parts):
    share = wide // parts
    return jnp.concatenate(
        [ref[rows, (3 * p + which) * share : (3 * p + which + 1) * share] for p in range(parts)],
        axis=1,
    )


def put(ref, rows, which, wide, parts, start, value):
    share = wide // parts
    for tile in range(0, value.shape[1], 128):
        lane = start + tile
        at = (3 * (lane // share) + which) * share + lane % share
        ref[rows, at : at + 128] = value[:, tile : tile + 128]


def toeplitz(taps_ref, group):
    parts = []
    for i in range(PACK):
        head = group * PACK + i
        line = jnp.broadcast_to(taps_ref[head : head + 1, :], (ROWS, 256))
        parts.append(pltpu.roll(line, 0, 1, stride=1, stride_axis=0)[:, :WINDOW])
    return jnp.concatenate(parts, axis=0).astype(BF)


def diagonal_lanes(stacked):
    col = lax.broadcasted_iota(jnp.int32, (ROWS, WIDE), 1) // HEAD
    out = stacked[:ROWS]
    for i in range(1, PACK):
        out = jnp.where(col == i, stacked[i * ROWS : (i + 1) * ROWS], out)
    return out


def attn_fwd_kernel(slot, groups, parts, cuts, *refs):
    n = 0 if cuts is None else max(c[0] for c in cuts) + 1
    len_ref, qkv_ref, taps_ref = refs[:3]
    shards, wholes = refs[3 : 3 + n], refs[3 + n : 3 + 2 * n]
    ctx_ref, qh_ref, kh_ref, vp_ref, k1_ref, k3_ref, small_ref, chain_ref = refs[3 + 2 * n : 11 + 2 * n]
    z_ref, k2_ref, s_ref, top_ref, t_ref = refs[11 + 2 * n : 16 + 2 * n]
    slots = []
    if n:
        place = Place()
        greet(place)
        slots = schedule(gather_parts(place, cuts, shards, wholes, *refs[16 + 2 * n :]), 0)

    def advance():
        if slots:
            for step in slots.pop(0):
                step()

    advance()
    count = slot // ROWS
    marks = ROWS // 16
    scale = HEAD ** -0.25
    length = len_ref[0]
    avg = average_matrix()
    wide = groups * WIDE
    vp_ref[0:EDGE, :] = jnp.zeros((EDGE, wide), BF)
    vp_ref[slot + EDGE : slot + 2 * EDGE, :] = jnp.zeros((EDGE, wide), BF)

    def load(i, carry):
        rows = pl.ds(pl.multiple_of(i * ROWS, ROWS), ROWS)
        row = lax.broadcasted_iota(jnp.int32, (ROWS, 1), 0) + i * ROWS
        valid = (row < length).astype(F32)
        few = pl.ds(pl.multiple_of(i * marks, marks), marks)
        q = picked(qkv_ref, rows, 0, wide, parts) * (valid * scale)
        high, low = halves(q)
        qh_ref[rows, :] = high
        small_ref[0, few, :] = mm(avg, high) + mm(avg, low)
        k = picked(qkv_ref, rows, 1, wide, parts) * (valid * scale)
        high, low = halves(k)
        kh_ref[rows, :] = high
        small_ref[1, few, :] = mm(avg, high) + mm(avg, low)
        vp_ref[pl.ds(pl.multiple_of(i * ROWS + EDGE, EDGE), ROWS), :] = (
            picked(qkv_ref, rows, 2, wide, parts) * valid
        ).astype(BF)
        return carry

    lax.fori_loop(0, count, load, 0)
    mask = block_mask()
    one = eye()

    for g in range(groups):
        at = lanes_of(g)
        ql, kl = spread(small_ref[0, :, at], mask), spread(small_ref[1, :, at], mask)
        a2 = jnp.where(mask, mm3f(ql, kl, NT), -1e30)
        e2 = jnp.where(mask, jnp.exp(a2 - jnp.max(a2, axis=1, keepdims=True)), 0.0)
        k2 = e2 / jnp.sum(e2, axis=1, keepdims=True)
        top = segment_reduce(jnp.sum(k2, axis=0, keepdims=True), -1e30, jnp.max)
        k2_ref[g] = k2
        small_ref[2, :, at] = gather_up(k2)
        z_ref[g] = jnp.transpose(k2) / top

    advance()

    def newton(step, carry):
        for g in range(groups):
            at = lanes_of(g)
            z = z_ref[g]
            zs = halves(z)
            p = mm3(halves(k2_ref[g]), zs)
            ps = halves(p)
            t2 = 15.0 * one - mm3(ps, halves(7.0 * one - p))
            t3 = 13.0 * one - mm3(ps, halves(t2))
            chain_ref[step, 0, :, at] = gather_up(z)
            chain_ref[step, 1, :, at] = gather_up(p)
            chain_ref[step, 2, :, at] = gather_up(t2)
            chain_ref[step, 3, :, at] = gather_up(t3)
            z_ref[g] = 0.25 * mm3(zs, halves(t3))
        return carry

    lax.fori_loop(0, STEPS // 2, newton, 0)
    advance()
    lax.fori_loop(STEPS // 2, STEPS, newton, 0)

    for g in range(groups):
        at = lanes_of(g)
        ql = spread(small_ref[0, :, at], mask).astype(BF)
        top_ref[...] = jnp.full(top_ref.shape, -jnp.inf, F32)

        def scores(i, carry):
            rows = pl.ds(pl.multiple_of(i * ROWS, ROWS), ROWS)
            row = lax.broadcasted_iota(jnp.int32, (ROWS, 1), 0) + i * ROWS
            a3 = jnp.where(row < length, mm(kh_ref[rows, at], ql, NT), -1e9)
            s_ref[rows, :] = a3
            top_ref[0:1, :] = jnp.maximum(top_ref[0:1, :], jnp.max(a3, axis=0, keepdims=True))
            return carry

        lax.fori_loop(0, count, scores, 0)
        peak = top_ref[0:1, :]
        top_ref[0:1, :] = jnp.zeros((1, WIDE), F32)

        def powers(i, carry):
            rows = pl.ds(pl.multiple_of(i * ROWS, ROWS), ROWS)
            e3 = jnp.exp(s_ref[rows, :] - peak)
            s_ref[rows, :] = e3
            top_ref[0:1, :] += jnp.sum(e3, axis=0, keepdims=True)
            return carry

        lax.fori_loop(0, count, powers, 0)
        inverse = 1.0 / top_ref[0:1, :]

        def weigh(i, carry):
            rows = pl.ds(pl.multiple_of(i * ROWS, ROWS), ROWS)
            k3_ref[rows, at] = (s_ref[rows, :] * inverse).astype(BF)
            return carry

        lax.fori_loop(0, count, weigh, 0)
        b = mm(k3_ref[:, at], vp_ref[EDGE : slot + EDGE, at], TN)
        b = jnp.where(mask, b, 0.0)
        z = z_ref[g]
        c = mm3f(z, b)
        small_ref[3, :, at] = gather_up(b)
        small_ref[4, :, at] = gather_up(c)
        small_ref[5, :, at] = gather_up(z)
        t_ref[...] = toeplitz(taps_ref, g)
        cb = c.astype(BF)
        kl = spread(small_ref[1, :, at], mask).astype(BF)
        ones = mask.astype(F32).astype(BF)

        def mix(i, carry):
            rows = pl.ds(pl.multiple_of(i * ROWS, ROWS), ROWS)
            a1 = mm(qh_ref[rows, at], kl, NT)
            e1 = jnp.exp(a1 - segment_reduce(a1, -jnp.inf, jnp.max)).astype(BF)
            k1 = (e1.astype(F32) / mm(e1, ones)).astype(BF)
            k1_ref[rows, at] = k1
            window = vp_ref[pl.ds(pl.multiple_of(i * ROWS, ROWS), WINDOW), at]
            ctx_ref[rows, at] = (
                mm(k1, cb) + diagonal_lanes(mm(t_ref[...], window))
            ).astype(BF)
            return carry

        lax.fori_loop(0, count, mix, 0)
        if g != 1:
            advance()

    while slots:
        advance()


def attn_bwd_kernel(slot, groups, parts, cuts, *refs):
    n = 0 if cuts is None else max(c[0] for c in cuts) + 1
    len_ref, g_ref, qh_ref, kh_ref, vp_ref, k1_ref, k3_ref, small_ref, chain_ref, flip_ref = refs[:10]
    fulls, outs = refs[10 : 10 + n], refs[10 + n : 10 + 2 * n]
    dqkv_ref, conv_ref = refs[10 + 2 * n : 12 + 2 * n]
    (gp_ref, da1_ref, da3_ref, dk_ref, dz_ref, k2_ref,
     dql_ref, dkl_ref, t_ref, acc_ref) = refs[12 + 2 * n : 22 + 2 * n]
    slots = []
    if n:
        place = Place()
        greet(place)
        slots = schedule(scatter_parts(place, cuts, fulls, outs, refs[22 + 2 * n :]), 0)

    def advance():
        if slots:
            for step in slots.pop(0):
                step()

    advance()
    count = slot // ROWS
    marks = ROWS // 16
    scale = HEAD ** -0.25
    length = len_ref[0]
    wide = groups * WIDE
    mask = block_mask()
    one = eye()
    ones = mask.astype(F32).astype(BF)
    gp_ref[0:EDGE, :] = jnp.zeros((EDGE, wide), BF)
    gp_ref[slot + EDGE : slot + 2 * EDGE, :] = jnp.zeros((EDGE, wide), BF)
    gp_ref[EDGE : slot + EDGE, :] = g_ref[...]
    col = lax.broadcasted_iota(jnp.int32, (ROWS, WIDE), 1) // HEAD
    up, across = grid_of((ROWS, ROWS))
    flip = jnp.where(up + across == ROWS - 1, 1.0, 0.0).astype(BF)

    for g in range(groups):
        at = lanes_of(g)
        c = spread(small_ref[4, :, at], mask)
        cb = c.astype(BF)

        def first(i, carry):
            rows = pl.ds(pl.multiple_of(i * ROWS, ROWS), ROWS)
            k1 = k1_ref[rows, at].astype(F32)
            dk1 = mm(g_ref[rows, at], cb, NT)
            high, low = halves(dk1 * k1)
            da1_ref[rows, at] = (k1 * (dk1 - (mm(high, ones) + mm(low, ones)))).astype(BF)
            return carry

        lax.fori_loop(0, count, first, 0)
        dc = jnp.where(mask, mm(k1_ref[:, at], g_ref[:, at], TN), 0.0)
        dkl_ref[g] = jnp.where(mask, mm(da1_ref[:, at], qh_ref[:, at], TN), 0.0)
        b = spread(small_ref[3, :, at], mask)
        z = spread(small_ref[5, :, at], mask)
        dcs = halves(dc)
        dz_ref[g] = mm3(halves(b), dcs, NT)
        db = mm3(halves(z), dcs, TN)
        dbb = db.astype(BF)
        high, low = halves(db * b)
        many = jnp.ones((8, WIDE), BF)
        total = (mm(many, high, NT) + mm(many, low, NT))[0:1, :]
        t_ref[...] = toeplitz(flip_ref, g)
        acc_ref[...] = jnp.zeros(acc_ref.shape, F32)

        def second(i, carry):
            rows = pl.ds(pl.multiple_of(i * ROWS, ROWS), ROWS)
            row = lax.broadcasted_iota(jnp.int32, (ROWS, 1), 0) + i * ROWS
            valid = (row < length).astype(F32)
            k3 = k3_ref[rows, at]
            vh = vp_ref[pl.ds(pl.multiple_of(i * ROWS + EDGE, EDGE), ROWS), at]
            dk3 = mm(vh, dbb, NT)
            da3_ref[rows, at] = (k3.astype(F32) * (dk3 - total)).astype(BF)
            window = pl.ds(pl.multiple_of(i * ROWS, ROWS), WINDOW)
            dv = mm(k3, dbb) + diagonal_lanes(mm(t_ref[...], gp_ref[window, at]))
            put(dqkv_ref, rows, 2, wide, parts, g * WIDE, (dv * valid).astype(BF))
            grad = g_ref[rows, at]
            split = jnp.concatenate(
                [jnp.where(col == h, grad, jnp.zeros_like(grad)) for h in range(PACK)], axis=0
            )
            acc_ref[:, :WINDOW] += mm(split, vp_ref[window, at], NT)
            return carry

        lax.fori_loop(0, count, second, 0)
        for h in range(PACK):
            high, low = halves(acc_ref[h * ROWS : (h + 1) * ROWS, :])
            turned = pltpu.roll(mm(flip, high) + mm(flip, low), 0, 1, stride=1, stride_axis=0)
            conv_ref[g * PACK + h : g * PACK + h + 1, :] = jnp.sum(turned, axis=0, keepdims=True)
        dql_ref[g] = jnp.where(mask, mm(da3_ref[:, at], kh_ref[:, at], TN), 0.0)
        dk_ref[g] = jnp.zeros((WIDE, WIDE), F32)
        k2_ref[g] = spread(small_ref[2, :, at], mask)
        if g != 1:
            advance()

    def newton(back, carry):
        step = STEPS - 1 - back
        for g in range(groups):
            at = lanes_of(g)
            zs = halves(spread(chain_ref[step, 0, :, at], mask))
            p = spread(chain_ref[step, 1, :, at], mask)
            t2s = halves(spread(chain_ref[step, 2, :, at], mask))
            t3s = halves(spread(chain_ref[step, 3, :, at], mask))
            ps = halves(p)
            t1s = halves(7.0 * one - p)
            dzs = halves(0.25 * dz_ref[g])
            dt3 = halves(mm3(dzs, zs))
            dp = -mm3(t2s, dt3)
            dt2f = -mm3(dt3, ps)
            dt2 = halves(dt2f)
            dp = dp - mm3(t1s, dt2) + mm3(dt2, ps)
            dps = halves(dp)
            dk_ref[g] += mm3(zs, dps)
            dz_ref[g] = mm3(t3s, dzs) + mm3(dps, halves(k2_ref[g]))
        return carry

    lax.fori_loop(0, STEPS // 2, newton, 0)
    advance()
    lax.fori_loop(STEPS // 2, STEPS, newton, 0)
    advance()

    for g in range(groups):
        at = lanes_of(g)
        k2 = k2_ref[g]
        sums = jnp.sum(k2, axis=0, keepdims=True)
        top = segment_reduce(sums, -1e30, jnp.max)
        hit = (sums == top).astype(F32)
        ties = segment_reduce(hit, 0.0, jnp.sum)
        dz0 = dz_ref[g]
        dtop = -segment_reduce(jnp.sum(dz0 * k2, axis=0, keepdims=True), 0.0, jnp.sum) / (top * top)
        dk2 = jnp.transpose(dk_ref[g]) + dz0 / top + hit * (dtop / ties)
        dk2 = jnp.where(mask, dk2, 0.0)
        da2 = k2 * (dk2 - jnp.sum(dk2 * k2, axis=1, keepdims=True))
        da2s = halves(da2)
        ql, kl = spread(small_ref[0, :, at], mask), spread(small_ref[1, :, at], mask)
        qls, kls = halves(ql), halves(kl)
        dql = gather_up(dql_ref[g] + mm3(da2s, kls))
        dkl = gather_up(dkl_ref[g] + mm3(da2s, qls, TN))
        dql_ref[g, 0:MARKS, :] = dql
        dkl_ref[g, 0:MARKS, :] = dkl
        qlb, klb = qls[0], kls[0]
        back = average_back()

        def third(i, carry):
            rows = pl.ds(pl.multiple_of(i * ROWS, ROWS), ROWS)
            few = pl.ds(pl.multiple_of(i * marks, marks), marks)
            row = lax.broadcasted_iota(jnp.int32, (ROWS, 1), 0) + i * ROWS
            valid = jnp.where(row < length, scale, 0.0)
            dq = mm(da1_ref[rows, at], klb) + mm(back, dql_ref[g, few, :].astype(BF))
            dk = mm(da3_ref[rows, at], qlb) + mm(back, dkl_ref[g, few, :].astype(BF))
            put(dqkv_ref, rows, 0, wide, parts, g * WIDE, (dq * valid).astype(BF))
            put(dqkv_ref, rows, 1, wide, parts, g * WIDE, (dk * valid).astype(BF))
            return carry

        lax.fori_loop(0, count, third, 0)

    while slots:
        advance()


VM = pl.BlockSpec(memory_space=pltpu.VMEM)
SM = pl.BlockSpec(memory_space=pltpu.SMEM)
LIMIT = 60 * 1024 * 1024


def attn_fwd(length, qkv, taps, parts, shards=(), cuts=None, collective_id=1):
    slot, wide = qkv.shape[0], qkv.shape[1] // 3
    groups = wide // WIDE
    shape = jax.ShapeDtypeStruct
    talks = dict(collective_id=collective_id, has_side_effects=True) if shards else {}
    n = len(shards)
    outs = pl.pallas_call(
        partial(attn_fwd_kernel, slot, groups, parts, cuts),
        out_shape=gather_shapes(shards)
        + (
            shape((slot, wide), BF),
            shape((slot, wide), BF),
            shape((slot, wide), BF),
            shape((slot + 2 * EDGE, wide), BF),
            shape((slot, wide), BF),
            shape((slot, wide), BF),
            shape((6, MARKS, wide), F32),
            shape((STEPS, KEPT, MARKS, wide), F32),
        ),
        in_specs=[SM, VM, VM] + [VM] * n,
        out_specs=[ANY] * n + [VM] * 8,
        scratch_shapes=[
            pltpu.VMEM((groups, WIDE, WIDE), F32),
            pltpu.VMEM((groups, WIDE, WIDE), F32),
            pltpu.VMEM((slot, WIDE), F32),
            pltpu.VMEM((8, WIDE), F32),
            pltpu.VMEM((PACK * ROWS, WINDOW), BF),
        ]
        + (gather_scratch(cuts) if n else []),
        compiler_params=pltpu.CompilerParams(vmem_limit_bytes=LIMIT, **talks),
        name="attn_fwd",
    )(length, qkv, taps, *shards)
    return outs[:n], outs[n:]


def attn_bwd(length, g, saved, flip, parts, fulls=(), cuts=None, collective_id=2):
    slot, wide = g.shape
    groups = wide // WIDE
    shape = jax.ShapeDtypeStruct
    talks = dict(collective_id=collective_id, has_side_effects=True) if fulls else {}
    n = len(fulls)
    rows = fulls[0].shape[0] // 16 if n else 0
    fulls = [f.reshape(2, 2, 2, 2, rows, f.shape[1]) for f in fulls]
    outs = pl.pallas_call(
        partial(attn_bwd_kernel, slot, groups, parts, cuts),
        out_shape=tuple(shape((rows, f.shape[-1] // 2), F32) for f in fulls)
        + (shape((slot, 3 * wide), BF), shape((16, 256), F32)),
        in_specs=[SM] + [VM] * 9 + [ANY] * n,
        out_specs=[VM] * (n + 2),
        scratch_shapes=[
            pltpu.VMEM((slot + 2 * EDGE, wide), BF),
            pltpu.VMEM((slot, wide), BF),
            pltpu.VMEM((slot, wide), BF),
            pltpu.VMEM((groups, WIDE, WIDE), F32),
            pltpu.VMEM((groups, WIDE, WIDE), F32),
            pltpu.VMEM((groups, WIDE, WIDE), F32),
            pltpu.VMEM((groups, WIDE, WIDE), F32),
            pltpu.VMEM((groups, WIDE, WIDE), F32),
            pltpu.VMEM((PACK * ROWS, WINDOW), BF),
            pltpu.VMEM((PACK * ROWS, 256), F32),
        ]
        + (all_scatter_scratch(cuts, rows) if n else []),
        compiler_params=pltpu.CompilerParams(vmem_limit_bytes=LIMIT, **talks),
        name="attn_bwd",
    )(length, g, *saved, flip, *fulls)
    return outs[:n], outs[n], outs[n + 1]
MESH = pl.DeviceIdType.MESH
WAYS = ("zh", "zl", "y", "x", "c")
COPIES = 11
STAGES = 6


class Place:
    def __init__(self):
        dp = lax.axis_index("dp")
        self.x = lax.axis_index("tensor")
        self.zh, self.zl = dp // 8, (dp // 4) % 2
        self.y, self.c = (dp // 2) % 2, dp % 2

    def at(self, way):
        spot = {w: getattr(self, w) for w in WAYS}
        spot[way] = 1 - spot[way]
        return {
            "dp": spot["zh"] * 8 + spot["zl"] * 4 + spot["y"] * 2 + spot["c"],
            "tensor": spot["x"],
        }


def greet(place):
    barrier = pltpu.get_barrier_semaphore()
    for way in WAYS:
        pl.semaphore_signal(barrier, inc=1, device_id=place.at(way), device_id_type=MESH)
    pl.semaphore_wait(barrier, len(WAYS))


class Mover:
    def __init__(self, place, send, recv, base):
        self.place, self.send, self.recv, self.base = place, send, recv, base
        self.started = []

    def copy(self, index, src, dst, way):
        return pltpu.make_async_remote_copy(
            src_ref=src, dst_ref=dst,
            send_sem=self.send.at[self.base + index], recv_sem=self.recv.at[self.base + index],
            device_id=self.place.at(way), device_id_type=MESH,
        )

    def push(self, index, src, dst, way):
        copy = self.copy(index, src, dst, way)
        copy.start()
        self.started.append(copy)

    def arrive(self, index, ref, way):
        self.copy(index, ref, ref, way).wait_recv()

    def drain(self):
        for copy in self.started:
            copy.wait_send()


class Gather(Mover):
    def __init__(self, place, shard, whole, lane, width, order, send, recv, base, local):
        super().__init__(place, send, recv, base)
        self.shard, self.whole, self.local = shard.at[:, pl.ds(lane, width)], whole, local
        self.lane, self.width, self.order = lane, width, order

    def view(self, zh, zl, y, c, x):
        half = self.whole.shape[-1] // 2
        lanes = pl.ds(pl.multiple_of(x * half + self.lane, 128), self.width)
        return self.whole.at[zh, zl, y, c, :, lanes]

    def steps(self, c):
        p, every = self.place, slice(None)
        yield "zh", [self.view(p.zh, p.zl, p.y, c, p.x)], [self.view(1 - p.zh, p.zl, p.y, c, p.x)]
        yield "zl", [self.view(every, p.zl, p.y, c, p.x)], [self.view(every, 1 - p.zl, p.y, c, p.x)]
        if self.order == "yx":
            yield "y", [self.view(every, every, p.y, c, p.x)], [self.view(every, every, 1 - p.y, c, p.x)]
            yield "x", [self.view(every, every, every, c, p.x)], [self.view(every, every, every, c, 1 - p.x)]
        else:
            yield "x", [self.view(every, every, p.y, c, p.x)], [self.view(every, every, p.y, c, 1 - p.x)]
            yield (
                "y",
                [self.view(every, every, p.y, c, x) for x in (0, 1)],
                [self.view(every, every, 1 - p.y, c, x) for x in (0, 1)],
            )

    def run(self, stage):
        p = self.place
        here = self.view(p.zh, p.zl, p.y, p.c, p.x)
        if stage == 0:
            self.mine, self.other = list(self.steps(p.c)), list(self.steps(1 - p.c))
            self.push(0, self.shard, here, "zh")
            self.push(5, self.shard, here, "c")
            self.own = pltpu.make_async_copy(self.shard, here, self.local)
            self.own.start()
        elif stage < 5:
            way, _, landed = self.mine[stage - 1]
            for i, ref in enumerate(landed):
                self.arrive(stage - 1 + i, ref, way)
            if stage == 1:
                self.own.wait()
            if stage < 4:
                way, outgoing, _ = self.mine[stage]
                for i, ref in enumerate(outgoing):
                    self.push(stage + i, ref, ref, way)
            for i, ref in enumerate(landed):
                self.push(5 + stage + i, ref, ref, "c")
        else:
            self.arrive(5, self.view(p.zh, p.zl, p.y, 1 - p.c, p.x), "c")
            for k in range(4):
                for i, ref in enumerate(self.other[k][2]):
                    self.arrive(6 + k + i, ref, "c")
            self.drain()


class Scatter(Mover):
    def __init__(self, place, full, lane, width, order, out, bufs, send, recv, base, local):
        super().__init__(place, send, recv, base)
        self.full, self.lane, self.width, self.order = full, lane, width, order
        self.out, self.local = out, local
        self.sums, self.in_c, self.in_1, self.in_2, self.in_l, self.in_h = bufs

    def lanes(self, x):
        half = self.full.shape[-1] // 2
        return pl.ds(x * half + self.lane, self.width)

    def add(self, target, landed):
        lead = landed.shape[:-2]
        total = 1
        for n in lead:
            total *= n
        flat_dims = lead

        def one(i, carry):
            index = []
            for n in reversed(flat_dims):
                index.append(i % n)
                i = i // n
            index = tuple(reversed(index))
            target[index] = target[index] + landed[index]
            return carry

        if total == 1:
            one(0, 0)
        else:
            lax.fori_loop(0, total, one, 0)

    def run(self, stage):
        p, every = self.place, slice(None)
        if stage == 0:
            self.loads = []
            for x in (0, 1):
                self.push(x, self.full.at[:, :, :, 1 - p.c, :, self.lanes(x)], self.in_c.at[x], "c")
                load = pltpu.make_async_copy(
                    self.full.at[:, :, :, p.c, :, self.lanes(x)], self.sums.at[x], self.local.at[x]
                )
                load.start()
                self.loads.append(load)
            return
        if stage == 1:
            for x in (0, 1):
                self.arrive(x, self.in_c.at[x], "c")
                self.loads[x].wait()
            self.add(self.sums, self.in_c)
            if self.order == "xy":
                self.push(2, self.sums.at[1 - p.x], self.in_1.at[...], "x")
            else:
                for x in (0, 1):
                    self.push(2 + x, self.sums.at[x, :, :, 1 - p.y], self.in_1.at[x], "y")
        elif stage == 2:
            if self.order == "xy":
                self.arrive(2, self.in_1, "x")
                self.add(self.sums.at[p.x], self.in_1)
                self.push(4, self.sums.at[p.x, :, :, 1 - p.y], self.in_2, "y")
            else:
                for x in (0, 1):
                    self.arrive(2 + x, self.in_1.at[x], "y")
                    self.add(self.sums.at[x, :, :, p.y], self.in_1.at[x])
                self.push(4, self.sums.at[1 - p.x, :, :, p.y], self.in_2, "x")
        elif stage == 3:
            self.arrive(4, self.in_2, "y" if self.order == "xy" else "x")
            self.add(self.sums.at[p.x, :, :, p.y], self.in_2)
            self.push(5, self.sums.at[p.x, :, 1 - p.zl, p.y], self.in_l, "zl")
        elif stage == 4:
            self.arrive(5, self.in_l, "zl")
            self.add(self.sums.at[p.x, :, p.zl, p.y], self.in_l)
            self.push(6, self.sums.at[p.x, 1 - p.zh, p.zl, p.y], self.in_h, "zh")
        else:
            self.arrive(6, self.in_h, "zh")
            self.out[:, self.lane : self.lane + self.width] = (
                self.sums[p.x, p.zh, p.zl, p.y].astype(F32) + self.in_h[...].astype(F32)
            )
            self.drain()


def scatter_scratch(rows, width, order):
    first = (2, 2, 2) if order == "xy" else (2, 2, 2)
    return [
        pltpu.VMEM((2, 2, 2, 2, rows, width), BF),
        pltpu.VMEM((2, 2, 2, 2, rows, width), BF),
        pltpu.VMEM(first + (rows, width), BF),
        pltpu.VMEM((2, 2, rows, width), BF),
        pltpu.VMEM((2, rows, width), BF),
        pltpu.VMEM((rows, width), BF),
    ]


class Total(Mover):
    def __init__(self, place, block, out, sums, landed, send, recv, base):
        super().__init__(place, send, recv, base)
        self.block, self.out, self.sums, self.landed = block, out, sums, landed

    def run(self, stage):
        if stage == 0:
            self.sums[0] = self.block[...]
        else:
            self.arrive(stage - 1, self.landed.at[stage - 1], WAYS[stage - 1])
            self.sums[stage] = self.sums[stage - 1] + self.landed[stage - 1]
        if stage < 5:
            self.push(stage, self.sums.at[stage], self.landed.at[stage], WAYS[stage])
        else:
            self.out[...] = self.sums[5]
            self.drain()


def schedule(parts, lag=1):
    slots = [[] for _ in range(STAGES + lag * (len(parts) - 1))]
    for i, part in enumerate(parts):
        for stage in range(STAGES):
            slots[stage + lag * i].append((part, stage))
    return [[partial(part.run, stage) for part, stage in slot] for slot in slots]


def cut(widths, piece):
    out = []
    for i, width in enumerate(widths):
        lane = 0
        while lane < width:
            take = min(piece, width - lane)
            out.append((i, lane, take, ("yx", "xy")[len(out) % 2]))
            lane += take
    return tuple(out)


def gather_parts(place, cuts, shards, wholes, send, recv, local):
    return [
        Gather(place, shards[i], wholes[i], lane, width, order, send, recv, COPIES * n, local.at[n])
        for n, (i, lane, width, order) in enumerate(cuts)
    ]


def gather_scratch(cuts):
    n = len(cuts)
    return [
        pltpu.SemaphoreType.DMA((COPIES * n,)),
        pltpu.SemaphoreType.DMA((COPIES * n,)),
        pltpu.SemaphoreType.DMA((n,)),
    ]


def gather_shapes(shards):
    return tuple(
        jax.ShapeDtypeStruct((2, 2, 2, 2, s.shape[0], 2 * s.shape[1]), s.dtype) for s in shards
    )


def gather_kernel(cuts, lag, n, *refs):
    shards, wholes = refs[:n], refs[n : 2 * n]
    place = Place()
    greet(place)
    parts = gather_parts(place, cuts, shards, wholes, *refs[2 * n :])
    for slot in schedule(parts, lag):
        for step in slot:
            step()


def gather_call(shards, cuts, lag, collective_id):
    n = len(shards)
    return pl.pallas_call(
        partial(gather_kernel, cuts, lag, n),
        out_shape=gather_shapes(shards),
        in_specs=[VM] * n,
        out_specs=[ANY] * n,
        scratch_shapes=gather_scratch(cuts),
        compiler_params=pltpu.CompilerParams(
            collective_id=collective_id, has_side_effects=True, vmem_limit_bytes=LIMIT
        ),
        name=f"gather_{collective_id}",
    )(*shards)


SUM_COPIES = 7


def scatter_parts(place, cuts, fulls, outs, refs):
    send, recv, local = refs[-3:]
    return [
        Scatter(place, fulls[i], lane, width, order, outs[i], refs[6 * n : 6 * n + 6],
                send, recv, SUM_COPIES * n, local.at[n])
        for n, (i, lane, width, order) in enumerate(cuts)
    ]


def all_scatter_scratch(cuts, rows, extra=0):
    out = []
    for _, _, width, order in cuts:
        out += scatter_scratch(rows, width, order)
    n = len(cuts)
    return out + [
        pltpu.SemaphoreType.DMA((SUM_COPIES * n + extra,)),
        pltpu.SemaphoreType.DMA((SUM_COPIES * n + extra,)),
        pltpu.SemaphoreType.DMA((n, 2)),
    ]


def scatter_kernel(cuts, lag, n, block_ref, *refs):
    fulls, outs, sum_ref = refs[:n], refs[n : 2 * n], refs[2 * n]
    sums, landed = refs[2 * n + 1 : 2 * n + 3]
    rest = refs[2 * n + 3 :]
    place = Place()
    greet(place)
    parts = scatter_parts(place, cuts, fulls, outs, rest)
    total = Total(place, block_ref, sum_ref, sums, landed, rest[-3], rest[-2], SUM_COPIES * len(cuts))
    slots = schedule(parts, lag)
    for i in range(STAGES):
        slots[i].append(partial(total.run, i))
    for slot in slots:
        for step in slot:
            step()


def scatter_call(block, fulls, cuts, lag, collective_id):
    n = len(fulls)
    rows = fulls[0].shape[0] // 16
    shape = jax.ShapeDtypeStruct
    fulls = [f.reshape(2, 2, 2, 2, rows, f.shape[1]) for f in fulls]
    return pl.pallas_call(
        partial(scatter_kernel, cuts, lag, n),
        out_shape=tuple(shape((rows, f.shape[-1] // 2), F32) for f in fulls)
        + (shape(block.shape, F32),),
        in_specs=[VM] + [ANY] * n,
        out_specs=[VM] * (n + 1),
        scratch_shapes=[pltpu.VMEM((6,) + block.shape, F32), pltpu.VMEM((5,) + block.shape, F32)]
        + all_scatter_scratch(cuts, rows, 5),
        compiler_params=pltpu.CompilerParams(
            collective_id=collective_id, has_side_effects=True, vmem_limit_bytes=LIMIT
        ),
        name=f"scatter_{collective_id}",
    )(block, *fulls)


D = 768
BOTH = ("tensor", "dp")


def rows_sum(left_op, right_op):
    return lax.dot_general(left_op, right_op, (TN, ((), ())), preferred_element_type=F32)


def cols_sum(left_op, right_op):
    return lax.dot_general(left_op, right_op, (NT, ((), ())), preferred_element_type=F32)


def dense(left_op, right_op):
    return jnp.dot(left_op, right_op, preferred_element_type=F32)


def norm_parts(values):
    centre = values - jnp.mean(values, axis=-1, keepdims=True)
    spread_of = jnp.mean(centre * centre, axis=-1, keepdims=True)
    inverse = lax.rsqrt(spread_of + 1e-05)
    return centre * inverse, inverse


def norm_back(grad, gain, normal, inverse):
    scaled = grad * gain
    lean = jnp.mean(scaled, axis=-1, keepdims=True)
    along = jnp.mean(scaled * normal, axis=-1, keepdims=True)
    return (
        inverse * (scaled - lean - normal * along),
        jnp.sum(grad * normal, axis=0),
        jnp.sum(grad, axis=0),
    )


def gather_plain(pieces):
    sizes = lax.axis_size("tensor"), lax.axis_size("dp")
    out = []
    for piece in pieces:
        joined = lax.all_gather(piece, BOTH, axis=0, tiled=True)
        joined = joined.reshape(sizes[0], sizes[1] * piece.shape[0], piece.shape[1])
        out.append(joined.transpose(1, 0, 2).reshape(joined.shape[1], -1))
    return out


def scatter_plain(fulls):
    parts = lax.axis_size("tensor")
    out = []
    for full in fulls:
        stacked = full.reshape(full.shape[0], parts, -1).transpose(1, 0, 2).reshape(-1, full.shape[1] // parts)
        out.append(lax.psum_scatter(stacked, BOTH, scatter_dimension=0, tiled=True).astype(F32))
    return out


def per_device(own, x_in, lengths, cotangent, w_query, w_key, w_value, w_out, w_in, w_down,
               conv_weight, ln1_gain, ln1_bias, ln2_gain, ln2_bias):
    tensor_index = lax.axis_index("tensor")
    slot = x_in.shape[0]
    parts = lax.axis_size("tensor")
    length = lax.dynamic_slice_in_dim(lengths, tensor_index, 1)
    valid = (jnp.arange(slot, dtype=jnp.int32) < length[0]).astype(F32)[:, None]

    first = jnp.concatenate([w_query, w_key, w_value], axis=1)
    later = (w_out.T, w_in, w_down.T)
    few, own_heads, count = ln1_gain.shape[0], conv_weight.shape[0], conv_weight.shape[1]
    if own:
        vectors = jnp.pad(
            jnp.stack([ln1_gain, ln1_bias, ln2_gain, ln2_bias]), ((0, 4), (0, 128 - few))
        )
        block = jnp.concatenate(
            [vectors, jnp.pad(conv_weight, ((0, 8 - own_heads), (0, 128 - count)))], axis=0
        )
        qkv_w, blocks = gather_call([first, block], FIRST_CUTS, 0, 0)
        qkv_w = qkv_w.reshape(D, -1)
        blocks = blocks.reshape(lax.axis_size("dp"), 16, parts, 128)
        gains = blocks[:, :4, :, :few].transpose(1, 0, 2, 3).reshape(4, D)
        taps = blocks[0, 8 : 8 + own_heads, :, :count].transpose(1, 0, 2).reshape(-1, count)
    else:
        (qkv_w,) = gather_plain([first])
        gains = lax.all_gather(
            jnp.stack([ln1_gain, ln1_bias, ln2_gain, ln2_bias]), ("dp", "tensor"), axis=1, tiled=True
        )
        taps = lax.all_gather(conv_weight, "tensor", axis=0, tiled=True)
    gain_one, bias_one, gain_two, bias_two = gains[0], gains[1], gains[2], gains[3]
    heads = own_heads * parts
    room = ((0, 16 - heads), (0, 256 - count))

    tokens = x_in.astype(F32)
    qkv = dense(x_in, qkv_w)
    if own:
        wholes, saved = attn_fwd(length, qkv, jnp.pad(taps, room), parts, later, LATER_CUTS)
        out_w, in_w, down_w = (w.reshape(D, -1) for w in wholes)
    else:
        _, saved = attn_fwd(length, qkv, jnp.pad(taps, room), parts)
        out_w, in_w, down_w = gather_plain(later)
    ctx, saved = saved[0], saved[1:]
    attn_branch = cols_sum(ctx, out_w)
    normal_one, inverse_one = norm_parts(tokens + attn_branch)
    hidden = (normal_one * gain_one + bias_one).astype(BF)
    pre = dense(hidden, in_w)
    below = 0.5 * (1.0 + lax.erf(pre * 0.5**0.5))
    act = (pre * below).astype(BF)
    slope = (below + pre * jnp.exp(-0.5 * pre * pre) * (2.0 * jnp.pi) ** -0.5).astype(BF)
    ffn_branch = cols_sum(act, down_w)
    normal_two, inverse_two = norm_parts(hidden.astype(F32) + ffn_branch)
    output = (normal_two * gain_two + bias_two).astype(BF)
    grad_result = cotangent.astype(F32) * valid
    d_res2, grad_gain_two, grad_bias_two = norm_back(grad_result, gain_two, normal_two, inverse_two)
    d_ffn = d_res2.astype(BF)
    grad_down = rows_sum(d_ffn, act)
    d_pre = (dense(d_ffn, down_w) * slope.astype(F32)).astype(BF)
    grad_in = rows_sum(hidden, d_pre)
    d_hidden = cols_sum(d_pre, in_w) + d_res2
    d_res1, grad_gain_one, grad_bias_one = norm_back(d_hidden, gain_one, normal_one, inverse_one)
    d_attn = d_res1.astype(BF)
    grad_out = rows_sum(d_attn, ctx)
    d_ctx = dense(d_attn, out_w).astype(BF)
    fulls = [grad_out.astype(BF), grad_in.astype(BF), grad_down.astype(BF)]
    flip = jnp.pad(taps[:, ::-1], room)
    if own:
        early, d_qkv, conv_rows = attn_bwd(length, d_ctx, saved, flip, parts, fulls, LATER_CUTS)
    else:
        _, d_qkv, conv_rows = attn_bwd(length, d_ctx, saved, flip, parts)
        early = scatter_plain(fulls)
    grad_qkv = rows_sum(x_in, d_qkv).astype(BF)
    input_grad = (d_res1 + cols_sum(d_qkv, qkv_w)).astype(BF)

    def total(branch):
        return jnp.sum(valid * branch * branch)

    sums = jnp.concatenate(
        [
            grad_gain_one, grad_bias_one, grad_gain_two, grad_bias_two,
            conv_rows[:heads, ROWS - 1 : ROWS - 1 + count].reshape(-1),
            jnp.stack([total(tokens), total(attn_branch), total(ffn_branch), jnp.sum(valid)]),
        ]
    )
    if own:
        late, summed = scatter_call(
            jnp.pad(sums, (0, 4096 - sums.shape[0])).reshape(32, 128), [grad_qkv], LAST_CUTS, 0, 3
        )
        summed = summed.reshape(-1)
    else:
        (late,) = scatter_plain([grad_qkv])
        summed = lax.psum(sums, ("dp", "tensor"))
    share = D // lax.axis_size(("dp", "tensor"))
    start_at = lax.axis_index(("dp", "tensor")) * share
    vectors = lax.dynamic_slice_in_dim(summed[: 4 * D].reshape(4, D), start_at, share, 1)
    conv_all = summed[4 * D : 4 * D + heads * count].reshape(heads, count)
    conv_grad = lax.dynamic_slice_in_dim(conv_all, tensor_index * own_heads, own_heads, 0)
    sums = summed[4 * D + heads * count :]
    stats = jnp.sqrt(sums[:3] / (sums[3] * D))
    width = late.shape[1] // 3
    return (
        output, input_grad, late[:, :width], late[:, width : 2 * width], late[:, 2 * width :], early[0].T, early[1], early[2].T,
        conv_grad, vectors[0], vectors[1], vectors[2], vectors[3], stats,
    )


FIRST_CUTS = ((0, 0, 640, "yx"), (0, 640, 512, "xy"), (1, 0, 128, "yx"))
LATER_CUTS = ((1, 0, 1536, "xy"), (2, 0, 1536, "yx"), (0, 0, 384, "xy"))
LAST_CUTS = ((0, 0, 640, "yx"), (0, 640, 512, "xy"))


def solution(mesh):
    own = mesh.shape["dp"] == 16 and mesh.shape["tensor"] == 2
    rows, both = P(("dp", "tensor"), None), P(("dp", "tensor"))
    split, crossed = P("dp", "tensor"), P("tensor", "dp")
    return jax.shard_map(
        partial(per_device, own),
        mesh=mesh,
        in_specs=(rows, P("dp"), rows, split, split, split, crossed, split, crossed,
                  P("tensor", None), both, both, both, both),
        out_specs=(rows, rows, split, split, split, crossed, split, crossed,
                   P("tensor", None), both, both, both, both, P()),
        check_vma=False,
    )
```

```python
from functools import partial

import jax
import jax.numpy as jnp
from jax import lax
from jax.experimental import pallas as pl
from jax.experimental.pallas import tpu as pltpu
from jax.sharding import PartitionSpec as P

ANY = pl.BlockSpec(memory_space=pl.ANY)
F32, BF = jnp.float32, jnp.bfloat16
NN, NT, TN = ((1,), (0,)), ((1,), (1,)), ((0,), (0,))
MARKS = 64
HEAD = 64
PACK = 4
WIDE = PACK * HEAD
TAPS = 33
EDGE = TAPS // 2
ROWS = 128
TALL = 256
TAPS_AT, FLIP_AT, BLOCK = 8, 16, 24
WINDOW = ROWS + 2 * EDGE
STEPS = 6
KEPT = 4


def mm(a, b, dims=NN):
    return lax.dot_general(a, b, (dims, ((), ())), preferred_element_type=F32)


def halves(a):
    high = a.astype(BF)
    return high, (a - high.astype(F32)).astype(BF)


def mm3(a, b, dims=NN):
    (ah, al), (bh, bl) = a, b
    return mm(ah, bh, dims) + (mm(ah, bl, dims) + mm(al, bh, dims))


def mm3f(a, b, dims=NN):
    return mm3(halves(a), halves(b), dims)


def grid_of(shape):
    return (
        lax.broadcasted_iota(jnp.int32, shape, 0),
        lax.broadcasted_iota(jnp.int32, shape, 1),
    )


def block_mask():
    row, col = grid_of((WIDE, WIDE))
    return row // HEAD == col // HEAD


def eye():
    row, col = grid_of((WIDE, WIDE))
    return (row == col).astype(F32)


def spread(packed, mask):
    full = jnp.concatenate([packed] * PACK, axis=0)
    return jnp.where(mask, full, jnp.zeros_like(full))


def gather_up(full):
    return sum(full[i * MARKS : (i + 1) * MARKS] for i in range(PACK))


def segment_reduce(a, fill, op):
    lane = lax.broadcasted_iota(jnp.int32, (a.shape[0], 128), 1) < HEAD
    parts = []
    for tile in range(a.shape[1] // 128):
        piece = a[:, tile * 128 : (tile + 1) * 128]
        low = op(jnp.where(lane, piece, fill), axis=1, keepdims=True)
        high = op(jnp.where(lane, fill, piece), axis=1, keepdims=True)
        parts.append(jnp.where(lane, low, high))
    return jnp.concatenate(parts, axis=1)


def average_matrix():
    row, col = grid_of((TALL // 16, TALL))
    return jnp.where(row == col // 16, 1.0 / 16, 0.0).astype(BF)


def average_back():
    row, col = grid_of((ROWS, ROWS // 16))
    return jnp.where(row // 16 == col, 1.0 / 16, 0.0).astype(BF)


def lanes_of(group):
    return slice(group * WIDE, (group + 1) * WIDE)


def put(ref, rows, which, wide, parts, start, value):
    share = wide // parts
    for tile in range(0, value.shape[1], 128):
        lane = start + tile
        at = (3 * (lane // share) + which) * share + lane % share
        ref[rows, at : at + 128] = value[:, tile : tile + 128]


def lhs(a):
    return jnp.concatenate(halves(a), axis=1)


def rhs(b):
    high, low = halves(b)
    return jnp.concatenate(
        [
            jnp.concatenate([high, low], axis=1),
            jnp.concatenate([high, jnp.zeros_like(high)], axis=1),
        ],
        axis=0,
    )


def pair_mm(left, right):
    out = mm(left, right)
    return out[:, :128] + out[:, 128:]


def fold(full):
    return full[:MARKS] + full[MARKS:]


def unfold(packed, mask):
    full = jnp.concatenate([packed, packed], axis=0)
    return jnp.where(mask, full, 0.0)


def pair_lanes(pair):
    return slice(pair * 128, (pair + 1) * 128)


def pair_consts():
    row, col = grid_of((128, 128))
    return row // HEAD == col // HEAD, (row == col).astype(F32)


def toeplitz(taps_ref, first, own_heads, group):
    parts = []
    for i in range(PACK):
        half, head = divmod(group * PACK + i, own_heads)
        line = taps_ref[first + head : first + head + 1, half * 128 : (half + 1) * 128]
        line = jnp.concatenate([line, jnp.zeros_like(line)], axis=1)
        line = jnp.broadcast_to(line, (ROWS, 256))
        parts.append(pltpu.roll(line, 0, 1, stride=1, stride_axis=0)[:, :WINDOW])
    return jnp.concatenate(parts, axis=0).astype(BF)


def diagonal_lanes(stacked):
    col = lax.broadcasted_iota(jnp.int32, (ROWS, WIDE), 1) // HEAD
    out = stacked[:ROWS]
    for i in range(1, PACK):
        out = jnp.where(col == i, stacked[i * ROWS : (i + 1) * ROWS], out)
    return out


def attn_fwd_kernel(slot, groups, parts, own, *refs):
    len_ref, x_ref = refs[:2]
    if own:
        shards, outs, refs = refs[2:7], refs[7:12], refs[12:]
        weight, taps_ref = outs[0], outs[1].at[0, 0, 0, 0]
    else:
        weight, taps_ref, refs = refs[2], refs[3], refs[4:]
    ctx_ref, qh_ref, kh_ref, vp_ref, k1_ref, k3_ref, small_ref, chain_ref = refs[:8]
    z_ref, k2_ref, s_ref, top_ref, t_ref = refs[8:13]
    slots = []
    if own:
        place = Place()
        greet(place)
        slots = schedule(gather_parts(place, GATHERS, shards, outs, *refs[13:]), GATHER_LAGS)

    def advance(count=1):
        for _ in range(count):
            if slots:
                for step in slots.pop(0):
                    step()

    advance(6)
    count = slot // ROWS
    scale = HEAD ** -0.25
    length = len_ref[0]
    avg = average_matrix()
    wide = groups * WIDE
    share = wide // parts
    own_heads = share // HEAD
    vp_ref[0:EDGE, :] = jnp.zeros((EDGE, wide), BF)
    vp_ref[slot + EDGE : slot + 2 * EDGE, :] = jnp.zeros((EDGE, wide), BF)

    def columns(start, width):
        if own:
            return weight[:, :, :, :, :, start : start + width].reshape(-1, width)
        return weight[:, start : start + width]

    def valid_of(i, rows):
        row = lax.broadcasted_iota(jnp.int32, (rows, 1), 0) + i * rows
        return (row < length).astype(F32)

    def load(i, carry):
        rows = pl.ds(pl.multiple_of(i * TALL, TALL), TALL)
        few = pl.ds(pl.multiple_of(i * (TALL // 16), TALL // 16), TALL // 16)
        factor = valid_of(i, TALL) * scale
        for p in range(parts):
            both = mm(x_ref[rows, :], columns(3 * p * share, 2 * share)) * factor
            at = slice(p * share, (p + 1) * share)
            high, low = halves(both)
            qh_ref[rows, at] = high[:, :share]
            kh_ref[rows, at] = high[:, share:]
            means = mm(avg, high) + mm(avg, low)
            small_ref[0, few, at] = means[:, :share]
            small_ref[1, few, at] = means[:, share:]
        return carry

    lax.fori_loop(0, slot // TALL, load, 0)
    mask = block_mask()
    pmask, one = pair_consts()
    pairs = 2 * groups

    for j in range(pairs):
        at = pair_lanes(j)
        ql, kl = unfold(small_ref[0, :, at], pmask), unfold(small_ref[1, :, at], pmask)
        a2 = jnp.where(pmask, mm3f(ql, kl, NT), -1e30)
        e2 = jnp.where(pmask, jnp.exp(a2 - jnp.max(a2, axis=1, keepdims=True)), 0.0)
        k2 = e2 / jnp.sum(e2, axis=1, keepdims=True)
        top = segment_reduce(jnp.sum(k2, axis=0, keepdims=True), -1e30, jnp.max)
        k2_ref[j] = lhs(k2)
        small_ref[2, :, at] = fold(k2)
        z_ref[j] = jnp.transpose(k2) / top

    def newton(step, carry):
        for j in range(pairs):
            at = pair_lanes(j)
            z = z_ref[j]
            p = pair_mm(k2_ref[j], rhs(z))
            left = lhs(p)
            t2 = 15.0 * one - pair_mm(left, rhs(7.0 * one - p))
            t3 = 13.0 * one - pair_mm(left, rhs(t2))
            chain_ref[step, 0, :, at] = fold(z)
            chain_ref[step, 1, :, at] = fold(p)
            chain_ref[step, 2, :, at] = fold(t2)
            chain_ref[step, 3, :, at] = fold(t3)
            z_ref[j] = 0.25 * pair_mm(lhs(z), rhs(t3))
        return carry

    lax.fori_loop(0, STEPS // 2, newton, 0)
    advance()
    lax.fori_loop(STEPS // 2, STEPS, newton, 0)
    advance()

    def load_values(i, carry):
        rows = pl.ds(pl.multiple_of(i * TALL + EDGE, EDGE), TALL)
        valid = valid_of(i, TALL)
        x = x_ref[pl.ds(pl.multiple_of(i * TALL, TALL), TALL), :]
        for p in range(parts):
            value = mm(x, columns((3 * p + 2) * share, share)) * valid
            vp_ref[rows, p * share : (p + 1) * share] = value.astype(BF)
        return carry

    lax.fori_loop(0, slot // TALL, load_values, 0)

    for g in range(groups):
        at = lanes_of(g)
        ql = spread(small_ref[0, :, at], mask).astype(BF)
        top_ref[...] = jnp.full(top_ref.shape, -jnp.inf, F32)

        def scores(i, carry):
            rows = pl.ds(pl.multiple_of(i * ROWS, ROWS), ROWS)
            row = lax.broadcasted_iota(jnp.int32, (ROWS, 1), 0) + i * ROWS
            a3 = jnp.where(row < length, mm(kh_ref[rows, at], ql, NT), -1e9)
            s_ref[rows, :] = a3
            top_ref[0:1, :] = jnp.maximum(top_ref[0:1, :], jnp.max(a3, axis=0, keepdims=True))
            return carry

        lax.fori_loop(0, count, scores, 0)
        peak = top_ref[0:1, :]
        top_ref[0:1, :] = jnp.zeros((1, WIDE), F32)

        def powers(i, carry):
            rows = pl.ds(pl.multiple_of(i * ROWS, ROWS), ROWS)
            e3 = jnp.exp(s_ref[rows, :] - peak)
            s_ref[rows, :] = e3
            top_ref[0:1, :] += jnp.sum(e3, axis=0, keepdims=True)
            return carry

        lax.fori_loop(0, count, powers, 0)
        inverse = 1.0 / top_ref[0:1, :]

        def weigh(i, carry):
            rows = pl.ds(pl.multiple_of(i * ROWS, ROWS), ROWS)
            k3_ref[rows, at] = (s_ref[rows, :] * inverse).astype(BF)
            return carry

        lax.fori_loop(0, count, weigh, 0)
        b = mm(k3_ref[:, at], vp_ref[EDGE : slot + EDGE, at], TN)
        b = jnp.where(mask, b, 0.0)
        for sub in range(2):
            j, inner = 2 * g + sub, pair_lanes(sub)
            z, piece = z_ref[j], b[inner, inner]
            small_ref[3, :, pair_lanes(j)] = fold(piece)
            small_ref[4, :, pair_lanes(j)] = fold(mm3f(z, piece))
            small_ref[5, :, pair_lanes(j)] = fold(z)
        t_ref[...] = toeplitz(taps_ref, TAPS_AT, own_heads, g)
        cb = spread(small_ref[4, :, at], mask).astype(BF)
        kl = spread(small_ref[1, :, at], mask).astype(BF)
        ones = mask.astype(F32).astype(BF)

        def mix(i, carry):
            rows = pl.ds(pl.multiple_of(i * ROWS, ROWS), ROWS)
            a1 = mm(qh_ref[rows, at], kl, NT)
            e1 = jnp.exp(a1 - segment_reduce(a1, -jnp.inf, jnp.max)).astype(BF)
            k1 = (e1.astype(F32) / mm(e1, ones)).astype(BF)
            k1_ref[rows, at] = k1
            window = vp_ref[pl.ds(pl.multiple_of(i * ROWS, ROWS), WINDOW), at]
            ctx_ref[rows, at] = (
                mm(k1, cb) + diagonal_lanes(mm(t_ref[...], window))
            ).astype(BF)
            return carry

        lax.fori_loop(0, count, mix, 0)
        if g < 2:
            advance()

    while slots:
        advance()


def attn_bwd_kernel(slot, groups, parts, own, *refs):
    (len_ref, g_ref, qh_ref, kh_ref, vp_ref, k1_ref, k3_ref, small_ref, chain_ref, taps_ref,
     xt_ref, w_ref, dres_ref, block_ref) = refs[:14]
    if own:
        fulls, refs = refs[14:17], refs[17:]
        outs, refs = refs[:4], refs[4:]
    else:
        outs, refs = (refs[14],), refs[15:]
    dx_ref, sum_ref = refs[:2]
    (dqkv_ref, gp_ref, da1_ref, da3_ref, dk_ref, dz_ref, k2_ref,
     dql_ref, dkl_ref, t_ref, acc_ref) = refs[2:13]
    todo = {}
    if own:
        grad_ref, totals, landed = refs[13:16]
        place = Place()
        greet(place)
        scatters = scatter_parts(place, SCATTERS, fulls + (grad_ref,), outs, refs[16:])
        total = Total(place, totals.at[0], sum_ref, totals, landed, refs[-3], refs[-2],
                      SUM_COPIES * len(SCATTERS))
        todo = SCATTER_AT
    else:
        grad_ref = outs[0]
        totals = sum_ref

    def advance(name):
        for which, stage in todo.get(name, ()):
            if which == "t":
                total.run(stage)
            else:
                for part, wave in zip(scatters, SCATTER_WAVES):
                    if wave == which:
                        part.run(stage)

    advance("start")
    count = slot // ROWS
    marks = ROWS // 16
    scale = HEAD ** -0.25
    length = len_ref[0]
    wide = groups * WIDE
    share = wide // parts
    own_heads = share // HEAD
    pairs = 2 * groups
    mask = block_mask()
    pmask, one = pair_consts()
    ones = mask.astype(F32).astype(BF)
    gp_ref[0:EDGE, :] = jnp.zeros((EDGE, wide), BF)
    gp_ref[slot + EDGE : slot + 2 * EDGE, :] = jnp.zeros((EDGE, wide), BF)
    gp_ref[EDGE : slot + EDGE, :] = g_ref[...]
    col = lax.broadcasted_iota(jnp.int32, (ROWS, WIDE), 1) // HEAD
    up, across = grid_of((ROWS, ROWS))
    flip = jnp.where(up + across == ROWS - 1, 1.0, 0.0).astype(BF)
    taps_lane = lax.broadcasted_iota(jnp.int32, (1, 128), 1) < TAPS

    def totals_row(row):
        return (0, slice(row, row + 1)) if own else slice(row, row + 1)

    if own:
        totals[0] = block_ref[...]
    else:
        sum_ref[...] = block_ref[...]

    for g in range(groups):
        at = lanes_of(g)
        cb = spread(small_ref[4, :, at], mask).astype(BF)

        def first(i, carry):
            rows = pl.ds(pl.multiple_of(i * ROWS, ROWS), ROWS)
            k1 = k1_ref[rows, at].astype(F32)
            dk1 = mm(g_ref[rows, at], cb, NT)
            high, low = halves(dk1 * k1)
            da1_ref[rows, at] = (k1 * (dk1 - (mm(high, ones) + mm(low, ones)))).astype(BF)
            return carry

        lax.fori_loop(0, count, first, 0)
        advance(f"first{g}")
        dc = jnp.where(mask, mm(k1_ref[:, at], g_ref[:, at], TN), 0.0)
        dkl_ref[:, at] = gather_up(jnp.where(mask, mm(da1_ref[:, at], qh_ref[:, at], TN), 0.0))
        many = jnp.ones((8, 128), BF)
        totals_of = []
        for sub in range(2):
            j, inner = 2 * g + sub, pair_lanes(sub)
            b, z = (unfold(small_ref[n, :, pair_lanes(j)], pmask) for n in (3, 5))
            piece = halves(dc[inner, inner])
            dz_ref[j] = mm3(halves(b), piece, NT)
            db = mm3(halves(z), piece, TN)
            dql_ref[:, pair_lanes(j)] = fold(db)
            high, low = halves(db * b)
            totals_of.append((mm(many, high, NT) + mm(many, low, NT))[0:1, :])
        peak = jnp.concatenate(totals_of, axis=1)
        dbb = spread(dql_ref[:, at], mask).astype(BF)
        t_ref[...] = toeplitz(taps_ref, FLIP_AT, own_heads, g)
        acc_ref[...] = jnp.zeros(acc_ref.shape, F32)

        def second(i, carry):
            rows = pl.ds(pl.multiple_of(i * ROWS, ROWS), ROWS)
            row = lax.broadcasted_iota(jnp.int32, (ROWS, 1), 0) + i * ROWS
            valid = (row < length).astype(F32)
            k3 = k3_ref[rows, at]
            vh = vp_ref[pl.ds(pl.multiple_of(i * ROWS + EDGE, EDGE), ROWS), at]
            dk3 = mm(vh, dbb, NT)
            da3_ref[rows, at] = (k3.astype(F32) * (dk3 - peak)).astype(BF)
            window = pl.ds(pl.multiple_of(i * ROWS, ROWS), WINDOW)
            dv = mm(k3, dbb) + diagonal_lanes(mm(t_ref[...], gp_ref[window, at]))
            put(dqkv_ref, rows, 2, wide, parts, g * WIDE, (dv * valid).astype(BF))
            grad = g_ref[rows, at]
            split = jnp.concatenate(
                [jnp.where(col == h, grad, jnp.zeros_like(grad)) for h in range(PACK)], axis=0
            )
            acc_ref[:, :WINDOW] += mm(split, vp_ref[window, at], NT)
            return carry

        lax.fori_loop(0, count, second, 0)
        for h in range(PACK):
            high, low = halves(acc_ref[h * ROWS : (h + 1) * ROWS, :])
            turned = pltpu.roll(mm(flip, high) + mm(flip, low), 0, 1, stride=1, stride_axis=0)
            line = pltpu.roll(jnp.sum(turned, axis=0, keepdims=True), 129, 1)[:, :128]
            totals[totals_row(24 + g * PACK + h)] = jnp.where(taps_lane, line, 0.0)
        dql_ref[:, at] = gather_up(jnp.where(mask, mm(da3_ref[:, at], kh_ref[:, at], TN), 0.0))
        advance(f"second{g}")

    def weight_grad(start, width):
        for p in range(parts):
            lanes = slice(3 * p * share + start, 3 * p * share + start + width)
            for block in range(4):
                size = xt_ref.shape[0] // 4
                here = mm(xt_ref[block * size : (block + 1) * size, :], dqkv_ref[:, lanes]).astype(BF)
                if own:
                    rows = grad_ref.shape[-2]
                    grad_ref[block // 2, block % 2, :, :, :, lanes] = here.reshape(2, 2, rows, width)
                else:
                    grad_ref[block * size : (block + 1) * size, lanes] = here

    weight_grad(2 * share, share)
    advance("values")
    for j in range(pairs):
        dk_ref[j] = jnp.zeros((128, 128), F32)
        k2_ref[j] = unfold(small_ref[2, :, pair_lanes(j)], pmask)

    def newton(back, carry):
        step = STEPS - 1 - back
        for j in range(pairs):
            at = pair_lanes(j)
            z, p, t2, t3 = (unfold(chain_ref[step, n, :, at], pmask) for n in range(KEPT))
            p_right = rhs(p)
            z_left = lhs(z)
            dz = 0.25 * dz_ref[j]
            dt3 = pair_mm(lhs(dz), rhs(z))
            dt2 = -pair_mm(lhs(dt3), p_right)
            dp = pair_mm(lhs(dt2), p_right) - pair_mm(lhs(t2), rhs(dt3)) - pair_mm(
                lhs(7.0 * one - p), rhs(dt2)
            )
            dk_ref[j] += pair_mm(z_left, rhs(dp))
            dz_ref[j] = pair_mm(lhs(t3), rhs(dz)) + pair_mm(lhs(dp), rhs(k2_ref[j]))
        return carry

    for third_of in range(3):
        lax.fori_loop(third_of * STEPS // 3, (third_of + 1) * STEPS // 3, newton, 0)
        advance(f"newton{third_of}")

    for j in range(pairs):
        at = pair_lanes(j)
        k2 = k2_ref[j]
        sums = jnp.sum(k2, axis=0, keepdims=True)
        top = segment_reduce(sums, -1e30, jnp.max)
        hit = (sums == top).astype(F32)
        ties = segment_reduce(hit, 0.0, jnp.sum)
        dz0 = dz_ref[j]
        dtop = -segment_reduce(jnp.sum(dz0 * k2, axis=0, keepdims=True), 0.0, jnp.sum) / (top * top)
        dk2 = jnp.where(pmask, jnp.transpose(dk_ref[j]) + dz0 / top + hit * (dtop / ties), 0.0)
        da2 = halves(k2 * (dk2 - jnp.sum(dk2 * k2, axis=1, keepdims=True)))
        qls, kls = (halves(unfold(small_ref[n, :, at], pmask)) for n in (0, 1))
        dql_ref[:, at] += fold(mm3(da2, kls))
        dkl_ref[:, at] += fold(mm3(da2, qls, TN))
    back = average_back()

    for g in range(groups):
        at = lanes_of(g)
        qlb, klb = (spread(small_ref[n, :, at].astype(BF), mask) for n in (0, 1))

        def third(i, carry):
            rows = pl.ds(pl.multiple_of(i * ROWS, ROWS), ROWS)
            few = pl.ds(pl.multiple_of(i * marks, marks), marks)
            row = lax.broadcasted_iota(jnp.int32, (ROWS, 1), 0) + i * ROWS
            valid = jnp.where(row < length, scale, 0.0)
            dq = mm(da1_ref[rows, at], klb) + mm(back, dql_ref[few, at].astype(BF))
            dk = mm(da3_ref[rows, at], qlb) + mm(back, dkl_ref[few, at].astype(BF))
            put(dqkv_ref, rows, 0, wide, parts, g * WIDE, (dq * valid).astype(BF))
            put(dqkv_ref, rows, 1, wide, parts, g * WIDE, (dk * valid).astype(BF))
            return carry

        lax.fori_loop(0, count, third, 0)
        advance(f"third{g}")

    weight_grad(0, 2 * share)
    advance("keys")
    for i in range(slot // TALL):
        rows = slice(i * TALL, (i + 1) * TALL)
        dx_ref[rows, :] = (dres_ref[rows, :] + mm(dqkv_ref[rows, :], w_ref[...], NT)).astype(BF)
        advance(f"input{i}")
    advance("end")


VM = pl.BlockSpec(memory_space=pltpu.VMEM)
SM = pl.BlockSpec(memory_space=pltpu.SMEM)
LIMIT = 60 * 1024 * 1024


def attn_fwd(length, x, parts, own, weights):
    slot, wide = x.shape
    groups = wide // WIDE
    shape = jax.ShapeDtypeStruct
    talks = dict(collective_id=1, has_side_effects=True) if own else {}
    gathered = gather_shapes(weights) if own else ()
    outs = pl.pallas_call(
        partial(attn_fwd_kernel, slot, groups, parts, own),
        out_shape=gathered
        + (
            shape((slot, wide), BF),
            shape((slot, wide), BF),
            shape((slot, wide), BF),
            shape((slot + 2 * EDGE, wide), BF),
            shape((slot, wide), BF),
            shape((slot, wide), BF),
            shape((6, MARKS, wide), F32),
            shape((STEPS, KEPT, MARKS, wide), F32),
        ),
        in_specs=[SM, VM] + [VM] * len(weights),
        out_specs=([VM, VM, ANY, ANY, ANY] if own else []) + [VM] * 8,
        scratch_shapes=[
            pltpu.VMEM((2 * groups, 128, 128), F32),
            pltpu.VMEM((2 * groups, 128, 256), BF),
            pltpu.VMEM((slot, WIDE), F32),
            pltpu.VMEM((8, WIDE), F32),
            pltpu.VMEM((PACK * ROWS, WINDOW), BF),
        ]
        + (gather_scratch(GATHERS) if own else []),
        compiler_params=pltpu.CompilerParams(vmem_limit_bytes=LIMIT, **talks),
        name="attn_fwd",
    )(length, x, *weights)
    return outs[: len(gathered)], outs[len(gathered) :]


def attn_bwd(length, g, saved, taps, xt, weight, dres, block, parts, own, fulls):
    slot, wide = g.shape
    groups = wide // WIDE
    shape = jax.ShapeDtypeStruct
    talks = dict(collective_id=2, has_side_effects=True) if own else {}
    ends = (shape((slot, wide), BF), shape(block.shape, F32))
    if own:
        rows = fulls[0].shape[0] // 16
        fulls = [f.reshape(2, 2, 2, 2, rows, f.shape[1]) for f in fulls]
        outs = tuple(shape((rows, f.shape[-1] // 2), F32) for f in fulls) + (
            shape((rows, 3 * wide // 2), F32),
        )
        extra = [
            pltpu.VMEM((2, 2, 2, 2, rows, 3 * wide), BF),
            pltpu.VMEM((6,) + block.shape, F32),
            pltpu.VMEM((5,) + block.shape, F32),
        ] + all_scatter_scratch(SCATTERS, rows, 5)
    else:
        fulls, extra = [], []
        outs = (shape((wide, 3 * wide), BF),)
    return pl.pallas_call(
        partial(attn_bwd_kernel, slot, groups, parts, own),
        out_shape=outs + ends,
        in_specs=[SM] + [VM] * 13 + [ANY] * len(fulls),
        out_specs=[VM] * (len(outs) + 2),
        scratch_shapes=[
            pltpu.VMEM((slot, 3 * wide), BF),
            pltpu.VMEM((slot + 2 * EDGE, wide), BF),
            pltpu.VMEM((slot, wide), BF),
            pltpu.VMEM((slot, wide), BF),
            pltpu.VMEM((2 * groups, 128, 128), F32),
            pltpu.VMEM((2 * groups, 128, 128), F32),
            pltpu.VMEM((2 * groups, 128, 128), F32),
            pltpu.VMEM((MARKS, wide), F32),
            pltpu.VMEM((MARKS, wide), F32),
            pltpu.VMEM((PACK * ROWS, WINDOW), BF),
            pltpu.VMEM((PACK * ROWS, 256), F32),
        ]
        + extra,
        compiler_params=pltpu.CompilerParams(vmem_limit_bytes=67043328, **talks),
        name="attn_bwd",
    )(length, g, *saved, taps, xt, weight, dres, block, *fulls)
MESH = pl.DeviceIdType.MESH
WAYS = ("zh", "zl", "y", "x", "c")
COPIES = 11
STAGES = 6


class Place:
    def __init__(self):
        dp = lax.axis_index("dp")
        self.x = lax.axis_index("tensor")
        self.zh, self.zl = dp // 8, (dp // 4) % 2
        self.y, self.c = (dp // 2) % 2, dp % 2

    def at(self, way):
        spot = {w: getattr(self, w) for w in WAYS}
        spot[way] = 1 - spot[way]
        return {
            "dp": spot["zh"] * 8 + spot["zl"] * 4 + spot["y"] * 2 + spot["c"],
            "tensor": spot["x"],
        }


def greet(place):
    barrier = pltpu.get_barrier_semaphore()
    for way in WAYS:
        pl.semaphore_signal(barrier, inc=1, device_id=place.at(way), device_id_type=MESH)
    pl.semaphore_wait(barrier, len(WAYS))


class Mover:
    def __init__(self, place, send, recv, base):
        self.place, self.send, self.recv, self.base = place, send, recv, base
        self.started = []

    def copy(self, index, src, dst, way):
        return pltpu.make_async_remote_copy(
            src_ref=src, dst_ref=dst,
            send_sem=self.send.at[self.base + index], recv_sem=self.recv.at[self.base + index],
            device_id=self.place.at(way), device_id_type=MESH,
        )

    def push(self, index, src, dst, way):
        copy = self.copy(index, src, dst, way)
        copy.start()
        self.started.append(copy)

    def arrive(self, index, ref, way):
        self.copy(index, ref, ref, way).wait_recv()

    def drain(self):
        for copy in self.started:
            copy.wait_send()


class Gather(Mover):
    def __init__(self, place, shard, whole, lane, width, order, send, recv, base, local):
        super().__init__(place, send, recv, base)
        self.shard, self.whole, self.local = shard.at[:, pl.ds(lane, width)], whole, local
        self.lane, self.width, self.order = lane, width, order

    def view(self, zh, zl, y, c, x):
        half = self.whole.shape[-1] // 2
        lanes = pl.ds(pl.multiple_of(x * half + self.lane, 128), self.width)
        return self.whole.at[zh, zl, y, c, :, lanes]

    def steps(self, c):
        p, every = self.place, slice(None)
        yield "zh", [self.view(p.zh, p.zl, p.y, c, p.x)], [self.view(1 - p.zh, p.zl, p.y, c, p.x)]
        yield "zl", [self.view(every, p.zl, p.y, c, p.x)], [self.view(every, 1 - p.zl, p.y, c, p.x)]
        if self.order == "yx":
            yield "y", [self.view(every, every, p.y, c, p.x)], [self.view(every, every, 1 - p.y, c, p.x)]
            yield "x", [self.view(every, every, every, c, p.x)], [self.view(every, every, every, c, 1 - p.x)]
        else:
            yield "x", [self.view(every, every, p.y, c, p.x)], [self.view(every, every, p.y, c, 1 - p.x)]
            yield (
                "y",
                [self.view(every, every, p.y, c, x) for x in (0, 1)],
                [self.view(every, every, 1 - p.y, c, x) for x in (0, 1)],
            )

    def run(self, stage):
        p = self.place
        here = self.view(p.zh, p.zl, p.y, p.c, p.x)
        if stage == 0:
            self.mine, self.other = list(self.steps(p.c)), list(self.steps(1 - p.c))
            self.push(0, self.shard, here, "zh")
            self.push(5, self.shard, here, "c")
            self.own = pltpu.make_async_copy(self.shard, here, self.local)
            self.own.start()
        elif stage < 5:
            way, _, landed = self.mine[stage - 1]
            for i, ref in enumerate(landed):
                self.arrive(stage - 1 + i, ref, way)
            if stage == 1:
                self.own.wait()
            if stage < 4:
                way, outgoing, _ = self.mine[stage]
                for i, ref in enumerate(outgoing):
                    self.push(stage + i, ref, ref, way)
            for i, ref in enumerate(landed):
                self.push(5 + stage + i, ref, ref, "c")
        else:
            self.arrive(5, self.view(p.zh, p.zl, p.y, 1 - p.c, p.x), "c")
            for k in range(4):
                for i, ref in enumerate(self.other[k][2]):
                    self.arrive(6 + k + i, ref, "c")
            self.drain()


class Scatter(Mover):
    def __init__(self, place, full, lane, width, order, out, bufs, send, recv, base, local):
        super().__init__(place, send, recv, base)
        self.full, self.lane, self.width, self.order = full, lane, width, order
        self.out, self.local = out, local
        self.sums, self.in_c, self.in_1, self.in_2, self.in_l, self.in_h = bufs

    def lanes(self, x):
        half = self.full.shape[-1] // 2
        return pl.ds(x * half + self.lane, self.width)

    def add(self, target, landed):
        lead = landed.shape[:-2]
        total = 1
        for n in lead:
            total *= n
        flat_dims = lead

        def one(i, carry):
            index = []
            for n in reversed(flat_dims):
                index.append(i % n)
                i = i // n
            index = tuple(reversed(index))
            target[index] = target[index] + landed[index]
            return carry

        if total == 1:
            one(0, 0)
        else:
            lax.fori_loop(0, total, one, 0)

    def run(self, stage):
        p, every = self.place, slice(None)
        if stage == 0:
            self.loads = []
            for x in (0, 1):
                self.push(x, self.full.at[:, :, :, 1 - p.c, :, self.lanes(x)], self.in_c.at[x], "c")
                load = pltpu.make_async_copy(
                    self.full.at[:, :, :, p.c, :, self.lanes(x)], self.sums.at[x], self.local.at[x]
                )
                load.start()
                self.loads.append(load)
            return
        if stage == 1:
            for x in (0, 1):
                self.arrive(x, self.in_c.at[x], "c")
                self.loads[x].wait()
            self.add(self.sums, self.in_c)
            if self.order == "xy":
                self.push(2, self.sums.at[1 - p.x], self.in_1.at[...], "x")
            else:
                for x in (0, 1):
                    self.push(2 + x, self.sums.at[x, :, :, 1 - p.y], self.in_1.at[x], "y")
        elif stage == 2:
            if self.order == "xy":
                self.arrive(2, self.in_1, "x")
                self.add(self.sums.at[p.x], self.in_1)
                self.push(4, self.sums.at[p.x, :, :, 1 - p.y], self.in_2, "y")
            else:
                for x in (0, 1):
                    self.arrive(2 + x, self.in_1.at[x], "y")
                    self.add(self.sums.at[x, :, :, p.y], self.in_1.at[x])
                self.push(4, self.sums.at[1 - p.x, :, :, p.y], self.in_2, "x")
        elif stage == 3:
            self.arrive(4, self.in_2, "y" if self.order == "xy" else "x")
            self.add(self.sums.at[p.x, :, :, p.y], self.in_2)
            self.push(5, self.sums.at[p.x, :, 1 - p.zl, p.y], self.in_l, "zl")
        elif stage == 4:
            self.arrive(5, self.in_l, "zl")
            self.add(self.sums.at[p.x, :, p.zl, p.y], self.in_l)
            self.push(6, self.sums.at[p.x, 1 - p.zh, p.zl, p.y], self.in_h, "zh")
        else:
            self.arrive(6, self.in_h, "zh")
            self.out[:, self.lane : self.lane + self.width] = (
                self.sums[p.x, p.zh, p.zl, p.y].astype(F32) + self.in_h[...].astype(F32)
            )
            self.drain()


def scatter_scratch(rows, width, order):
    first = (2, 2, 2) if order == "xy" else (2, 2, 2)
    return [
        pltpu.VMEM((2, 2, 2, 2, rows, width), BF),
        pltpu.VMEM((2, 2, 2, 2, rows, width), BF),
        pltpu.VMEM(first + (rows, width), BF),
        pltpu.VMEM((2, 2, rows, width), BF),
        pltpu.VMEM((2, rows, width), BF),
        pltpu.VMEM((rows, width), BF),
    ]


class Total(Mover):
    def __init__(self, place, block, out, sums, landed, send, recv, base):
        super().__init__(place, send, recv, base)
        self.block, self.out, self.sums, self.landed = block, out, sums, landed

    def run(self, stage):
        if stage > 0:
            self.arrive(stage - 1, self.landed.at[stage - 1], WAYS[stage - 1])
            self.sums[stage] = self.sums[stage - 1] + self.landed[stage - 1]
        if stage < 5:
            self.push(stage, self.sums.at[stage], self.landed.at[stage], WAYS[stage])
        else:
            self.out[...] = self.sums[5]
            self.drain()


GATHERS = (
    (0, 0, 384, "yx"), (0, 384, 384, "xy"), (1, 0, 128, "yx"),
    (0, 768, 384, "yx"), (2, 0, 384, "xy"), (3, 0, 768, "yx"), (3, 768, 768, "xy"),
    (4, 0, 768, "yx"), (4, 768, 768, "xy"),
)
GATHER_LAGS = (0, 0, 0, 2, 2, 2, 2, 4, 4)
SCATTERS = (
    (1, 0, 768, "xy"), (1, 768, 768, "yx"), (0, 0, 384, "yx"),
    (2, 0, 768, "xy"), (2, 768, 768, "yx"),
    (3, 768, 256, "xy"), (3, 1024, 128, "yx"),
    (3, 0, 384, "xy"), (3, 384, 384, "yx"),
)
SCATTER_WAVES = "aaabbvvkk"
SCATTER_AT = {
    "start": (("a", 0), ("b", 0)),
    "first0": (("a", 1),),
    "second0": (("b", 1),),
    "first2": (("a", 2),),
    "second2": (("t", 0),),
    "values": (("v", 0), ("t", 1)),
    "newton0": (("b", 2), ("t", 2), ("v", 1)),
    "newton1": (("a", 3), ("t", 3)),
    "newton2": (("t", 4),),
    "third0": (("b", 3), ("a", 4)),
    "third1": (("v", 2), ("t", 5)),
    "third2": (("b", 4), ("a", 5)),
    "keys": (("k", 0), ("v", 3), ("b", 5)),
    "input0": (("k", 1), ("v", 4)),
    "input1": (("k", 2),),
    "input2": (("v", 5),),
    "input3": (("k", 3),),
    "end": (("k", 4), ("k", 5)),
}


def schedule(parts, lags):
    slots = [[] for _ in range(STAGES + max(lags))]
    for part, lag in zip(parts, lags):
        for stage in range(STAGES):
            slots[stage + lag].append(partial(part.run, stage))
    return slots


def gather_parts(place, cuts, shards, wholes, send, recv, local):
    return [
        Gather(place, shards[i], wholes[i], lane, width, order, send, recv, COPIES * n, local.at[n])
        for n, (i, lane, width, order) in enumerate(cuts)
    ]


def gather_scratch(cuts):
    n = len(cuts)
    return [
        pltpu.SemaphoreType.DMA((COPIES * n,)),
        pltpu.SemaphoreType.DMA((COPIES * n,)),
        pltpu.SemaphoreType.DMA((n,)),
    ]


def gather_shapes(shards):
    return tuple(
        jax.ShapeDtypeStruct((2, 2, 2, 2, s.shape[0], 2 * s.shape[1]), s.dtype) for s in shards
    )


SUM_COPIES = 7


def scatter_parts(place, cuts, fulls, outs, refs):
    send, recv, local = refs[-3:]
    return [
        Scatter(place, fulls[i], lane, width, order, outs[i], refs[6 * n : 6 * n + 6],
                send, recv, SUM_COPIES * n, local.at[n])
        for n, (i, lane, width, order) in enumerate(cuts)
    ]


def all_scatter_scratch(cuts, rows, extra=0):
    out = []
    for _, _, width, order in cuts:
        out += scatter_scratch(rows, width, order)
    n = len(cuts)
    return out + [
        pltpu.SemaphoreType.DMA((SUM_COPIES * n + extra,)),
        pltpu.SemaphoreType.DMA((SUM_COPIES * n + extra,)),
        pltpu.SemaphoreType.DMA((n, 2)),
    ]


D = 768
BOTH = ("tensor", "dp")


def rows_sum(left_op, right_op):
    return lax.dot_general(left_op, right_op, (TN, ((), ())), preferred_element_type=F32)


def cols_sum(left_op, right_op):
    return lax.dot_general(left_op, right_op, (NT, ((), ())), preferred_element_type=F32)


def dense(left_op, right_op):
    return jnp.dot(left_op, right_op, preferred_element_type=F32)


def norm_parts(values):
    centre = values - jnp.mean(values, axis=-1, keepdims=True)
    spread_of = jnp.mean(centre * centre, axis=-1, keepdims=True)
    inverse = lax.rsqrt(spread_of + 1e-05)
    return centre * inverse, inverse


def norm_back(grad, gain, normal, inverse):
    scaled = grad * gain
    lean = jnp.mean(scaled, axis=-1, keepdims=True)
    along = jnp.mean(scaled * normal, axis=-1, keepdims=True)
    return (
        inverse * (scaled - lean - normal * along),
        jnp.sum(grad * normal, axis=0),
        jnp.sum(grad, axis=0),
    )


def gather_plain(pieces):
    sizes = lax.axis_size("tensor"), lax.axis_size("dp")
    out = []
    for piece in pieces:
        joined = lax.all_gather(piece, BOTH, axis=0, tiled=True)
        joined = joined.reshape(sizes[0], sizes[1] * piece.shape[0], piece.shape[1])
        out.append(joined.transpose(1, 0, 2).reshape(joined.shape[1], -1))
    return out


def scatter_plain(fulls):
    parts = lax.axis_size("tensor")
    out = []
    for full in fulls:
        stacked = full.reshape(full.shape[0], parts, -1).transpose(1, 0, 2).reshape(-1, full.shape[1] // parts)
        out.append(lax.psum_scatter(stacked, BOTH, scatter_dimension=0, tiled=True).astype(F32))
    return out


def per_device(own, x_in, lengths, cotangent, w_query, w_key, w_value, w_out, w_in, w_down,
               conv_weight, ln1_gain, ln1_bias, ln2_gain, ln2_bias):
    tensor_index = lax.axis_index("tensor")
    slot = x_in.shape[0]
    parts = lax.axis_size("tensor")
    length = lax.dynamic_slice_in_dim(lengths, tensor_index, 1)
    valid = (jnp.arange(slot, dtype=jnp.int32) < length[0]).astype(F32)[:, None]

    first = jnp.concatenate([w_query, w_key, w_value], axis=1)
    later = (w_out.T, w_in, w_down.T)
    few, own_heads, count = ln1_gain.shape[0], conv_weight.shape[0], conv_weight.shape[1]

    def rows_of(array, rows):
        return jnp.pad(array, ((0, rows - array.shape[0]), (0, 128 - array.shape[1])))

    vectors = jnp.stack([ln1_gain, ln1_bias, ln2_gain, ln2_bias])
    block = jnp.concatenate(
        [rows_of(vectors, TAPS_AT), rows_of(conv_weight, FLIP_AT - TAPS_AT),
         rows_of(conv_weight[:, ::-1], BLOCK - FLIP_AT)],
        axis=0,
    )
    if own:
        wholes, saved = attn_fwd(length, x_in, parts, own, (first, block) + later)
        qkv_w, blocks, out_w, in_w, down_w = (w.reshape(-1, w.shape[-1]) for w in wholes)
        taps = blocks[:BLOCK]
        blocks = blocks.reshape(lax.axis_size("dp"), BLOCK, parts, 128)
    else:
        qkv_w, out_w, in_w, down_w = gather_plain((first,) + later)
        blocks = lax.all_gather(block, ("dp", "tensor"), axis=0)
        blocks = blocks.reshape(-1, parts, BLOCK, 128).transpose(0, 2, 1, 3)
        taps = blocks[0].reshape(BLOCK, parts * 128)
        _, saved = attn_fwd(length, x_in, parts, own, (qkv_w, taps))
    gains = blocks[:, :4, :, :few].transpose(1, 0, 2, 3).reshape(4, D)
    gain_one, bias_one, gain_two, bias_two = gains[0], gains[1], gains[2], gains[3]
    ctx, saved = saved[0], saved[1:]

    tokens = x_in.astype(F32)
    attn_branch = cols_sum(ctx, out_w)
    normal_one, inverse_one = norm_parts(tokens + attn_branch)
    hidden = (normal_one * gain_one + bias_one).astype(BF)
    pre = dense(hidden, in_w)
    below = 0.5 * (1.0 + lax.erf(pre * 0.5**0.5))
    act = (pre * below).astype(BF)
    slope = (below + pre * jnp.exp(-0.5 * pre * pre) * (2.0 * jnp.pi) ** -0.5).astype(BF)
    ffn_branch = cols_sum(act, down_w)
    normal_two, inverse_two = norm_parts(hidden.astype(F32) + ffn_branch)
    output = (normal_two * gain_two + bias_two).astype(BF)
    grad_result = cotangent.astype(F32) * valid
    d_res2, grad_gain_two, grad_bias_two = norm_back(grad_result, gain_two, normal_two, inverse_two)
    d_ffn = d_res2.astype(BF)
    grad_down = rows_sum(d_ffn, act)
    d_pre = (dense(d_ffn, down_w) * slope.astype(F32)).astype(BF)
    grad_in = rows_sum(hidden, d_pre)
    d_hidden = cols_sum(d_pre, in_w) + d_res2
    d_res1, grad_gain_one, grad_bias_one = norm_back(d_hidden, gain_one, normal_one, inverse_one)
    d_attn = d_res1.astype(BF)
    grad_out = rows_sum(d_attn, ctx)
    d_ctx = dense(d_attn, out_w).astype(BF)
    fulls = [grad_out.astype(BF), grad_in.astype(BF), grad_down.astype(BF)]

    def total(branch):
        return jnp.sum(valid * branch * branch)

    sums = jnp.stack([total(tokens), total(attn_branch), total(ffn_branch), jnp.sum(valid)])
    ends = jnp.concatenate(
        [
            jnp.stack([grad_gain_one, grad_bias_one, grad_gain_two, grad_bias_two]).reshape(24, 128),
            jnp.zeros((12, 128), F32),
            jnp.pad(sums[None], ((0, 3), (0, 124))),
        ],
        axis=0,
    )
    grads = attn_bwd(length, d_ctx, saved, taps, x_in.T, qkv_w, d_res1, ends, parts, own, fulls)
    input_grad, summed = grads[-2:]
    if own:
        early, late = grads[:3], grads[3]
    else:
        early, (late,) = scatter_plain(fulls), scatter_plain([grads[0]])
        summed = lax.psum(summed, ("dp", "tensor"))
    share = D // lax.axis_size(("dp", "tensor"))
    start_at = lax.axis_index(("dp", "tensor")) * share
    vectors = lax.dynamic_slice_in_dim(summed[:24].reshape(4, D), start_at, share, 1)
    conv_grad = lax.dynamic_slice_in_dim(summed, 24 + tensor_index * own_heads, own_heads, 0)[:, :count]
    stats = jnp.sqrt(summed[36, :3] / (summed[36, 3] * D))
    width = late.shape[1] // 3
    return (
        output, input_grad, late[:, :width], late[:, width : 2 * width], late[:, 2 * width :], early[0].T, early[1], early[2].T,
        conv_grad, vectors[0], vectors[1], vectors[2], vectors[3], stats,
    )


def solution(mesh):
    own = mesh.shape["dp"] == 16 and mesh.shape["tensor"] == 2
    rows, both = P(("dp", "tensor"), None), P(("dp", "tensor"))
    split, crossed = P("dp", "tensor"), P("tensor", "dp")
    return jax.shard_map(
        partial(per_device, own),
        mesh=mesh,
        in_specs=(rows, P("dp"), rows, split, split, split, crossed, split, crossed,
                  P("tensor", None), both, both, both, both),
        out_specs=(rows, rows, split, split, split, crossed, split, crossed,
                   P("tensor", None), both, both, both, both, P()),
        check_vma=False,
    )
```

```python
from functools import partial

import jax
import jax.numpy as jnp
from jax import lax
from jax.experimental import pallas as pl
from jax.experimental.pallas import tpu as pltpu
from jax.sharding import PartitionSpec as P

ANY = pl.BlockSpec(memory_space=pl.ANY)
F32, BF = jnp.float32, jnp.bfloat16
NN, NT, TN = ((1,), (0,)), ((1,), (1,)), ((0,), (0,))
MARKS = 64
HEAD = 64
PACK = 4
WIDE = PACK * HEAD
TAPS = 33
EDGE = TAPS // 2
ROWS = 128
TALL = 256
TAPS_AT, FLIP_AT, BLOCK = 8, 16, 24
WINDOW = ROWS + 2 * EDGE
STEPS = 6
KEPT = 4


def mm(a, b, dims=NN):
    return lax.dot_general(a, b, (dims, ((), ())), preferred_element_type=F32)


def halves(a):
    high = a.astype(BF)
    return high, (a - high.astype(F32)).astype(BF)


def mm3(a, b, dims=NN):
    (ah, al), (bh, bl) = a, b
    return mm(ah, bh, dims) + (mm(ah, bl, dims) + mm(al, bh, dims))


def mm3f(a, b, dims=NN):
    return mm3(halves(a), halves(b), dims)


def grid_of(shape):
    return (
        lax.broadcasted_iota(jnp.int32, shape, 0),
        lax.broadcasted_iota(jnp.int32, shape, 1),
    )


def block_mask():
    row, col = grid_of((WIDE, WIDE))
    return row // HEAD == col // HEAD


def eye():
    row, col = grid_of((WIDE, WIDE))
    return (row == col).astype(F32)


def spread(packed, mask):
    full = jnp.concatenate([packed] * PACK, axis=0)
    return jnp.where(mask, full, jnp.zeros_like(full))


def gather_up(full):
    return sum(full[i * MARKS : (i + 1) * MARKS] for i in range(PACK))


def segment_reduce(a, fill, op):
    lane = lax.broadcasted_iota(jnp.int32, (a.shape[0], 128), 1) < HEAD
    parts = []
    for tile in range(a.shape[1] // 128):
        piece = a[:, tile * 128 : (tile + 1) * 128]
        low = op(jnp.where(lane, piece, fill), axis=1, keepdims=True)
        high = op(jnp.where(lane, fill, piece), axis=1, keepdims=True)
        parts.append(jnp.where(lane, low, high))
    return jnp.concatenate(parts, axis=1)


def average_matrix():
    row, col = grid_of((TALL // 16, TALL))
    return jnp.where(row == col // 16, 1.0 / 16, 0.0).astype(BF)


def average_back():
    row, col = grid_of((ROWS, ROWS // 16))
    return jnp.where(row // 16 == col, 1.0 / 16, 0.0).astype(BF)


def lanes_of(group):
    return slice(group * WIDE, (group + 1) * WIDE)


def put(ref, rows, which, wide, parts, start, value):
    share = wide // parts
    for tile in range(0, value.shape[1], 128):
        lane = start + tile
        at = (3 * (lane // share) + which) * share + lane % share
        ref[rows, at : at + 128] = value[:, tile : tile + 128]


def lhs(a):
    return jnp.concatenate(halves(a), axis=1)


def rhs(b):
    high, low = halves(b)
    return jnp.concatenate(
        [
            jnp.concatenate([high, low], axis=1),
            jnp.concatenate([high, jnp.zeros_like(high)], axis=1),
        ],
        axis=0,
    )


def pair_mm(left, right):
    out = mm(left, right)
    return out[:, :128] + out[:, 128:]


def fold(full):
    return full[:MARKS] + full[MARKS:]


def unfold(packed, mask):
    full = jnp.concatenate([packed, packed], axis=0)
    return jnp.where(mask, full, 0.0)


def pair_lanes(pair):
    return slice(pair * 128, (pair + 1) * 128)


def pair_consts():
    row, col = grid_of((128, 128))
    return row // HEAD == col // HEAD, (row == col).astype(F32)


def toeplitz(taps_ref, first, own_heads, group):
    parts = []
    for i in range(PACK):
        half, head = divmod(group * PACK + i, own_heads)
        line = taps_ref[first + head : first + head + 1, half * 128 : (half + 1) * 128]
        line = jnp.concatenate([line, jnp.zeros_like(line)], axis=1)
        line = jnp.broadcast_to(line, (ROWS, 256))
        parts.append(pltpu.roll(line, 0, 1, stride=1, stride_axis=0)[:, :WINDOW])
    return jnp.concatenate(parts, axis=0).astype(BF)


def diagonal_lanes(stacked):
    col = lax.broadcasted_iota(jnp.int32, (ROWS, WIDE), 1) // HEAD
    out = stacked[:ROWS]
    for i in range(1, PACK):
        out = jnp.where(col == i, stacked[i * ROWS : (i + 1) * ROWS], out)
    return out


def attn_fwd_kernel(slot, groups, parts, own, *refs):
    len_ref, x_ref = refs[:2]
    if own:
        shards, outs, refs = refs[2:7], refs[7:12], refs[12:]
        weight, taps_ref = outs[0], outs[1].at[0, 0, 0, 0]
    else:
        weight, taps_ref, refs = refs[2], refs[3], refs[4:]
    ctx_ref, qh_ref, kh_ref, vp_ref, k1_ref, k3_ref, small_ref, chain_ref = refs[:8]
    z_ref, k2_ref, s_ref, top_ref, t_ref = refs[8:13]
    slots = []
    if own:
        place = Place()
        greet(place)
        slots = schedule(gather_parts(place, GATHERS, shards, outs, *refs[13:]), GATHER_LAGS)

    def advance(count=1):
        for _ in range(count):
            if slots:
                for step in slots.pop(0):
                    step()

    advance(6)
    count = slot // ROWS
    scale = HEAD ** -0.25
    length = len_ref[0]
    avg = average_matrix()
    wide = groups * WIDE
    share = wide // parts
    own_heads = share // HEAD
    vp_ref[0:EDGE, :] = jnp.zeros((EDGE, wide), BF)
    vp_ref[slot + EDGE : slot + 2 * EDGE, :] = jnp.zeros((EDGE, wide), BF)

    def columns(start, width):
        if own:
            return weight[:, :, :, :, :, start : start + width].reshape(-1, width)
        return weight[:, start : start + width]

    def valid_of(i, rows):
        row = lax.broadcasted_iota(jnp.int32, (rows, 1), 0) + i * rows
        return (row < length).astype(F32)

    def load(i, carry):
        rows = pl.ds(pl.multiple_of(i * TALL, TALL), TALL)
        few = pl.ds(pl.multiple_of(i * (TALL // 16), TALL // 16), TALL // 16)
        factor = valid_of(i, TALL) * scale
        for p in range(parts):
            both = mm(x_ref[rows, :], columns(3 * p * share, 2 * share)) * factor
            at = slice(p * share, (p + 1) * share)
            high, low = halves(both)
            qh_ref[rows, at] = high[:, :share]
            kh_ref[rows, at] = high[:, share:]
            means = mm(avg, high) + mm(avg, low)
            small_ref[0, few, at] = means[:, :share]
            small_ref[1, few, at] = means[:, share:]
        return carry

    lax.fori_loop(0, slot // TALL, load, 0)
    mask = block_mask()
    pmask, one = pair_consts()
    pairs = 2 * groups

    for j in range(pairs):
        at = pair_lanes(j)
        ql, kl = unfold(small_ref[0, :, at], pmask), unfold(small_ref[1, :, at], pmask)
        a2 = jnp.where(pmask, mm3f(ql, kl, NT), -1e30)
        e2 = jnp.where(pmask, jnp.exp(a2 - jnp.max(a2, axis=1, keepdims=True)), 0.0)
        k2 = e2 / jnp.sum(e2, axis=1, keepdims=True)
        top = segment_reduce(jnp.sum(k2, axis=0, keepdims=True), -1e30, jnp.max)
        k2_ref[j] = lhs(k2)
        small_ref[2, :, at] = fold(k2)
        z_ref[j] = jnp.transpose(k2) / top

    def newton(step, carry):
        every = range(pairs)
        z = [z_ref[j] for j in every]
        p = [pair_mm(k2_ref[j], rhs(z[j])) for j in every]
        left = [lhs(p[j]) for j in every]
        t2 = [15.0 * one - pair_mm(left[j], rhs(7.0 * one - p[j])) for j in every]
        t3 = [13.0 * one - pair_mm(left[j], rhs(t2[j])) for j in every]
        new = [0.25 * pair_mm(lhs(z[j]), rhs(t3[j])) for j in every]
        for j in every:
            for n, value in enumerate((z, p, t2, t3)):
                chain_ref[step, n, :, pair_lanes(j)] = fold(value[j])
            z_ref[j] = new[j]
        return carry

    lax.fori_loop(0, STEPS // 2, newton, 0)
    advance()
    lax.fori_loop(STEPS // 2, STEPS, newton, 0)
    advance()

    def load_values(i, carry):
        rows = pl.ds(pl.multiple_of(i * TALL + EDGE, EDGE), TALL)
        valid = valid_of(i, TALL)
        x = x_ref[pl.ds(pl.multiple_of(i * TALL, TALL), TALL), :]
        for p in range(parts):
            value = mm(x, columns((3 * p + 2) * share, share)) * valid
            vp_ref[rows, p * share : (p + 1) * share] = value.astype(BF)
        return carry

    lax.fori_loop(0, slot // TALL, load_values, 0)

    for g in range(groups):
        at = lanes_of(g)
        ql = spread(small_ref[0, :, at], mask).astype(BF)
        top_ref[...] = jnp.full(top_ref.shape, -jnp.inf, F32)

        def scores(i, carry):
            rows = pl.ds(pl.multiple_of(i * ROWS, ROWS), ROWS)
            row = lax.broadcasted_iota(jnp.int32, (ROWS, 1), 0) + i * ROWS
            a3 = jnp.where(row < length, mm(kh_ref[rows, at], ql, NT), -1e9)
            s_ref[rows, :] = a3
            top_ref[0:1, :] = jnp.maximum(top_ref[0:1, :], jnp.max(a3, axis=0, keepdims=True))
            return carry

        lax.fori_loop(0, count, scores, 0)
        peak = top_ref[0:1, :]
        top_ref[0:1, :] = jnp.zeros((1, WIDE), F32)

        def powers(i, carry):
            rows = pl.ds(pl.multiple_of(i * ROWS, ROWS), ROWS)
            e3 = jnp.exp(s_ref[rows, :] - peak)
            s_ref[rows, :] = e3
            top_ref[0:1, :] += jnp.sum(e3, axis=0, keepdims=True)
            return carry

        lax.fori_loop(0, count, powers, 0)
        inverse = 1.0 / top_ref[0:1, :]

        def weigh(i, carry):
            rows = pl.ds(pl.multiple_of(i * ROWS, ROWS), ROWS)
            k3_ref[rows, at] = (s_ref[rows, :] * inverse).astype(BF)
            return carry

        lax.fori_loop(0, count, weigh, 0)
        b = mm(k3_ref[:, at], vp_ref[EDGE : slot + EDGE, at], TN)
        b = jnp.where(mask, b, 0.0)
        for sub in range(2):
            j, inner = 2 * g + sub, pair_lanes(sub)
            z, piece = z_ref[j], b[inner, inner]
            small_ref[3, :, pair_lanes(j)] = fold(piece)
            small_ref[4, :, pair_lanes(j)] = fold(mm3f(z, piece))
            small_ref[5, :, pair_lanes(j)] = fold(z)
        t_ref[...] = toeplitz(taps_ref, TAPS_AT, own_heads, g)
        cb = spread(small_ref[4, :, at], mask).astype(BF)
        kl = spread(small_ref[1, :, at], mask).astype(BF)
        ones = mask.astype(F32).astype(BF)

        def mix(i, carry):
            rows = pl.ds(pl.multiple_of(i * ROWS, ROWS), ROWS)
            a1 = mm(qh_ref[rows, at], kl, NT)
            e1 = jnp.exp(a1 - segment_reduce(a1, -jnp.inf, jnp.max)).astype(BF)
            k1 = (e1.astype(F32) / mm(e1, ones)).astype(BF)
            k1_ref[rows, at] = k1
            window = vp_ref[pl.ds(pl.multiple_of(i * ROWS, ROWS), WINDOW), at]
            ctx_ref[rows, at] = (
                mm(k1, cb) + diagonal_lanes(mm(t_ref[...], window))
            ).astype(BF)
            return carry

        lax.fori_loop(0, count, mix, 0)
        if g < 2:
            advance()

    while slots:
        advance()


def attn_bwd_kernel(slot, groups, parts, own, *refs):
    (len_ref, g_ref, qh_ref, kh_ref, vp_ref, k1_ref, k3_ref, small_ref, chain_ref, taps_ref,
     xt_ref, w_ref, dres_ref, block_ref) = refs[:14]
    if own:
        fulls, quarter_ref, refs = refs[14:16], refs[16], refs[17:]
        outs, down_out, refs = refs[:3], refs[3], refs[4:]
    else:
        outs, refs = (refs[14],), refs[15:]
    dx_ref, sum_ref = refs[:2]
    (dqkv_ref, gp_ref, da1_ref, da3_ref, dk_ref, dz_ref, k2_ref,
     dql_ref, dkl_ref, t_ref, acc_ref) = refs[2:13]
    todo = {}
    if own:
        grad_ref, totals, landed = refs[13:16]
        place = Place()
        greet(place)
        scatters = scatter_parts(place, SCATTERS, fulls + (grad_ref,), outs, refs[19:])
        base = SUM_COPIES * len(SCATTERS)
        total = Total(place, totals.at[0], sum_ref, totals, landed, refs[-3], refs[-2], base)
        tail = ScatterEnd(place, quarter_ref, down_out, refs[16:19], refs[-3], refs[-2], base + 5)
        todo = SCATTER_AT
    else:
        grad_ref = outs[0]
        totals = sum_ref

    def advance(name):
        for which, stage in todo.get(name, ()):
            if which == "t":
                total.run(stage)
            elif which == "d":
                tail.run(stage)
            else:
                for part, wave in zip(scatters, SCATTER_WAVES):
                    if wave == which:
                        part.run(stage)

    advance("start")
    count = slot // ROWS
    marks = ROWS // 16
    scale = HEAD ** -0.25
    length = len_ref[0]
    wide = groups * WIDE
    share = wide // parts
    own_heads = share // HEAD
    pairs = 2 * groups
    mask = block_mask()
    pmask, one = pair_consts()
    ones = mask.astype(F32).astype(BF)
    gp_ref[0:EDGE, :] = jnp.zeros((EDGE, wide), BF)
    gp_ref[slot + EDGE : slot + 2 * EDGE, :] = jnp.zeros((EDGE, wide), BF)
    gp_ref[EDGE : slot + EDGE, :] = g_ref[...]
    col = lax.broadcasted_iota(jnp.int32, (ROWS, WIDE), 1) // HEAD
    up, across = grid_of((ROWS, ROWS))
    flip = jnp.where(up + across == ROWS - 1, 1.0, 0.0).astype(BF)
    taps_lane = lax.broadcasted_iota(jnp.int32, (1, 128), 1) < TAPS

    def totals_row(row):
        return (0, slice(row, row + 1)) if own else slice(row, row + 1)

    if own:
        totals[0] = block_ref[...]
    else:
        sum_ref[...] = block_ref[...]

    for g in range(groups):
        at = lanes_of(g)
        cb = spread(small_ref[4, :, at], mask).astype(BF)

        def first(i, carry):
            rows = pl.ds(pl.multiple_of(i * ROWS, ROWS), ROWS)
            k1 = k1_ref[rows, at].astype(F32)
            dk1 = mm(g_ref[rows, at], cb, NT)
            high, low = halves(dk1 * k1)
            da1_ref[rows, at] = (k1 * (dk1 - (mm(high, ones) + mm(low, ones)))).astype(BF)
            return carry

        lax.fori_loop(0, count, first, 0)
        advance(f"first{g}")
        dc = jnp.where(mask, mm(k1_ref[:, at], g_ref[:, at], TN), 0.0)
        dkl_ref[:, at] = gather_up(jnp.where(mask, mm(da1_ref[:, at], qh_ref[:, at], TN), 0.0))
        many = jnp.ones((8, 128), BF)
        totals_of = []
        for sub in range(2):
            j, inner = 2 * g + sub, pair_lanes(sub)
            b, z = (unfold(small_ref[n, :, pair_lanes(j)], pmask) for n in (3, 5))
            piece = halves(dc[inner, inner])
            dz_ref[j] = mm3(halves(b), piece, NT)
            db = mm3(halves(z), piece, TN)
            dql_ref[:, pair_lanes(j)] = fold(db)
            high, low = halves(db * b)
            totals_of.append((mm(many, high, NT) + mm(many, low, NT))[0:1, :])
        peak = jnp.concatenate(totals_of, axis=1)
        dbb = spread(dql_ref[:, at], mask).astype(BF)
        t_ref[...] = toeplitz(taps_ref, FLIP_AT, own_heads, g)
        acc_ref[...] = jnp.zeros(acc_ref.shape, F32)

        def second(i, carry):
            rows = pl.ds(pl.multiple_of(i * ROWS, ROWS), ROWS)
            row = lax.broadcasted_iota(jnp.int32, (ROWS, 1), 0) + i * ROWS
            valid = (row < length).astype(F32)
            k3 = k3_ref[rows, at]
            vh = vp_ref[pl.ds(pl.multiple_of(i * ROWS + EDGE, EDGE), ROWS), at]
            dk3 = mm(vh, dbb, NT)
            da3_ref[rows, at] = (k3.astype(F32) * (dk3 - peak)).astype(BF)
            window = pl.ds(pl.multiple_of(i * ROWS, ROWS), WINDOW)
            dv = mm(k3, dbb) + diagonal_lanes(mm(t_ref[...], gp_ref[window, at]))
            put(dqkv_ref, rows, 2, wide, parts, g * WIDE, (dv * valid).astype(BF))
            grad = g_ref[rows, at]
            split = jnp.concatenate(
                [jnp.where(col == h, grad, jnp.zeros_like(grad)) for h in range(PACK)], axis=0
            )
            acc_ref[:, :WINDOW] += mm(split, vp_ref[window, at], NT)
            return carry

        lax.fori_loop(0, count, second, 0)
        for h in range(PACK):
            high, low = halves(acc_ref[h * ROWS : (h + 1) * ROWS, :])
            turned = pltpu.roll(mm(flip, high) + mm(flip, low), 0, 1, stride=1, stride_axis=0)
            line = pltpu.roll(jnp.sum(turned, axis=0, keepdims=True), 129, 1)[:, :128]
            totals[totals_row(24 + g * PACK + h)] = jnp.where(taps_lane, line, 0.0)
        dql_ref[:, at] = gather_up(jnp.where(mask, mm(da3_ref[:, at], kh_ref[:, at], TN), 0.0))
        advance(f"second{g}")

    def weight_grad(start, width):
        for p in range(parts):
            lanes = slice(3 * p * share + start, 3 * p * share + start + width)
            for block in range(4):
                size = xt_ref.shape[0] // 4
                here = mm(xt_ref[block * size : (block + 1) * size, :], dqkv_ref[:, lanes]).astype(BF)
                if own:
                    rows = grad_ref.shape[-2]
                    grad_ref[block // 2, block % 2, :, :, :, lanes] = here.reshape(2, 2, rows, width)
                else:
                    grad_ref[block * size : (block + 1) * size, lanes] = here

    weight_grad(2 * share, share)
    advance("values")
    for j in range(pairs):
        dk_ref[j] = jnp.zeros((128, 128), F32)
        k2_ref[j] = unfold(small_ref[2, :, pair_lanes(j)], pmask)

    def newton(back, carry):
        step = STEPS - 1 - back
        every = range(pairs)
        z, p, t2, t3 = (
            [unfold(chain_ref[step, n, :, pair_lanes(j)], pmask) for j in every] for n in range(KEPT)
        )
        dz = [0.25 * dz_ref[j] for j in every]
        dt3 = [pair_mm(lhs(dz[j]), rhs(z[j])) for j in every]
        dt2 = [-pair_mm(lhs(dt3[j]), rhs(p[j])) for j in every]
        dp = [pair_mm(lhs(dt2[j]), rhs(p[j])) - pair_mm(lhs(t2[j]), rhs(dt3[j])) for j in every]
        dp = [dp[j] - pair_mm(lhs(7.0 * one - p[j]), rhs(dt2[j])) for j in every]
        for j in every:
            dk_ref[j] += pair_mm(lhs(z[j]), rhs(dp[j]))
        new = [pair_mm(lhs(t3[j]), rhs(dz[j])) + pair_mm(lhs(dp[j]), rhs(k2_ref[j])) for j in every]
        for j in every:
            dz_ref[j] = new[j]
        return carry

    for third_of in range(3):
        lax.fori_loop(third_of * STEPS // 3, (third_of + 1) * STEPS // 3, newton, 0)
        advance(f"newton{third_of}")

    for j in range(pairs):
        at = pair_lanes(j)
        k2 = k2_ref[j]
        sums = jnp.sum(k2, axis=0, keepdims=True)
        top = segment_reduce(sums, -1e30, jnp.max)
        hit = (sums == top).astype(F32)
        ties = segment_reduce(hit, 0.0, jnp.sum)
        dz0 = dz_ref[j]
        dtop = -segment_reduce(jnp.sum(dz0 * k2, axis=0, keepdims=True), 0.0, jnp.sum) / (top * top)
        dk2 = jnp.where(pmask, jnp.transpose(dk_ref[j]) + dz0 / top + hit * (dtop / ties), 0.0)
        da2 = halves(k2 * (dk2 - jnp.sum(dk2 * k2, axis=1, keepdims=True)))
        qls, kls = (halves(unfold(small_ref[n, :, at], pmask)) for n in (0, 1))
        dql_ref[:, at] += fold(mm3(da2, kls))
        dkl_ref[:, at] += fold(mm3(da2, qls, TN))
    back = average_back()

    for g in range(groups):
        at = lanes_of(g)
        qlb, klb = (spread(small_ref[n, :, at].astype(BF), mask) for n in (0, 1))

        def third(i, carry):
            rows = pl.ds(pl.multiple_of(i * ROWS, ROWS), ROWS)
            few = pl.ds(pl.multiple_of(i * marks, marks), marks)
            row = lax.broadcasted_iota(jnp.int32, (ROWS, 1), 0) + i * ROWS
            valid = jnp.where(row < length, scale, 0.0)
            dq = mm(da1_ref[rows, at], klb) + mm(back, dql_ref[few, at].astype(BF))
            dk = mm(da3_ref[rows, at], qlb) + mm(back, dkl_ref[few, at].astype(BF))
            put(dqkv_ref, rows, 0, wide, parts, g * WIDE, (dq * valid).astype(BF))
            put(dqkv_ref, rows, 1, wide, parts, g * WIDE, (dk * valid).astype(BF))
            return carry

        lax.fori_loop(0, count, third, 0)
        advance(f"third{g}")

    weight_grad(0, 2 * share)
    advance("keys")
    for i in range(slot // TALL):
        rows = slice(i * TALL, (i + 1) * TALL)
        dx_ref[rows, :] = (dres_ref[rows, :] + mm(dqkv_ref[rows, :], w_ref[...], NT)).astype(BF)
        advance(f"input{i}")
    advance("end")


VM = pl.BlockSpec(memory_space=pltpu.VMEM)
SM = pl.BlockSpec(memory_space=pltpu.SMEM)
LIMIT = 60 * 1024 * 1024


def attn_fwd(length, x, parts, own, weights):
    slot, wide = x.shape
    groups = wide // WIDE
    shape = jax.ShapeDtypeStruct
    talks = dict(collective_id=1, has_side_effects=True) if own else {}
    gathered = gather_shapes(weights) if own else ()
    outs = pl.pallas_call(
        partial(attn_fwd_kernel, slot, groups, parts, own),
        out_shape=gathered
        + (
            shape((slot, wide), BF),
            shape((slot, wide), BF),
            shape((slot, wide), BF),
            shape((slot + 2 * EDGE, wide), BF),
            shape((slot, wide), BF),
            shape((slot, wide), BF),
            shape((6, MARKS, wide), F32),
            shape((STEPS, KEPT, MARKS, wide), F32),
        ),
        in_specs=[SM, VM] + [VM] * len(weights),
        out_specs=([VM, VM, ANY, ANY, ANY] if own else []) + [VM] * 8,
        scratch_shapes=[
            pltpu.VMEM((2 * groups, 128, 128), F32),
            pltpu.VMEM((2 * groups, 128, 256), BF),
            pltpu.VMEM((slot, WIDE), F32),
            pltpu.VMEM((8, WIDE), F32),
            pltpu.VMEM((PACK * ROWS, WINDOW), BF),
        ]
        + (gather_scratch(GATHERS) if own else []),
        compiler_params=pltpu.CompilerParams(vmem_limit_bytes=LIMIT, **talks),
        name="attn_fwd",
    )(length, x, *weights)
    return outs[: len(gathered)], outs[len(gathered) :]


def attn_bwd(length, g, saved, taps, xt, weight, dres, block, parts, own, fulls, quarter=None):
    slot, wide = g.shape
    groups = wide // WIDE
    shape = jax.ShapeDtypeStruct
    talks = dict(collective_id=2, has_side_effects=True) if own else {}
    ends = (shape((slot, wide), BF), shape(block.shape, F32))
    if own:
        rows = fulls[0].shape[0] // 16
        fulls = [f.reshape(2, 2, 2, 2, rows, f.shape[1]) for f in fulls]
        outs = tuple(shape((rows, f.shape[-1] // 2), F32) for f in fulls) + (
            shape((rows, 3 * wide // 2), F32),
            shape((rows, quarter.shape[-1]), F32),
        )
        width = quarter.shape[-1]
        extra = [
            pltpu.VMEM((2, 2, 2, 2, rows, 3 * wide), BF),
            pltpu.VMEM((6,) + block.shape, F32),
            pltpu.VMEM((5,) + block.shape, F32),
            pltpu.VMEM((2, rows, width), BF),
            pltpu.VMEM((2, rows, width), BF),
            pltpu.VMEM((rows, width), BF),
        ] + all_scatter_scratch(SCATTERS, rows, 7)
    else:
        fulls, extra = [], []
        outs = (shape((wide, 3 * wide), BF),)
    return pl.pallas_call(
        partial(attn_bwd_kernel, slot, groups, parts, own),
        out_shape=outs + ends,
        in_specs=[SM] + [VM] * 13 + [ANY] * len(fulls) + ([VM] if own else []),
        out_specs=[VM] * (len(outs) + 2),
        scratch_shapes=[
            pltpu.VMEM((slot, 3 * wide), BF),
            pltpu.VMEM((slot + 2 * EDGE, wide), BF),
            pltpu.VMEM((slot, wide), BF),
            pltpu.VMEM((slot, wide), BF),
            pltpu.VMEM((2 * groups, 128, 128), F32),
            pltpu.VMEM((2 * groups, 128, 128), F32),
            pltpu.VMEM((2 * groups, 128, 128), F32),
            pltpu.VMEM((MARKS, wide), F32),
            pltpu.VMEM((MARKS, wide), F32),
            pltpu.VMEM((PACK * ROWS, WINDOW), BF),
            pltpu.VMEM((PACK * ROWS, 256), F32),
        ]
        + extra,
        compiler_params=pltpu.CompilerParams(vmem_limit_bytes=67043328, **talks),
        name="attn_bwd",
    )(length, g, *saved, taps, xt, weight, dres, block, *fulls, *([quarter] if own else []))
MESH = pl.DeviceIdType.MESH
WAYS = ("zh", "zl", "y", "x", "c")
COPIES = 11
STAGES = 6


class Place:
    def __init__(self):
        dp = lax.axis_index("dp")
        self.x = lax.axis_index("tensor")
        self.zh, self.zl = dp // 8, (dp // 4) % 2
        self.y, self.c = (dp // 2) % 2, dp % 2

    def at(self, way):
        spot = {w: getattr(self, w) for w in WAYS}
        spot[way] = 1 - spot[way]
        return {
            "dp": spot["zh"] * 8 + spot["zl"] * 4 + spot["y"] * 2 + spot["c"],
            "tensor": spot["x"],
        }


def greet(place):
    barrier = pltpu.get_barrier_semaphore()
    for way in WAYS:
        pl.semaphore_signal(barrier, inc=1, device_id=place.at(way), device_id_type=MESH)
    pl.semaphore_wait(barrier, len(WAYS))


class Mover:
    def __init__(self, place, send, recv, base):
        self.place, self.send, self.recv, self.base = place, send, recv, base
        self.started = []

    def copy(self, index, src, dst, way):
        return pltpu.make_async_remote_copy(
            src_ref=src, dst_ref=dst,
            send_sem=self.send.at[self.base + index], recv_sem=self.recv.at[self.base + index],
            device_id=self.place.at(way), device_id_type=MESH,
        )

    def push(self, index, src, dst, way):
        copy = self.copy(index, src, dst, way)
        copy.start()
        self.started.append(copy)

    def arrive(self, index, ref, way):
        self.copy(index, ref, ref, way).wait_recv()

    def drain(self):
        for copy in self.started:
            copy.wait_send()


class Gather(Mover):
    def __init__(self, place, shard, whole, lane, width, order, send, recv, base, local, last=4):
        super().__init__(place, send, recv, base)
        self.last = last
        self.shard, self.whole, self.local = shard.at[:, pl.ds(lane, width)], whole, local
        self.lane, self.width, self.order = lane, width, order

    def view(self, zh, zl, y, c, x):
        half = self.whole.shape[-1] // 2
        lanes = pl.ds(pl.multiple_of(x * half + self.lane, 128), self.width)
        return self.whole.at[zh, zl, y, c, :, lanes]

    def steps(self, c):
        p, every = self.place, slice(None)
        yield "zh", [self.view(p.zh, p.zl, p.y, c, p.x)], [self.view(1 - p.zh, p.zl, p.y, c, p.x)]
        yield "zl", [self.view(every, p.zl, p.y, c, p.x)], [self.view(every, 1 - p.zl, p.y, c, p.x)]
        if self.order == "yx":
            yield "y", [self.view(every, every, p.y, c, p.x)], [self.view(every, every, 1 - p.y, c, p.x)]
            yield "x", [self.view(every, every, every, c, p.x)], [self.view(every, every, every, c, 1 - p.x)]
        else:
            yield "x", [self.view(every, every, p.y, c, p.x)], [self.view(every, every, p.y, c, 1 - p.x)]
            yield (
                "y",
                [self.view(every, every, p.y, c, x) for x in (0, 1)],
                [self.view(every, every, 1 - p.y, c, x) for x in (0, 1)],
            )

    def run(self, stage):
        p = self.place
        here = self.view(p.zh, p.zl, p.y, p.c, p.x)
        if stage == 0:
            self.mine, self.other = list(self.steps(p.c)), list(self.steps(1 - p.c))
            self.push(0, self.shard, here, "zh")
            self.push(5, self.shard, here, "c")
            self.own = pltpu.make_async_copy(self.shard, here, self.local)
            self.own.start()
        elif stage <= self.last:
            way, _, landed = self.mine[stage - 1]
            for i, ref in enumerate(landed):
                self.arrive(stage - 1 + i, ref, way)
            if stage == 1:
                self.own.wait()
            if stage < self.last:
                way, outgoing, _ = self.mine[stage]
                for i, ref in enumerate(outgoing):
                    self.push(stage + i, ref, ref, way)
            for i, ref in enumerate(landed):
                self.push(5 + stage + i, ref, ref, "c")
        elif stage == self.last + 1:
            self.arrive(5, self.view(p.zh, p.zl, p.y, 1 - p.c, p.x), "c")
            for k in range(self.last):
                for i, ref in enumerate(self.other[k][2]):
                    self.arrive(6 + k + i, ref, "c")
            self.drain()


class GatherEnd(Gather):
    def __init__(self, place, early, whole, lane, width, order, send, recv, base, local):
        Mover.__init__(self, place, send, recv, base)
        self.early, self.whole, self.local = early, whole, local
        self.lane, self.width, self.order = lane, width, order

    def halves_of(self, c):
        p, every = self.place, slice(None)
        if self.order == "yx":
            return "x", [(every, every, every, c, p.x)], [(every, every, every, c, 1 - p.x)]
        return (
            "y",
            [(every, every, p.y, c, x) for x in (0, 1)],
            [(every, every, 1 - p.y, c, x) for x in (0, 1)],
        )

    def old(self, spot):
        now, self.whole = self.whole, self.early
        ref = self.view(*spot)
        self.whole = now
        return ref

    def run(self, stage):
        p, every = self.place, slice(None)
        way, sent, landed = self.halves_of(p.c)
        if stage == 0:
            for i, spot in enumerate(sent):
                self.push(i, self.old(spot), self.view(*spot), way)
            self.loads = []
            if self.order == "yx":
                spots = [(every, every, every, every, p.x)]
            else:
                spots = [(every, every, p.y, every, x) for x in (0, 1)]
            for i, spot in enumerate(spots):
                load = pltpu.make_async_copy(self.old(spot), self.view(*spot), self.local.at[i])
                load.start()
                self.loads.append(load)
        elif stage == 1:
            for i, spot in enumerate(landed):
                self.arrive(i, self.view(*spot), way)
                self.push(2 + i, self.view(*spot), self.view(*spot), "c")
        else:
            for i, spot in enumerate(self.halves_of(1 - p.c)[2]):
                self.arrive(2 + i, self.view(*spot), "c")
            for load in self.loads:
                load.wait()
            self.drain()


class Scatter(Mover):
    def __init__(self, place, full, lane, width, order, out, bufs, send, recv, base, local):
        super().__init__(place, send, recv, base)
        self.full, self.lane, self.width, self.order = full, lane, width, order
        self.out, self.local = out, local
        self.sums, self.in_c, self.in_1, self.in_2, self.in_l, self.in_h = bufs

    def lanes(self, x):
        half = self.full.shape[-1] // 2
        return pl.ds(x * half + self.lane, self.width)

    def add(self, target, landed):
        lead = landed.shape[:-2]
        total = 1
        for n in lead:
            total *= n
        flat_dims = lead

        def one(i, carry):
            index = []
            for n in reversed(flat_dims):
                index.append(i % n)
                i = i // n
            index = tuple(reversed(index))
            target[index] = target[index] + landed[index]
            return carry

        if total == 1:
            one(0, 0)
        else:
            lax.fori_loop(0, total, one, 0)

    def run(self, stage):
        p, every = self.place, slice(None)
        if stage == 0:
            self.loads = []
            for x in (0, 1):
                self.push(x, self.full.at[:, :, :, 1 - p.c, :, self.lanes(x)], self.in_c.at[x], "c")
                load = pltpu.make_async_copy(
                    self.full.at[:, :, :, p.c, :, self.lanes(x)], self.sums.at[x], self.local.at[x]
                )
                load.start()
                self.loads.append(load)
            return
        if stage == 1:
            for x in (0, 1):
                self.arrive(x, self.in_c.at[x], "c")
                self.loads[x].wait()
            self.add(self.sums, self.in_c)
            if self.order == "xy":
                self.push(2, self.sums.at[1 - p.x], self.in_1.at[...], "x")
            else:
                for x in (0, 1):
                    self.push(2 + x, self.sums.at[x, :, :, 1 - p.y], self.in_1.at[x], "y")
        elif stage == 2:
            if self.order == "xy":
                self.arrive(2, self.in_1, "x")
                self.add(self.sums.at[p.x], self.in_1)
                self.push(4, self.sums.at[p.x, :, :, 1 - p.y], self.in_2, "y")
            else:
                for x in (0, 1):
                    self.arrive(2 + x, self.in_1.at[x], "y")
                    self.add(self.sums.at[x, :, :, p.y], self.in_1.at[x])
                self.push(4, self.sums.at[1 - p.x, :, :, p.y], self.in_2, "x")
        elif stage == 3:
            self.arrive(4, self.in_2, "y" if self.order == "xy" else "x")
            self.add(self.sums.at[p.x, :, :, p.y], self.in_2)
            self.push(5, self.sums.at[p.x, :, 1 - p.zl, p.y], self.in_l, "zl")
        elif stage == 4:
            self.arrive(5, self.in_l, "zl")
            self.add(self.sums.at[p.x, :, p.zl, p.y], self.in_l)
            self.push(6, self.sums.at[p.x, 1 - p.zh, p.zl, p.y], self.in_h, "zh")
        else:
            self.arrive(6, self.in_h, "zh")
            self.out[:, self.lane : self.lane + self.width] = (
                self.sums[p.x, p.zh, p.zl, p.y].astype(F32) + self.in_h[...].astype(F32)
            )
            self.drain()


class ScatterStart(Scatter):
    def run(self, stage):
        if stage < 3:
            super().run(stage)
            return
        p = self.place
        self.arrive(4, self.in_2, "y" if self.order == "xy" else "x")
        lanes = slice(self.lane, self.lane + self.width)
        for a in (0, 1):
            for b in (0, 1):
                self.out[a, b, :, lanes] = self.sums[p.x, a, b, p.y] + self.in_2[a, b]
        self.drain()


class ScatterEnd(Mover):
    def __init__(self, place, quarter, out, bufs, send, recv, base):
        super().__init__(place, send, recv, base)
        self.quarter, self.out = quarter, out
        self.in_l, self.sums, self.in_h = bufs

    def run(self, stage):
        p = self.place
        if stage == 0:
            self.push(0, self.quarter.at[:, 1 - p.zl], self.in_l, "zl")
        elif stage == 1:
            self.arrive(0, self.in_l, "zl")
            for a in (0, 1):
                self.sums[a] = self.quarter[a, p.zl] + self.in_l[a]
            self.push(1, self.sums.at[1 - p.zh], self.in_h, "zh")
        else:
            self.arrive(1, self.in_h, "zh")
            self.out[...] = self.sums[p.zh].astype(F32) + self.in_h[...].astype(F32)
            self.drain()


def scatter_scratch(rows, width, order):
    first = (2, 2, 2) if order == "xy" else (2, 2, 2)
    return [
        pltpu.VMEM((2, 2, 2, 2, rows, width), BF),
        pltpu.VMEM((2, 2, 2, 2, rows, width), BF),
        pltpu.VMEM(first + (rows, width), BF),
        pltpu.VMEM((2, 2, rows, width), BF),
        pltpu.VMEM((2, rows, width), BF),
        pltpu.VMEM((rows, width), BF),
    ]


class Total(Mover):
    def __init__(self, place, block, out, sums, landed, send, recv, base):
        super().__init__(place, send, recv, base)
        self.block, self.out, self.sums, self.landed = block, out, sums, landed

    def run(self, stage):
        if stage > 0:
            self.arrive(stage - 1, self.landed.at[stage - 1], WAYS[stage - 1])
            self.sums[stage] = self.sums[stage - 1] + self.landed[stage - 1]
        if stage < 5:
            self.push(stage, self.sums.at[stage], self.landed.at[stage], WAYS[stage])
        else:
            self.out[...] = self.sums[5]
            self.drain()


GATHERS = (
    (0, 0, 384, "yx"), (0, 384, 384, "xy"), (1, 0, 128, "yx"),
    (0, 768, 384, "yx"), (2, 0, 384, "xy"), (3, 0, 768, "yx"), (3, 768, 768, "xy"),
    (4, 0, 768, "yx"), (4, 768, 768, "xy"),
)
GATHER_LAGS = (0, 0, 0, 2, 2, 2, 2, 4, 4)
GATHER_LAST = (4, 4, 4, 4, 4, 4, 4, 3, 3)
DOWN_GATHERS = GATHERS[-2:]
DOWN_SCATTERS = ((0, 0, 768, "xy"), (0, 768, 768, "yx"))
SCATTERS = (
    (1, 0, 768, "xy"), (1, 768, 768, "yx"), (0, 0, 384, "yx"),
    (2, 768, 256, "xy"), (2, 1024, 128, "yx"),
    (2, 0, 384, "xy"), (2, 384, 384, "yx"),
)
SCATTER_WAVES = "aaavvkk"
SCATTER_AT = {
    "start": (("a", 0), ("d", 0)),
    "second0": (("a", 1), ("d", 1)),
    "second1": (("d", 2),),
    "first2": (("a", 2),),
    "second2": (("t", 0),),
    "values": (("v", 0), ("t", 1)),
    "newton0": (("a", 3), ("v", 1), ("t", 2)),
    "newton1": (("t", 3),),
    "newton2": (("v", 2), ("t", 4)),
    "third0": (("a", 4),),
    "third1": (("t", 5),),
    "third2": (("v", 3),),
    "keys": (("k", 0), ("a", 5)),
    "input0": (("k", 1), ("v", 4)),
    "input1": (("v", 5),),
    "input2": (("k", 2),),
    "input3": (("k", 3),),
    "end": (("k", 4), ("k", 5)),
}


def schedule(parts, lags):
    slots = [[] for _ in range(STAGES + max(lags))]
    for part, lag in zip(parts, lags):
        for stage in range(STAGES):
            slots[stage + lag].append(partial(part.run, stage))
    return slots


def gather_parts(place, cuts, shards, wholes, send, recv, local):
    return [
        Gather(place, shards[i], wholes[i], lane, width, order, send, recv, COPIES * n, local.at[n],
               GATHER_LAST[n])
        for n, (i, lane, width, order) in enumerate(cuts)
    ]


def gather_scratch(cuts):
    n = len(cuts)
    return [
        pltpu.SemaphoreType.DMA((COPIES * n,)),
        pltpu.SemaphoreType.DMA((COPIES * n,)),
        pltpu.SemaphoreType.DMA((n,)),
    ]


def gather_shapes(shards):
    return tuple(
        jax.ShapeDtypeStruct((2, 2, 2, 2, s.shape[0], 2 * s.shape[1]), s.dtype) for s in shards
    )


SUM_COPIES = 7


def scatter_parts(place, cuts, fulls, outs, refs):
    send, recv, local = refs[-3:]
    return [
        Scatter(place, fulls[i], lane, width, order, outs[i], refs[6 * n : 6 * n + 6],
                send, recv, SUM_COPIES * n, local.at[n])
        for n, (i, lane, width, order) in enumerate(cuts)
    ]


def all_scatter_scratch(cuts, rows, extra=0):
    out = []
    for _, _, width, order in cuts:
        out += scatter_scratch(rows, width, order)
    n = len(cuts)
    return out + [
        pltpu.SemaphoreType.DMA((SUM_COPIES * n + extra,)),
        pltpu.SemaphoreType.DMA((SUM_COPIES * n + extra,)),
        pltpu.SemaphoreType.DMA((n, 2)),
    ]


def norm_parts(values):
    centre = values - jnp.mean(values, axis=-1, keepdims=True)
    spread_of = jnp.mean(centre * centre, axis=-1, keepdims=True)
    inverse = lax.rsqrt(spread_of + 1e-05)
    return centre * inverse, inverse


def norm_grad(grad, gain, normal, inverse):
    scaled = grad * gain
    lean = jnp.mean(scaled, axis=-1, keepdims=True)
    along = jnp.mean(scaled * normal, axis=-1, keepdims=True)
    return inverse * (scaled - lean - normal * along)


TURNS = 12


def mid_kernel(slot, wide, *refs):
    (len_ref, ctx_ref, x_ref, cot_ref, outw_ref, inw_ref, partial_ref, gain_ref,
     dctx_ref, res_ref, out_ref, gin_ref, gout_ref, quarter_ref, ends_ref,
     downw_ref, hid_ref, turn_ref, act_ref, slope_ref, acc_ref, dlow_ref, gdown_ref, sum_ref) = refs[:24]
    place = Place()
    greet(place)
    gsend, grecv, glocal = refs[-3 - 3 : -3]
    late = [
        GatherEnd(place, partial_ref, downw_ref, lane, width, order, gsend, grecv, 4 * n, glocal.at[n])
        for n, (_, lane, width, order) in enumerate(DOWN_GATHERS)
    ]
    down = [
        ScatterStart(place, gdown_ref, lane, width, order, quarter_ref,
                     refs[24 + 6 * n : 30 + 6 * n], refs[-3], refs[-2], SUM_COPIES * n, refs[-1].at[n])
        for n, (_, lane, width, order) in enumerate(DOWN_SCATTERS)
    ]

    def both(parts, stage):
        for part in parts:
            part.run(stage)

    both(late, 0)
    hidden_units = act_ref.shape[1]
    step = hidden_units // TURNS
    length = len_ref[0]
    gain_one, bias_one = gain_ref[0:1, :], gain_ref[1:2, :]
    gain_two, bias_two = gain_ref[2:3, :], gain_ref[3:4, :]
    sum_ref[...] = jnp.zeros(sum_ref.shape, F32)

    def valid_of(i, rows):
        row = lax.broadcasted_iota(jnp.int32, (rows, 1), 0) + i * rows
        return (row < length).astype(F32)

    def span(i, rows):
        return pl.ds(pl.multiple_of(i * rows, rows), rows)

    def count(row, values):
        sum_ref[row : row + 1, :] += jnp.sum(values, axis=0, keepdims=True)

    def unit(i):
        return pl.ds(pl.multiple_of(i * step, 128), step)

    def weight(ref, lanes):
        return ref[:, :, :, :, :, lanes].reshape(wide, -1)

    def project(i, carry):
        rows = span(i, TALL)
        acc_ref[rows, :] = mm(ctx_ref[rows, :], outw_ref[...], NT)
        return carry

    lax.fori_loop(0, slot // TALL, project, 0)

    def norm_one(i, carry):
        rows = span(i, ROWS)
        valid = valid_of(i, ROWS)
        attn, x = acc_ref[rows, :], x_ref[rows, :].astype(F32)
        count(4, valid * x * x)
        count(5, valid * attn * attn)
        total = x + attn
        res_ref[rows, :] = total
        normal, _ = norm_parts(total)
        hid_ref[rows, :] = (normal * gain_one + bias_one).astype(BF)
        return carry

    lax.fori_loop(0, slot // ROWS, norm_one, 0)

    def expand(i, carry):
        lanes = unit(i)
        for block in range(slot // TALL):
            rows = slice(block * TALL, (block + 1) * TALL)
            pre = mm(hid_ref[rows, :], inw_ref[:, lanes])
            below = 0.5 * (1.0 + lax.erf(pre * 0.5**0.5))
            act_ref[rows, lanes] = (pre * below).astype(BF)
            slope = below + pre * jnp.exp(-0.5 * pre * pre) * (2.0 * jnp.pi) ** -0.5
            slope_ref[rows, lanes] = slope.astype(BF)
        return carry

    lax.fori_loop(0, TURNS, expand, 0)
    both(late, 1)
    both(late, 2)

    def contract(i, carry):
        rows = span(i, 512)
        acc_ref[rows, :] = mm(act_ref[rows, :], weight(downw_ref, slice(None)), NT)
        return carry

    lax.fori_loop(0, slot // 512, contract, 0)

    def norm_two(i, carry):
        rows = span(i, ROWS)
        valid = valid_of(i, ROWS)
        ffn = acc_ref[rows, :]
        count(6, valid * ffn * ffn)
        normal, inverse = norm_parts(hid_ref[rows, :].astype(F32) + ffn)
        out_ref[rows, :] = (normal * gain_two + bias_two).astype(BF)
        grad = cot_ref[rows, :].astype(F32) * valid
        count(2, grad * normal)
        count(3, grad)
        back = norm_grad(grad, gain_two, normal, inverse)
        acc_ref[rows, :] = back
        dlow_ref[rows, :] = back.astype(BF)
        return carry

    lax.fori_loop(0, slot // ROWS, norm_two, 0)
    turn_ref[...] = jnp.transpose(dlow_ref[...])

    def down_grad(i, carry):
        lanes = unit(i)
        value = mm(turn_ref[...], act_ref[:, lanes]).astype(BF)
        gdown_ref[:, :, :, :, :, lanes] = value.reshape(gdown_ref.shape[:-1] + (step,))
        return carry

    lax.fori_loop(0, TURNS, down_grad, 0)
    both(down, 0)
    turn_ref[...] = jnp.transpose(hid_ref[...])

    def back_grad(i, carry):
        lanes = unit(i)
        weights = weight(downw_ref, lanes)
        for block in range(slot // TALL):
            rows = slice(block * TALL, (block + 1) * TALL)
            pre = mm(dlow_ref[rows, :], weights) * slope_ref[rows, lanes].astype(F32)
            slope_ref[rows, lanes] = pre.astype(BF)
        gin_ref[:, lanes] = mm(turn_ref[...], slope_ref[:, lanes]).astype(BF)
        return carry

    lax.fori_loop(0, TURNS // 2, back_grad, 0)
    both(down, 1)
    lax.fori_loop(TURNS // 2, TURNS, back_grad, 0)

    def narrow(i, carry):
        rows = span(i, 512)
        acc_ref[rows, :] += mm(slope_ref[rows, :], inw_ref[...], NT)
        return carry

    lax.fori_loop(0, slot // 512, narrow, 0)
    both(down, 2)

    def norm_one_back(i, carry):
        rows = span(i, ROWS)
        grad = acc_ref[rows, :]
        normal, inverse = norm_parts(res_ref[rows, :])
        count(0, grad * normal)
        count(1, grad)
        back = norm_grad(grad, gain_one, normal, inverse)
        res_ref[rows, :] = back
        dlow_ref[rows, :] = back.astype(BF)
        return carry

    lax.fori_loop(0, slot // ROWS, norm_one_back, 0)
    turn_ref[...] = jnp.transpose(dlow_ref[...])
    for block in range(3):
        rows = slice(block * wide // 3, (block + 1) * wide // 3)
        gout_ref[rows, :] = mm(turn_ref[rows, :], ctx_ref[...]).astype(BF)

    def reach(i, carry):
        rows = span(i, TALL)
        dctx_ref[rows, :] = mm(dlow_ref[rows, :], outw_ref[...]).astype(BF)
        return carry

    lax.fori_loop(0, slot // TALL, reach, 0)
    ends_ref[...] = jnp.zeros(ends_ref.shape, F32)
    tiles = wide // 128
    for n in range(4):
        for tile in range(tiles):
            ends_ref[n * tiles + tile : n * tiles + tile + 1, :] = sum_ref[n : n + 1, tile * 128 : (tile + 1) * 128]
    lane = lax.broadcasted_iota(jnp.int32, (1, 128), 1)
    line = jnp.where(lane == 3, jnp.minimum(length, slot).astype(F32), 0.0)
    for n in range(3):
        line = jnp.where(lane == n, jnp.sum(sum_ref[4 + n : 5 + n, :], axis=1, keepdims=True), line)
    ends_ref[36:37, :] = line
    both(down, 3)


def mid_call(length, ctx, x, cot, outw, inw, part, gains):
    slot, wide = x.shape
    units = inw.shape[1]
    rows = part.shape[-2]
    shape = jax.ShapeDtypeStruct
    whole = (2, 2, 2, 2, rows, units)
    n = len(DOWN_GATHERS)
    return pl.pallas_call(
        partial(mid_kernel, slot, wide),
        out_shape=(
            shape((slot, wide), BF),
            shape((slot, wide), F32),
            shape((slot, wide), BF),
            shape((wide, units), BF),
            shape((wide, wide), BF),
            shape((2, 2, rows, units // 2), BF),
            shape((40, 128), F32),
        ),
        in_specs=[SM] + [VM] * 5 + [ANY, VM],
        out_specs=[VM] * 7,
        scratch_shapes=[
            pltpu.VMEM(whole, BF),
            pltpu.VMEM((slot, wide), BF),
            pltpu.VMEM((wide, slot), BF),
            pltpu.VMEM((slot, units), BF),
            pltpu.VMEM((slot, units), BF),
            pltpu.VMEM((slot, wide), F32),
            pltpu.VMEM((slot, wide), BF),
            pltpu.VMEM(whole, BF),
            pltpu.VMEM((8, wide), F32),
        ]
        + all_scatter_scratch(DOWN_SCATTERS, rows)[:-3]
        + [
            pltpu.SemaphoreType.DMA((4 * n,)),
            pltpu.SemaphoreType.DMA((4 * n,)),
            pltpu.SemaphoreType.DMA((n, 2)),
        ]
        + all_scatter_scratch(DOWN_SCATTERS, rows)[-3:],
        compiler_params=pltpu.CompilerParams(
            vmem_limit_bytes=67043328, collective_id=4, has_side_effects=True
        ),
        name="middle",
    )(length, ctx, x, cot, outw, inw, part, gains)


D = 768
BOTH = ("tensor", "dp")


def rows_sum(left_op, right_op):
    return lax.dot_general(left_op, right_op, (TN, ((), ())), preferred_element_type=F32)


def cols_sum(left_op, right_op):
    return lax.dot_general(left_op, right_op, (NT, ((), ())), preferred_element_type=F32)


def dense(left_op, right_op):
    return jnp.dot(left_op, right_op, preferred_element_type=F32)


def norm_back(grad, gain, normal, inverse):
    return (
        norm_grad(grad, gain, normal, inverse),
        jnp.sum(grad * normal, axis=0),
        jnp.sum(grad, axis=0),
    )


def gather_plain(pieces):
    sizes = lax.axis_size("tensor"), lax.axis_size("dp")
    out = []
    for piece in pieces:
        joined = lax.all_gather(piece, BOTH, axis=0, tiled=True)
        joined = joined.reshape(sizes[0], sizes[1] * piece.shape[0], piece.shape[1])
        out.append(joined.transpose(1, 0, 2).reshape(joined.shape[1], -1))
    return out


def scatter_plain(fulls):
    parts = lax.axis_size("tensor")
    out = []
    for full in fulls:
        stacked = full.reshape(full.shape[0], parts, -1).transpose(1, 0, 2).reshape(-1, full.shape[1] // parts)
        out.append(lax.psum_scatter(stacked, BOTH, scatter_dimension=0, tiled=True).astype(F32))
    return out


def per_device(own, x_in, lengths, cotangent, w_query, w_key, w_value, w_out, w_in, w_down,
               conv_weight, ln1_gain, ln1_bias, ln2_gain, ln2_bias):
    tensor_index = lax.axis_index("tensor")
    slot = x_in.shape[0]
    parts = lax.axis_size("tensor")
    length = lax.dynamic_slice_in_dim(lengths, tensor_index, 1)
    valid = (jnp.arange(slot, dtype=jnp.int32) < length[0]).astype(F32)[:, None]

    first = jnp.concatenate([w_query, w_key, w_value], axis=1)
    later = (w_out.T, w_in, w_down.T)
    few, own_heads, count = ln1_gain.shape[0], conv_weight.shape[0], conv_weight.shape[1]

    def rows_of(array, rows):
        return jnp.pad(array, ((0, rows - array.shape[0]), (0, 128 - array.shape[1])))

    vectors = jnp.stack([ln1_gain, ln1_bias, ln2_gain, ln2_bias])
    block = jnp.concatenate(
        [rows_of(vectors, TAPS_AT), rows_of(conv_weight, FLIP_AT - TAPS_AT),
         rows_of(conv_weight[:, ::-1], BLOCK - FLIP_AT)],
        axis=0,
    )
    if own:
        wholes, saved = attn_fwd(length, x_in, parts, own, (first, block) + later)
        qkv_w, blocks, out_w, in_w = (w.reshape(-1, w.shape[-1]) for w in wholes[:4])
        taps = blocks[:BLOCK]
        blocks = blocks.reshape(lax.axis_size("dp"), BLOCK, parts, 128)
    else:
        qkv_w, out_w, in_w, down_w = gather_plain((first,) + later)
        blocks = lax.all_gather(block, ("dp", "tensor"), axis=0)
        blocks = blocks.reshape(-1, parts, BLOCK, 128).transpose(0, 2, 1, 3)
        taps = blocks[0].reshape(BLOCK, parts * 128)
        _, saved = attn_fwd(length, x_in, parts, own, (qkv_w, taps))
    gains = blocks[:, :4, :, :few].transpose(1, 0, 2, 3).reshape(4, D)
    gain_one, bias_one, gain_two, bias_two = gains[0], gains[1], gains[2], gains[3]
    ctx, saved = saved[0], saved[1:]

    if own:
        d_ctx, d_res1, output, grad_in, grad_out, quarter, ends = mid_call(
            length, ctx, x_in, cotangent, out_w, in_w, wholes[4], jnp.pad(gains, ((0, 4), (0, 0)))
        )
        fulls = [grad_out, grad_in]
    else:
        quarter = None
        tokens = x_in.astype(F32)
        attn_branch = cols_sum(ctx, out_w)
        normal_one, inverse_one = norm_parts(tokens + attn_branch)
        hidden = (normal_one * gain_one + bias_one).astype(BF)
        pre = dense(hidden, in_w)
        below = 0.5 * (1.0 + lax.erf(pre * 0.5**0.5))
        act = (pre * below).astype(BF)
        slope = (below + pre * jnp.exp(-0.5 * pre * pre) * (2.0 * jnp.pi) ** -0.5).astype(BF)
        ffn_branch = cols_sum(act, down_w)
        normal_two, inverse_two = norm_parts(hidden.astype(F32) + ffn_branch)
        output = (normal_two * gain_two + bias_two).astype(BF)
        grad_result = cotangent.astype(F32) * valid
        d_res2, grad_gain_two, grad_bias_two = norm_back(grad_result, gain_two, normal_two, inverse_two)
        d_ffn = d_res2.astype(BF)
        grad_down = rows_sum(d_ffn, act)
        d_pre = (dense(d_ffn, down_w) * slope.astype(F32)).astype(BF)
        grad_in = rows_sum(hidden, d_pre)
        d_hidden = cols_sum(d_pre, in_w) + d_res2
        d_res1, grad_gain_one, grad_bias_one = norm_back(d_hidden, gain_one, normal_one, inverse_one)
        d_attn = d_res1.astype(BF)
        grad_out = rows_sum(d_attn, ctx)
        d_ctx = dense(d_attn, out_w).astype(BF)
        fulls = [grad_out.astype(BF), grad_in.astype(BF), grad_down.astype(BF)]

        def total(branch):
            return jnp.sum(valid * branch * branch)

        sums = jnp.stack([total(tokens), total(attn_branch), total(ffn_branch), jnp.sum(valid)])
        ends = jnp.concatenate(
            [
                jnp.stack([grad_gain_one, grad_bias_one, grad_gain_two, grad_bias_two]).reshape(24, 128),
                jnp.zeros((12, 128), F32),
                jnp.pad(sums[None], ((0, 3), (0, 124))),
            ],
            axis=0,
        )
    grads = attn_bwd(length, d_ctx, saved, taps, x_in.T, qkv_w, d_res1, ends, parts, own, fulls, quarter)
    input_grad, summed = grads[-2:]
    if own:
        early, late = (grads[0], grads[1], grads[3]), grads[2]
    else:
        early, (late,) = scatter_plain(fulls), scatter_plain([grads[0]])
        summed = lax.psum(summed, ("dp", "tensor"))
    share = D // lax.axis_size(("dp", "tensor"))
    start_at = lax.axis_index(("dp", "tensor")) * share
    vectors = lax.dynamic_slice_in_dim(summed[:24].reshape(4, D), start_at, share, 1)
    conv_grad = lax.dynamic_slice_in_dim(summed, 24 + tensor_index * own_heads, own_heads, 0)[:, :count]
    stats = jnp.sqrt(summed[36, :3] / (summed[36, 3] * D))
    width = late.shape[1] // 3
    return (
        output, input_grad, late[:, :width], late[:, width : 2 * width], late[:, 2 * width :], early[0].T, early[1], early[2].T,
        conv_grad, vectors[0], vectors[1], vectors[2], vectors[3], stats,
    )


def solution(mesh):
    own = mesh.shape["dp"] == 16 and mesh.shape["tensor"] == 2
    rows, both = P(("dp", "tensor"), None), P(("dp", "tensor"))
    split, crossed = P("dp", "tensor"), P("tensor", "dp")
    return jax.shard_map(
        partial(per_device, own),
        mesh=mesh,
        in_specs=(rows, P("dp"), rows, split, split, split, crossed, split, crossed,
                  P("tensor", None), both, both, both, both),
        out_specs=(rows, rows, split, split, split, crossed, split, crossed,
                   P("tensor", None), both, both, both, both, P()),
        check_vma=False,
    )
```

```python
from functools import partial

import jax
import jax.numpy as jnp
from jax import lax
from jax.experimental import pallas as pl
from jax.experimental.pallas import tpu as pltpu
from jax.sharding import PartitionSpec as P

ANY = pl.BlockSpec(memory_space=pl.ANY)
F32, BF = jnp.float32, jnp.bfloat16
NN, NT, TN = ((1,), (0,)), ((1,), (1,)), ((0,), (0,))
MARKS = 64
HEAD = 64
PACK = 4
WIDE = PACK * HEAD
TAPS = 33
EDGE = TAPS // 2
ROWS = 128
TALL = 256
TAPS_AT, FLIP_AT, BLOCK = 8, 16, 24
STATS = 36
WINDOW = ROWS + 2 * EDGE
STEPS = 6
KEPT = 4


def mm(a, b, dims=NN):
    return lax.dot_general(a, b, (dims, ((), ())), preferred_element_type=F32)


def halves(a):
    high = a.astype(BF)
    return high, (a - high.astype(F32)).astype(BF)


def mm3(a, b, dims=NN):
    (ah, al), (bh, bl) = a, b
    return mm(ah, bh, dims) + (mm(ah, bl, dims) + mm(al, bh, dims))


def mm3f(a, b, dims=NN):
    return mm3(halves(a), halves(b), dims)


def grid_of(shape):
    return (
        lax.broadcasted_iota(jnp.int32, shape, 0),
        lax.broadcasted_iota(jnp.int32, shape, 1),
    )


def block_mask():
    row, col = grid_of((WIDE, WIDE))
    return row // HEAD == col // HEAD


def eye():
    row, col = grid_of((WIDE, WIDE))
    return (row == col).astype(F32)


def spread(packed, mask):
    full = jnp.concatenate([packed] * PACK, axis=0)
    return jnp.where(mask, full, jnp.zeros_like(full))


def gather_up(full):
    return sum(full[i * MARKS : (i + 1) * MARKS] for i in range(PACK))


def segment_reduce(a, fill, op):
    lane = lax.broadcasted_iota(jnp.int32, (a.shape[0], 128), 1) < HEAD
    parts = []
    for tile in range(a.shape[1] // 128):
        piece = a[:, tile * 128 : (tile + 1) * 128]
        low = op(jnp.where(lane, piece, fill), axis=1, keepdims=True)
        high = op(jnp.where(lane, fill, piece), axis=1, keepdims=True)
        parts.append(jnp.where(lane, low, high))
    return jnp.concatenate(parts, axis=1)


def average_matrix():
    row, col = grid_of((TALL // 16, TALL))
    return jnp.where(row == col // 16, 1.0 / 16, 0.0).astype(BF)


def average_back():
    row, col = grid_of((ROWS, ROWS // 16))
    return jnp.where(row // 16 == col, 1.0 / 16, 0.0).astype(BF)


def lanes_of(group):
    return slice(group * WIDE, (group + 1) * WIDE)


def put(ref, rows, which, wide, parts, start, value):
    share = wide // parts
    for tile in range(0, value.shape[1], 128):
        lane = start + tile
        at = (3 * (lane // share) + which) * share + lane % share
        ref[rows, at : at + 128] = value[:, tile : tile + 128]


def lhs(a):
    return jnp.concatenate(halves(a), axis=1)


def rhs(b):
    high, low = halves(b)
    return jnp.concatenate(
        [
            jnp.concatenate([high, low], axis=1),
            jnp.concatenate([high, jnp.zeros_like(high)], axis=1),
        ],
        axis=0,
    )


def pair_mm(left, right):
    out = mm(left, right)
    return out[:, :128] + out[:, 128:]


def fold(full):
    return full[:MARKS] + full[MARKS:]


def unfold(packed, mask):
    full = jnp.concatenate([packed, packed], axis=0)
    return jnp.where(mask, full, 0.0)


def pair_lanes(pair):
    return slice(pair * 128, (pair + 1) * 128)


def pair_consts():
    row, col = grid_of((128, 128))
    return row // HEAD == col // HEAD, (row == col).astype(F32)


def toeplitz(taps_ref, first, own_heads, group):
    parts = []
    for i in range(PACK):
        half, head = divmod(group * PACK + i, own_heads)
        line = taps_ref[first + head : first + head + 1, half * 128 : (half + 1) * 128]
        line = jnp.concatenate([line, jnp.zeros_like(line)], axis=1)
        line = jnp.broadcast_to(line, (ROWS, 256))
        parts.append(pltpu.roll(line, 0, 1, stride=1, stride_axis=0)[:, :WINDOW])
    return jnp.concatenate(parts, axis=0).astype(BF)


def diagonal_lanes(stacked):
    col = lax.broadcasted_iota(jnp.int32, (ROWS, WIDE), 1) // HEAD
    out = stacked[:ROWS]
    for i in range(1, PACK):
        out = jnp.where(col == i, stacked[i * ROWS : (i + 1) * ROWS], out)
    return out


def attn_fwd_kernel(slot, groups, parts, own, *refs):
    len_ref, x_ref = refs[:2]
    if own:
        shards, outs, refs = refs[2:9], refs[9:14], refs[14:]
        weight, taps_ref = outs[0], outs[1].at[0, 0, 0, 0]
    else:
        weight, taps_ref, refs = refs[2], refs[3], refs[4:]
    ctx_ref, qh_ref, kh_ref, vp_ref, k1_ref, k3_ref, small_ref, chain_ref = refs[:8]
    z_ref, k2_ref, s_ref, top_ref, t_ref = refs[8:13]
    moves = []
    if own:
        place = Place()
        greet(place)
        moves = gather_parts(place, GATHERS, shards, outs, *refs[13:])

    def advance(name):
        for which, stage in GATHER_AT.get(name, ()) if own else ():
            for part, wave in zip(moves, GATHER_WAVES):
                if wave == which:
                    part.run(stage)

    advance("start")
    count = slot // ROWS
    scale = HEAD ** -0.25
    length = len_ref[lax.axis_index("tensor")] if len_ref.shape[0] > 1 else len_ref[0]
    avg = average_matrix()
    wide = groups * WIDE
    share = wide // parts
    own_heads = share // HEAD
    vp_ref[0:EDGE, :] = jnp.zeros((EDGE, wide), BF)
    vp_ref[slot + EDGE : slot + 2 * EDGE, :] = jnp.zeros((EDGE, wide), BF)

    def columns(start, width):
        if own:
            return weight[:, :, :, :, :, start : start + width].reshape(-1, width)
        return weight[:, start : start + width]

    def valid_of(i, rows):
        row = lax.broadcasted_iota(jnp.int32, (rows, 1), 0) + i * rows
        return (row < length).astype(F32)

    def load(i, carry):
        rows = pl.ds(pl.multiple_of(i * TALL, TALL), TALL)
        few = pl.ds(pl.multiple_of(i * (TALL // 16), TALL // 16), TALL // 16)
        factor = valid_of(i, TALL) * scale
        for p in range(parts):
            both = mm(x_ref[rows, :], columns(3 * p * share, 2 * share)) * factor
            at = slice(p * share, (p + 1) * share)
            high, low = halves(both)
            qh_ref[rows, at] = high[:, :share]
            kh_ref[rows, at] = high[:, share:]
            means = mm(avg, high) + mm(avg, low)
            small_ref[0, few, at] = means[:, :share]
            small_ref[1, few, at] = means[:, share:]
        return carry

    lax.fori_loop(0, slot // TALL, load, 0)
    advance("load")
    mask = block_mask()
    pmask, one = pair_consts()
    pairs = 2 * groups

    for j in range(pairs):
        at = pair_lanes(j)
        ql, kl = unfold(small_ref[0, :, at], pmask), unfold(small_ref[1, :, at], pmask)
        a2 = jnp.where(pmask, mm3f(ql, kl, NT), -1e30)
        e2 = jnp.where(pmask, jnp.exp(a2 - jnp.max(a2, axis=1, keepdims=True)), 0.0)
        k2 = e2 / jnp.sum(e2, axis=1, keepdims=True)
        top = segment_reduce(jnp.sum(k2, axis=0, keepdims=True), -1e30, jnp.max)
        k2_ref[j] = lhs(k2)
        small_ref[2, :, at] = fold(k2)
        z_ref[j] = jnp.transpose(k2) / top

    def newton(step, carry):
        every = range(pairs)
        z = [z_ref[j] for j in every]
        p = [pair_mm(k2_ref[j], rhs(z[j])) for j in every]
        left = [lhs(p[j]) for j in every]
        t2 = [15.0 * one - pair_mm(left[j], rhs(7.0 * one - p[j])) for j in every]
        t3 = [13.0 * one - pair_mm(left[j], rhs(t2[j])) for j in every]
        new = [0.25 * pair_mm(lhs(z[j]), rhs(t3[j])) for j in every]
        for j in every:
            for n, value in enumerate((z, p, t2, t3)):
                chain_ref[step, n, :, pair_lanes(j)] = fold(value[j])
            z_ref[j] = new[j]
        return carry

    lax.fori_loop(0, STEPS // 2, newton, 0)
    advance("newton0")
    lax.fori_loop(STEPS // 2, STEPS, newton, 0)
    advance("newton1")

    for g in range(groups):
        at = lanes_of(g)
        ql = spread(small_ref[0, :, at], mask).astype(BF)
        top_ref[...] = jnp.full(top_ref.shape, -jnp.inf, F32)

        def scores(i, carry):
            rows = pl.ds(pl.multiple_of(i * ROWS, ROWS), ROWS)
            row = lax.broadcasted_iota(jnp.int32, (ROWS, 1), 0) + i * ROWS
            a3 = jnp.where(row < length, mm(kh_ref[rows, at], ql, NT), -1e9)
            s_ref[rows, :] = a3
            top_ref[0:1, :] = jnp.maximum(top_ref[0:1, :], jnp.max(a3, axis=0, keepdims=True))
            return carry

        lax.fori_loop(0, count, scores, 0)
        peak = top_ref[0:1, :]
        top_ref[0:1, :] = jnp.zeros((1, WIDE), F32)

        def powers(i, carry):
            rows = pl.ds(pl.multiple_of(i * ROWS, ROWS), ROWS)
            e3 = jnp.exp(s_ref[rows, :] - peak)
            s_ref[rows, :] = e3
            top_ref[0:1, :] += jnp.sum(e3, axis=0, keepdims=True)
            return carry

        lax.fori_loop(0, count, powers, 0)
        inverse = 1.0 / top_ref[0:1, :]

        def weigh(i, carry):
            rows = pl.ds(pl.multiple_of(i * ROWS, ROWS), ROWS)
            k3_ref[rows, at] = (s_ref[rows, :] * inverse).astype(BF)
            return carry

        lax.fori_loop(0, count, weigh, 0)
        advance(f"third{g}")

    ones = mask.astype(F32).astype(BF)
    for g in range(groups):
        at = lanes_of(g)
        kl = spread(small_ref[1, :, at], mask).astype(BF)

        def first(i, carry):
            rows = pl.ds(pl.multiple_of(i * ROWS, ROWS), ROWS)
            a1 = mm(qh_ref[rows, at], kl, NT)
            e1 = jnp.exp(a1 - segment_reduce(a1, -jnp.inf, jnp.max)).astype(BF)
            k1_ref[rows, at] = (e1.astype(F32) / mm(e1, ones)).astype(BF)
            return carry

        lax.fori_loop(0, count, first, 0)
        advance(f"first{g}")

    def load_values(i, carry):
        rows = pl.ds(pl.multiple_of(i * TALL + EDGE, EDGE), TALL)
        valid = valid_of(i, TALL)
        x = x_ref[pl.ds(pl.multiple_of(i * TALL, TALL), TALL), :]
        for p in range(parts):
            value = mm(x, columns((3 * p + 2) * share, share)) * valid
            vp_ref[rows, p * share : (p + 1) * share] = value.astype(BF)
        return carry

    lax.fori_loop(0, slot // TALL, load_values, 0)

    for g in range(groups):
        at = lanes_of(g)
        b = mm(k3_ref[:, at], vp_ref[EDGE : slot + EDGE, at], TN)
        b = jnp.where(mask, b, 0.0)
        for sub in range(2):
            j, inner = 2 * g + sub, pair_lanes(sub)
            z, piece = z_ref[j], b[inner, inner]
            small_ref[3, :, pair_lanes(j)] = fold(piece)
            small_ref[4, :, pair_lanes(j)] = fold(mm3f(z, piece))
            small_ref[5, :, pair_lanes(j)] = fold(z)
        t_ref[...] = toeplitz(taps_ref, TAPS_AT, own_heads, g)
        cb = spread(small_ref[4, :, at], mask).astype(BF)

        def mix(i, carry):
            rows = pl.ds(pl.multiple_of(i * ROWS, ROWS), ROWS)
            window = vp_ref[pl.ds(pl.multiple_of(i * ROWS, ROWS), WINDOW), at]
            ctx_ref[rows, at] = (
                mm(k1_ref[rows, at], cb) + diagonal_lanes(mm(t_ref[...], window))
            ).astype(BF)
            return carry

        lax.fori_loop(0, count, mix, 0)
        advance(f"mix{g}")
    advance("end")


def attn_bwd_kernel(slot, groups, parts, own, *refs):
    (len_ref, g_ref, qh_ref, kh_ref, vp_ref, k1_ref, k3_ref, small_ref, chain_ref, taps_ref,
     xt_ref, w_ref, dres_ref, block_ref) = refs[:14]
    if own:
        fulls, quarter_ref, refs = refs[14:16], refs[16], refs[17:]
        outs, down_out, refs = refs[:5], refs[5], refs[6:]
    else:
        outs, refs = (refs[14],), refs[15:]
    late_ref = {}
    for n, (name, ref) in enumerate(
        (("chain", chain_ref), ("xt", xt_ref), ("w", w_ref), ("dres", dres_ref))
    ):
        late_ref[name] = pltpu.make_async_copy(ref, refs[2 + n], refs[6].at[n])
    chain_ref, xt_ref, w_ref, dres_ref = refs[2:6]
    dx_ref, sum_ref = refs[:2]
    refs = refs[:2] + refs[7:]
    (dqkv_ref, gp_ref, da1_ref, da3_ref, dk_ref, dz_ref, k2_ref,
     dql_ref, dkl_ref, t_ref, acc_ref) = refs[2:13]
    todo = {}
    wide_of = groups * WIDE
    if own:
        grad_ref, totals, landed = refs[13:16]
        place = Place()
        greet(place)
        scatters = scatter_parts(place, SCATTERS, fulls + (grad_ref,), outs, refs[19:])
        base = SUM_COPIES * len(SCATTERS)
        total = Total(place, totals.at[0], sum_ref, totals, landed, refs[-3], refs[-2], base, wide_of)
        tail = ScatterEnd(place, quarter_ref, down_out, refs[16:19], refs[-3], refs[-2], base + 5)
        todo = SCATTER_AT
    else:
        grad_ref = outs[0]
        totals = sum_ref

    def advance(name):
        for which, stage in todo.get(name, ()):
            if which == "t":
                total.run(stage)
            elif which == "d":
                tail.run(stage)
            else:
                for part, wave in zip(scatters, SCATTER_WAVES):
                    if wave == which:
                        part.run(stage)

    advance("start")
    for copy in late_ref.values():
        copy.start()
    count = slot // ROWS
    marks = ROWS // 16
    scale = HEAD ** -0.25
    length = len_ref[lax.axis_index("tensor")] if len_ref.shape[0] > 1 else len_ref[0]
    wide = groups * WIDE
    share = wide // parts
    own_heads = share // HEAD
    pairs = 2 * groups
    mask = block_mask()
    pmask, one = pair_consts()
    ones = mask.astype(F32).astype(BF)
    gp_ref[0:EDGE, :] = jnp.zeros((EDGE, wide), BF)
    gp_ref[slot + EDGE : slot + 2 * EDGE, :] = jnp.zeros((EDGE, wide), BF)
    gp_ref[EDGE : slot + EDGE, :] = g_ref[...]
    col = lax.broadcasted_iota(jnp.int32, (ROWS, WIDE), 1) // HEAD
    up, across = grid_of((ROWS, ROWS))
    flip = jnp.where(up + across == ROWS - 1, 1.0, 0.0).astype(BF)
    taps_lane = lax.broadcasted_iota(jnp.int32, (1, 128), 1) < TAPS

    def totals_row(row):
        return (0, slice(row, row + 1)) if own else slice(row, row + 1)

    if own:
        totals[0] = block_ref[...]
    else:
        sum_ref[...] = block_ref[...]

    for g in range(groups):
        at = lanes_of(g)
        cb = spread(small_ref[4, :, at], mask).astype(BF)

        def first(i, carry):
            rows = pl.ds(pl.multiple_of(i * ROWS, ROWS), ROWS)
            k1 = k1_ref[rows, at].astype(F32)
            dk1 = mm(g_ref[rows, at], cb, NT)
            high, low = halves(dk1 * k1)
            da1_ref[rows, at] = (k1 * (dk1 - (mm(high, ones) + mm(low, ones)))).astype(BF)
            return carry

        lax.fori_loop(0, count, first, 0)
        advance(f"first{g}")
        dc = jnp.where(mask, mm(k1_ref[:, at], g_ref[:, at], TN), 0.0)
        dkl_ref[:, at] = gather_up(jnp.where(mask, mm(da1_ref[:, at], qh_ref[:, at], TN), 0.0))
        many = jnp.ones((8, 128), BF)
        totals_of = []
        for sub in range(2):
            j, inner = 2 * g + sub, pair_lanes(sub)
            b, z = (unfold(small_ref[n, :, pair_lanes(j)], pmask) for n in (3, 5))
            piece = halves(dc[inner, inner])
            dz_ref[j] = mm3(halves(b), piece, NT)
            db = mm3(halves(z), piece, TN)
            dql_ref[:, pair_lanes(j)] = fold(db)
            high, low = halves(db * b)
            totals_of.append((mm(many, high, NT) + mm(many, low, NT))[0:1, :])
        peak = jnp.concatenate(totals_of, axis=1)
        dbb = spread(dql_ref[:, at], mask).astype(BF)
        t_ref[...] = toeplitz(taps_ref, FLIP_AT, own_heads, g)
        acc_ref[...] = jnp.zeros(acc_ref.shape, F32)

        def second(i, carry):
            rows = pl.ds(pl.multiple_of(i * ROWS, ROWS), ROWS)
            row = lax.broadcasted_iota(jnp.int32, (ROWS, 1), 0) + i * ROWS
            valid = (row < length).astype(F32)
            k3 = k3_ref[rows, at]
            vh = vp_ref[pl.ds(pl.multiple_of(i * ROWS + EDGE, EDGE), ROWS), at]
            dk3 = mm(vh, dbb, NT)
            da3_ref[rows, at] = (k3.astype(F32) * (dk3 - peak)).astype(BF)
            window = pl.ds(pl.multiple_of(i * ROWS, ROWS), WINDOW)
            dv = mm(k3, dbb) + diagonal_lanes(mm(t_ref[...], gp_ref[window, at]))
            put(dqkv_ref, rows, 2, wide, parts, g * WIDE, (dv * valid).astype(BF))
            grad = g_ref[rows, at]
            split = jnp.concatenate(
                [jnp.where(col == h, grad, jnp.zeros_like(grad)) for h in range(PACK)], axis=0
            )
            acc_ref[:, :WINDOW] += mm(split, vp_ref[window, at], NT)
            return carry

        lax.fori_loop(0, count, second, 0)
        for h in range(PACK):
            high, low = halves(acc_ref[h * ROWS : (h + 1) * ROWS, :])
            turned = pltpu.roll(mm(flip, high) + mm(flip, low), 0, 1, stride=1, stride_axis=0)
            line = pltpu.roll(jnp.sum(turned, axis=0, keepdims=True), 129, 1)[:, :128]
            totals[totals_row(24 + g * PACK + h)] = jnp.where(taps_lane, line, 0.0)
        dql_ref[:, at] = gather_up(jnp.where(mask, mm(da3_ref[:, at], kh_ref[:, at], TN), 0.0))
        advance(f"second{g}")

    def weight_grad(start, width):
        size = xt_ref.shape[0] // 4

        def block_grad(block, carry):
            rows = pl.ds(pl.multiple_of(block * size, 64), size)
            for p in range(parts):
                lanes = slice(3 * p * share + start, 3 * p * share + start + width)
                here = mm(xt_ref[rows, :], dqkv_ref[:, lanes]).astype(BF)
                if own:
                    four = here.reshape(2, 2, grad_ref.shape[-2], width)
                    grad_ref[block // 2, block % 2, :, :, :, lanes] = four
                else:
                    grad_ref[rows, lanes] = here
            return carry

        lax.fori_loop(0, 4, block_grad, 0)

    late_ref["xt"].wait()
    weight_grad(2 * share, share)
    advance("values")
    late_ref["chain"].wait()
    for j in range(pairs):
        dk_ref[j] = jnp.zeros((128, 128), F32)
        k2_ref[j] = unfold(small_ref[2, :, pair_lanes(j)], pmask)

    def newton(back, carry):
        step = STEPS - 1 - back
        every = range(pairs)
        z, p, t2, t3 = (
            [unfold(chain_ref[step, n, :, pair_lanes(j)], pmask) for j in every] for n in range(KEPT)
        )
        dz = [0.25 * dz_ref[j] for j in every]
        dt3 = [pair_mm(lhs(dz[j]), rhs(z[j])) for j in every]
        dt2 = [-pair_mm(lhs(dt3[j]), rhs(p[j])) for j in every]
        dp = [pair_mm(lhs(dt2[j]), rhs(p[j])) - pair_mm(lhs(t2[j]), rhs(dt3[j])) for j in every]
        dp = [dp[j] - pair_mm(lhs(7.0 * one - p[j]), rhs(dt2[j])) for j in every]
        for j in every:
            dk_ref[j] += pair_mm(lhs(z[j]), rhs(dp[j]))
        new = [pair_mm(lhs(t3[j]), rhs(dz[j])) + pair_mm(lhs(dp[j]), rhs(k2_ref[j])) for j in every]
        for j in every:
            dz_ref[j] = new[j]
        return carry

    for third_of in range(3):
        lax.fori_loop(third_of * STEPS // 3, (third_of + 1) * STEPS // 3, newton, 0)
        advance(f"newton{third_of}")

    for j in range(pairs):
        at = pair_lanes(j)
        k2 = k2_ref[j]
        sums = jnp.sum(k2, axis=0, keepdims=True)
        top = segment_reduce(sums, -1e30, jnp.max)
        hit = (sums == top).astype(F32)
        ties = segment_reduce(hit, 0.0, jnp.sum)
        dz0 = dz_ref[j]
        dtop = -segment_reduce(jnp.sum(dz0 * k2, axis=0, keepdims=True), 0.0, jnp.sum) / (top * top)
        dk2 = jnp.where(pmask, jnp.transpose(dk_ref[j]) + dz0 / top + hit * (dtop / ties), 0.0)
        da2 = halves(k2 * (dk2 - jnp.sum(dk2 * k2, axis=1, keepdims=True)))
        qls, kls = (halves(unfold(small_ref[n, :, at], pmask)) for n in (0, 1))
        dql_ref[:, at] += fold(mm3(da2, kls))
        dkl_ref[:, at] += fold(mm3(da2, qls, TN))
    back = average_back()

    for g in range(groups):
        at = lanes_of(g)
        qlb, klb = (spread(small_ref[n, :, at].astype(BF), mask) for n in (0, 1))

        def third(i, carry):
            rows = pl.ds(pl.multiple_of(i * ROWS, ROWS), ROWS)
            few = pl.ds(pl.multiple_of(i * marks, marks), marks)
            row = lax.broadcasted_iota(jnp.int32, (ROWS, 1), 0) + i * ROWS
            valid = jnp.where(row < length, scale, 0.0)
            dq = mm(da1_ref[rows, at], klb) + mm(back, dql_ref[few, at].astype(BF))
            dk = mm(da3_ref[rows, at], qlb) + mm(back, dkl_ref[few, at].astype(BF))
            put(dqkv_ref, rows, 0, wide, parts, g * WIDE, (dq * valid).astype(BF))
            put(dqkv_ref, rows, 1, wide, parts, g * WIDE, (dk * valid).astype(BF))
            return carry

        lax.fori_loop(0, count, third, 0)
        advance(f"third{g}")

    weight_grad(0, share)
    advance("queries")
    weight_grad(share, share)
    advance("keys")
    late_ref["w"].wait()
    late_ref["dres"].wait()

    def input_rows(i, carry):
        rows = pl.ds(pl.multiple_of(i * TALL, TALL), TALL)
        dx_ref[rows, :] = (dres_ref[rows, :] + mm(dqkv_ref[rows, :], w_ref[...], NT)).astype(BF)
        return carry

    for half in range(2):
        turns = slot // TALL // 2
        lax.fori_loop(half * turns, (half + 1) * turns, input_rows, 0)
        advance(f"input{half}")
    advance("end")


VM = pl.BlockSpec(memory_space=pltpu.VMEM)
SM = pl.BlockSpec(memory_space=pltpu.SMEM)
LIMIT = 60 * 1024 * 1024


def attn_fwd(length, x, parts, own, weights):
    slot, wide = x.shape
    groups = wide // WIDE
    shape = jax.ShapeDtypeStruct
    talks = dict(collective_id=1, has_side_effects=True) if own else {}
    gathered = gather_shapes(weights[0].shape[0], wide, 2 * weights[-1].shape[1]) if own else ()
    outs = pl.pallas_call(
        partial(attn_fwd_kernel, slot, groups, parts, own),
        out_shape=gathered
        + (
            shape((slot, wide), BF),
            shape((slot, wide), BF),
            shape((slot, wide), BF),
            shape((slot + 2 * EDGE, wide), BF),
            shape((slot, wide), BF),
            shape((slot, wide), BF),
            shape((6, MARKS, wide), F32),
            shape((STEPS, KEPT, MARKS, wide), F32),
        ),
        in_specs=[SM, VM] + [VM] * len(weights),
        out_specs=([VM, VM, ANY, ANY, ANY] if own else []) + [VM] * 8,
        scratch_shapes=[
            pltpu.VMEM((2 * groups, 128, 128), F32),
            pltpu.VMEM((2 * groups, 128, 256), BF),
            pltpu.VMEM((slot, WIDE), F32),
            pltpu.VMEM((8, WIDE), F32),
            pltpu.VMEM((PACK * ROWS, WINDOW), BF),
        ]
        + (gather_scratch(GATHERS) if own else []),
        compiler_params=pltpu.CompilerParams(vmem_limit_bytes=LIMIT, **talks),
        name="attn_fwd",
    )(length, x, *weights)
    return outs[: len(gathered)], outs[len(gathered) :]


def attn_bwd(length, g, saved, taps, xt, weight, dres, block, parts, own, fulls, quarter=None):
    slot, wide = g.shape
    groups = wide // WIDE
    shape = jax.ShapeDtypeStruct
    talks = dict(collective_id=2, has_side_effects=True) if own else {}
    ends = (shape((slot, wide), BF), shape(block.shape, F32))
    if own:
        rows = fulls[0].shape[0] // 16
        fulls = [f.reshape(2, 2, 2, 2, rows, f.shape[1]) for f in fulls]
        width = quarter.shape[-1]
        outs = (shape((rows, wide // 2), F32), shape((rows, width), F32))
        outs += (shape((rows, wide // 2), F32),) * 3 + (shape((rows, width), F32),)
        extra = [
            pltpu.VMEM((2, 2, 2, 2, rows, 3 * wide), BF),
            pltpu.VMEM((6,) + block.shape, F32),
            pltpu.VMEM((5,) + block.shape, F32),
            pltpu.VMEM((2, rows, width), BF),
            pltpu.VMEM((2, rows, width), BF),
            pltpu.VMEM((rows, width), BF),
        ] + all_scatter_scratch(SCATTERS, rows, 7)
    else:
        fulls, extra = [], []
        outs = (shape((wide, 3 * wide), BF),)
    return pl.pallas_call(
        partial(attn_bwd_kernel, slot, groups, parts, own),
        out_shape=outs + ends,
        in_specs=[SM] + [VM] * 7 + [ANY, VM, ANY, ANY, ANY, VM] + [ANY] * len(fulls) + ([VM] if own else []),
        out_specs=[VM] * (len(outs) + 2),
        scratch_shapes=[
            pltpu.VMEM(saved[-1].shape, F32),
            pltpu.VMEM(xt.shape, BF),
            pltpu.VMEM(weight.shape, BF),
            pltpu.VMEM(dres.shape, F32),
            pltpu.SemaphoreType.DMA((4,)),
            pltpu.VMEM((slot, 3 * wide), BF),
            pltpu.VMEM((slot + 2 * EDGE, wide), BF),
            pltpu.VMEM((slot, wide), BF),
            pltpu.VMEM((slot, wide), BF),
            pltpu.VMEM((2 * groups, 128, 128), F32),
            pltpu.VMEM((2 * groups, 128, 128), F32),
            pltpu.VMEM((2 * groups, 128, 128), F32),
            pltpu.VMEM((MARKS, wide), F32),
            pltpu.VMEM((MARKS, wide), F32),
            pltpu.VMEM((PACK * ROWS, WINDOW), BF),
            pltpu.VMEM((PACK * ROWS, 256), F32),
        ]
        + extra,
        compiler_params=pltpu.CompilerParams(vmem_limit_bytes=67043328, **talks),
        name="attn_bwd",
    )(length, g, *saved, taps, xt, weight, dres, block, *fulls, *([quarter] if own else []))
MESH = pl.DeviceIdType.MESH
WAYS = ("zh", "zl", "y", "x", "c")
COPIES = 11
STAGES = 6


class Place:
    def __init__(self):
        dp = lax.axis_index("dp")
        self.x = lax.axis_index("tensor")
        self.zh, self.zl = dp // 8, (dp // 4) % 2
        self.y, self.c = (dp // 2) % 2, dp % 2

    def at(self, way):
        spot = {w: getattr(self, w) for w in WAYS}
        spot[way] = 1 - spot[way]
        return {
            "dp": spot["zh"] * 8 + spot["zl"] * 4 + spot["y"] * 2 + spot["c"],
            "tensor": spot["x"],
        }


def greet(place):
    barrier = pltpu.get_barrier_semaphore()
    for way in WAYS:
        pl.semaphore_signal(barrier, inc=1, device_id=place.at(way), device_id_type=MESH)
    pl.semaphore_wait(barrier, len(WAYS))


class Mover:
    def __init__(self, place, send, recv, base):
        self.place, self.send, self.recv, self.base = place, send, recv, base
        self.started = []

    def copy(self, index, src, dst, way):
        return pltpu.make_async_remote_copy(
            src_ref=src, dst_ref=dst,
            send_sem=self.send.at[self.base + index], recv_sem=self.recv.at[self.base + index],
            device_id=self.place.at(way), device_id_type=MESH,
        )

    def push(self, index, src, dst, way):
        copy = self.copy(index, src, dst, way)
        copy.start()
        self.started.append(copy)

    def arrive(self, index, ref, way):
        self.copy(index, ref, ref, way).wait_recv()

    def drain(self):
        for copy in self.started:
            copy.wait_send()


class Gather(Mover):
    def __init__(self, place, shard, whole, lane, width, order, send, recv, base, local, last=4):
        super().__init__(place, send, recv, base)
        self.last = last
        self.shard, self.whole, self.local = shard, whole, local
        self.lane, self.width, self.order = lane, width, order

    def view(self, zh, zl, y, c, x):
        half = self.whole.shape[-1] // 2
        lanes = pl.ds(pl.multiple_of(x * half + self.lane, 128), self.width)
        return self.whole.at[zh, zl, y, c, :, lanes]

    def steps(self, c):
        p, every = self.place, slice(None)
        yield "zh", [self.view(p.zh, p.zl, p.y, c, p.x)], [self.view(1 - p.zh, p.zl, p.y, c, p.x)]
        yield "zl", [self.view(every, p.zl, p.y, c, p.x)], [self.view(every, 1 - p.zl, p.y, c, p.x)]
        if self.order == "yx":
            yield "y", [self.view(every, every, p.y, c, p.x)], [self.view(every, every, 1 - p.y, c, p.x)]
            yield "x", [self.view(every, every, every, c, p.x)], [self.view(every, every, every, c, 1 - p.x)]
        else:
            yield "x", [self.view(every, every, p.y, c, p.x)], [self.view(every, every, p.y, c, 1 - p.x)]
            yield (
                "y",
                [self.view(every, every, p.y, c, x) for x in (0, 1)],
                [self.view(every, every, 1 - p.y, c, x) for x in (0, 1)],
            )

    def run(self, stage):
        p = self.place
        here = self.view(p.zh, p.zl, p.y, p.c, p.x)
        if stage == 0:
            self.mine, self.other = list(self.steps(p.c)), list(self.steps(1 - p.c))
            self.push(0, self.shard, here, "zh")
            self.push(5, self.shard, here, "c")
            self.own = pltpu.make_async_copy(self.shard, here, self.local)
            self.own.start()
        elif stage <= self.last:
            way, _, landed = self.mine[stage - 1]
            for i, ref in enumerate(landed):
                self.arrive(stage - 1 + i, ref, way)
            if stage == 1:
                self.own.wait()
            if stage < self.last:
                way, outgoing, _ = self.mine[stage]
                for i, ref in enumerate(outgoing):
                    self.push(stage + i, ref, ref, way)
            for i, ref in enumerate(landed):
                self.push(5 + stage + i, ref, ref, "c")
        elif stage == self.last + 1:
            self.arrive(5, self.view(p.zh, p.zl, p.y, 1 - p.c, p.x), "c")
            for k in range(self.last):
                for i, ref in enumerate(self.other[k][2]):
                    self.arrive(6 + k + i, ref, "c")
            self.drain()


class GatherEnd(Gather):
    def __init__(self, place, early, whole, lane, width, order, send, recv, base, local):
        Mover.__init__(self, place, send, recv, base)
        self.early, self.whole, self.local = early, whole, local
        self.lane, self.width, self.order = lane, width, order

    def halves_of(self, c):
        p, every = self.place, slice(None)
        if self.order == "yx":
            return "x", [(every, every, every, c, p.x)], [(every, every, every, c, 1 - p.x)]
        return (
            "y",
            [(every, every, p.y, c, x) for x in (0, 1)],
            [(every, every, 1 - p.y, c, x) for x in (0, 1)],
        )

    def old(self, spot):
        now, self.whole = self.whole, self.early
        ref = self.view(*spot)
        self.whole = now
        return ref

    def run(self, stage):
        p, every = self.place, slice(None)
        way, sent, landed = self.halves_of(p.c)
        if stage == 0:
            for i, spot in enumerate(sent):
                self.push(i, self.old(spot), self.view(*spot), way)
            self.loads = []
            if self.order == "yx":
                spots = [(every, every, every, every, p.x)]
            else:
                spots = [(every, every, p.y, every, x) for x in (0, 1)]
            for i, spot in enumerate(spots):
                load = pltpu.make_async_copy(self.old(spot), self.view(*spot), self.local.at[i])
                load.start()
                self.loads.append(load)
        elif stage == 1:
            for i, spot in enumerate(landed):
                self.arrive(i, self.view(*spot), way)
                self.push(2 + i, self.view(*spot), self.view(*spot), "c")
        else:
            for i, spot in enumerate(self.halves_of(1 - p.c)[2]):
                self.arrive(2 + i, self.view(*spot), "c")
            for load in self.loads:
                load.wait()
            self.drain()


class Scatter(Mover):
    def __init__(self, place, full, lane, width, order, out, bufs, send, recv, base, local):
        super().__init__(place, send, recv, base)
        self.full, self.lane, self.width, self.order = full, lane, width, order
        self.out, self.local = out, local
        self.sums, self.in_c, self.in_1, self.in_2, self.in_l, self.in_h = bufs

    def lanes(self, x):
        half = self.full.shape[-1] // 2
        return pl.ds(x * half + self.lane, self.width)

    def add(self, target, landed):
        lead = landed.shape[:-2]
        total = 1
        for n in lead:
            total *= n
        flat_dims = lead

        def one(i, carry):
            index = []
            for n in reversed(flat_dims):
                index.append(i % n)
                i = i // n
            index = tuple(reversed(index))
            target[index] = target[index] + landed[index]
            return carry

        if total == 1:
            one(0, 0)
        else:
            lax.fori_loop(0, total, one, 0)

    def run(self, stage):
        p, every = self.place, slice(None)
        if stage == 0:
            self.loads = []
            for x in (0, 1):
                self.push(x, self.full.at[:, :, :, 1 - p.c, :, self.lanes(x)], self.in_c.at[x], "c")
                load = pltpu.make_async_copy(
                    self.full.at[:, :, :, p.c, :, self.lanes(x)], self.sums.at[x], self.local.at[x]
                )
                load.start()
                self.loads.append(load)
            return
        if stage == 1:
            for x in (0, 1):
                self.arrive(x, self.in_c.at[x], "c")
                self.loads[x].wait()
            self.add(self.sums, self.in_c)
            if self.order == "xy":
                self.push(2, self.sums.at[1 - p.x], self.in_1.at[...], "x")
            else:
                for x in (0, 1):
                    self.push(2 + x, self.sums.at[x, :, :, 1 - p.y], self.in_1.at[x], "y")
        elif stage == 2:
            if self.order == "xy":
                self.arrive(2, self.in_1, "x")
                self.add(self.sums.at[p.x], self.in_1)
                self.push(4, self.sums.at[p.x, :, :, 1 - p.y], self.in_2, "y")
            else:
                for x in (0, 1):
                    self.arrive(2 + x, self.in_1.at[x], "y")
                    self.add(self.sums.at[x, :, :, p.y], self.in_1.at[x])
                self.push(4, self.sums.at[1 - p.x, :, :, p.y], self.in_2, "x")
        elif stage == 3:
            self.arrive(4, self.in_2, "y" if self.order == "xy" else "x")
            self.add(self.sums.at[p.x, :, :, p.y], self.in_2)
            self.push(5, self.sums.at[p.x, :, 1 - p.zl, p.y], self.in_l, "zl")
        elif stage == 4:
            self.arrive(5, self.in_l, "zl")
            self.add(self.sums.at[p.x, :, p.zl, p.y], self.in_l)
            self.push(6, self.sums.at[p.x, 1 - p.zh, p.zl, p.y], self.in_h, "zh")
        else:
            self.arrive(6, self.in_h, "zh")
            self.store(
                self.sums[p.x, p.zh, p.zl, p.y].astype(F32) + self.in_h[...].astype(F32)
            )
            self.drain()

    def store(self, value):
        ref, first = self.out
        ref[:, first : first + self.width] = value


class ScatterStart(Scatter):
    def run(self, stage):
        if stage < 3:
            super().run(stage)
            return
        p = self.place
        self.arrive(4, self.in_2, "y" if self.order == "xy" else "x")
        lanes = slice(self.lane, self.lane + self.width)
        for a in (0, 1):
            for b in (0, 1):
                self.out[a, b, :, lanes] = self.sums[p.x, a, b, p.y] + self.in_2[a, b]
        self.drain()


class ScatterEnd(Mover):
    def __init__(self, place, quarter, out, bufs, send, recv, base):
        super().__init__(place, send, recv, base)
        self.quarter, self.out = quarter, out
        self.in_l, self.sums, self.in_h = bufs

    def run(self, stage):
        p = self.place
        if stage == 0:
            self.push(0, self.quarter.at[:, 1 - p.zl], self.in_l, "zl")
        elif stage == 1:
            self.arrive(0, self.in_l, "zl")
            for a in (0, 1):
                self.sums[a] = self.quarter[a, p.zl] + self.in_l[a]
            self.push(1, self.sums.at[1 - p.zh], self.in_h, "zh")
        else:
            self.arrive(1, self.in_h, "zh")
            self.out[...] = self.sums[p.zh].astype(F32) + self.in_h[...].astype(F32)
            self.drain()


def scatter_scratch(rows, width, order):
    first = (2, 2, 2) if order == "xy" else (2, 2, 2)
    return [
        pltpu.VMEM((2, 2, 2, 2, rows, width), BF),
        pltpu.VMEM((2, 2, 2, 2, rows, width), BF),
        pltpu.VMEM(first + (rows, width), BF),
        pltpu.VMEM((2, 2, rows, width), BF),
        pltpu.VMEM((2, rows, width), BF),
        pltpu.VMEM((rows, width), BF),
    ]


class Total(Mover):
    def __init__(self, place, block, out, sums, landed, send, recv, base, features):
        super().__init__(place, send, recv, base)
        self.features = features
        self.block, self.out, self.sums, self.landed = block, out, sums, landed

    def run(self, stage):
        if stage > 0:
            self.arrive(stage - 1, self.landed.at[stage - 1], WAYS[stage - 1])
            self.sums[stage] = self.sums[stage - 1] + self.landed[stage - 1]
        if stage < 5:
            self.push(stage, self.sums.at[stage], self.landed.at[stage], WAYS[stage])
        else:
            final = self.sums[5]
            self.out[...] = final
            squares = final[STATS : STATS + 1, :]
            self.out[STATS + 1 : STATS + 2, :] = jnp.sqrt(squares / (squares[:, 3:4] * self.features))
            self.drain()


GATHERS = (
    (0, 0, 384, "yx", 0, 0), (0, 384, 384, "xy", 1, 0), (1, 0, 128, "yx", 3, 0),
    (0, 768, 256, "yx", 2, 0), (0, 1024, 128, "xy", 2, 256),
    (3, 0, 384, "yx", 5, 0), (3, 384, 384, "xy", 5, 384),
    (3, 768, 384, "yx", 5, 768), (3, 1152, 384, "xy", 5, 1152),
    (2, 0, 256, "yx", 4, 0), (2, 256, 128, "xy", 4, 256),
    (4, 0, 768, "yx", 6, 0), (4, 768, 768, "xy", 6, 768),
)
GATHER_WAVES = "qqqvvaabbbbdd"
GATHER_LAST = (4,) * 11 + (3, 3)
GATHER_AT = {
    "start": (("q", 0), ("q", 1), ("q", 2), ("v", 0), ("q", 3), ("v", 1), ("a", 0), ("v", 2),
              ("a", 1), ("q", 4), ("b", 0), ("q", 5), ("a", 2)),
    "load": (("v", 3), ("a", 3), ("b", 1), ("d", 0)),
    "newton1": (("v", 4), ("b", 2)),
    "third2": (("v", 5), ("a", 4), ("d", 1)),
    "first1": (("b", 3),),
    "first2": (("a", 5),),
    "mix0": (("d", 2),),
    "end": (("b", 4), ("d", 3), ("b", 5), ("d", 4)),
}
DOWN_GATHERS = GATHERS[-2:]
DOWN_SCATTERS = ((0, 0, 768, "xy"), (0, 768, 768, "yx"))
SCATTERS = (
    (1, 0, 768, "xy", 1, 0), (1, 768, 768, "yx", 1, 768),
    (0, 0, 256, "xy", 0, 0), (0, 256, 128, "yx", 0, 256),
    (2, 768, 256, "xy", 4, 0), (2, 1024, 128, "yx", 4, 256),
    (2, 0, 256, "yx", 2, 0), (2, 256, 128, "xy", 2, 256),
    (2, 384, 256, "xy", 3, 0), (2, 640, 128, "yx", 3, 256),
)
SCATTER_WAVES = "aaaavvqqkk"
SCATTER_AT = {
    "start": (("a", 0), ("d", 0)),
    "second0": (("d", 1), ("a", 1)),
    "second1": (("d", 2),),
    "second2": (("t", 0),),
    "values": (("v", 0), ("t", 1)),
    "newton0": (("t", 2),),
    "newton1": (("t", 3),),
    "newton2": (("a", 2), ("v", 1), ("t", 4)),
    "third1": (("t", 5),),
    "queries": (("q", 0), ("a", 3)),
    "keys": (("k", 0), ("q", 1), ("v", 2)),
    "input0": (("k", 1), ("v", 3), ("q", 2), ("a", 4)),
    "input1": (("k", 2), ("v", 4), ("q", 3), ("k", 3)),
    "end": (("v", 5), ("q", 4), ("k", 4), ("a", 5), ("q", 5), ("k", 5)),
}


def gather_parts(place, cuts, shards, wholes, send, recv, local):
    parts = []
    for n, (i, lane, width, order, source, first) in enumerate(cuts):
        shard = shards[source].at[:, pl.ds(first, width)]
        parts.append(Gather(place, shard, wholes[i], lane, width, order, send, recv, COPIES * n,
                            local.at[n], GATHER_LAST[n]))
    return parts


def gather_scratch(cuts):
    n = len(cuts)
    return [
        pltpu.SemaphoreType.DMA((COPIES * n,)),
        pltpu.SemaphoreType.DMA((COPIES * n,)),
        pltpu.SemaphoreType.DMA((n,)),
    ]


def gather_shapes(rows, wide, units):
    whole = (2, 2, 2, 2)
    return (
        jax.ShapeDtypeStruct(whole + (rows, 3 * wide), BF),
        jax.ShapeDtypeStruct(whole + (BLOCK, 256), F32),
        jax.ShapeDtypeStruct(whole + (rows, wide), BF),
        jax.ShapeDtypeStruct(whole + (rows, units), BF),
        jax.ShapeDtypeStruct(whole + (rows, units), BF),
    )


SUM_COPIES = 7


def scatter_parts(place, cuts, fulls, outs, refs):
    send, recv, local = refs[-3:]
    return [
        Scatter(place, fulls[i], lane, width, order, (outs[n_out], first),
                refs[6 * n : 6 * n + 6], send, recv, SUM_COPIES * n, local.at[n])
        for n, (i, lane, width, order, n_out, first) in enumerate(cuts)
    ]


def all_scatter_scratch(cuts, rows, extra=0):
    out = []
    for _, _, width, order, *_ in cuts:
        out += scatter_scratch(rows, width, order)
    n = len(cuts)
    return out + [
        pltpu.SemaphoreType.DMA((SUM_COPIES * n + extra,)),
        pltpu.SemaphoreType.DMA((SUM_COPIES * n + extra,)),
        pltpu.SemaphoreType.DMA((n, 2)),
    ]


def norm_parts(values):
    centre = values - jnp.mean(values, axis=-1, keepdims=True)
    spread_of = jnp.mean(centre * centre, axis=-1, keepdims=True)
    inverse = lax.rsqrt(spread_of + 1e-05)
    return centre * inverse, inverse


def norm_grad(grad, gain, normal, inverse):
    scaled = grad * gain
    lean = jnp.mean(scaled, axis=-1, keepdims=True)
    along = jnp.mean(scaled * normal, axis=-1, keepdims=True)
    return inverse * (scaled - lean - normal * along)


TURNS = 12


def mid_kernel(slot, wide, *refs):
    (len_ref, ctx_ref, x_ref, cot_ref, outw_ref, inw_ref, partial_ref, gain_ref,
     dctx_ref, res_ref, out_ref, gin_ref, gout_ref, quarter_ref, ends_ref,
     downw_ref, hid_ref, turn_ref, act_ref, slope_ref, acc_ref, dlow_ref, gdown_ref, sum_ref) = refs[:24]
    place = Place()
    greet(place)
    gsend, grecv, glocal = refs[-3 - 3 : -3]
    late = [
        GatherEnd(place, partial_ref, downw_ref, lane, width, order, gsend, grecv, 4 * n, glocal.at[n])
        for n, (_, lane, width, order, *_) in enumerate(DOWN_GATHERS)
    ]
    down = [
        ScatterStart(place, gdown_ref, lane, width, order, quarter_ref,
                     refs[24 + 6 * n : 30 + 6 * n], refs[-3], refs[-2], SUM_COPIES * n, refs[-1].at[n])
        for n, (_, lane, width, order) in enumerate(DOWN_SCATTERS)
    ]

    def both(parts, stage):
        for part in parts:
            part.run(stage)

    both(late, 0)
    hidden_units = act_ref.shape[1]
    step = hidden_units // TURNS
    length = len_ref[lax.axis_index("tensor")]
    gain_one, bias_one = gain_ref[0:1, :], gain_ref[1:2, :]
    gain_two, bias_two = gain_ref[2:3, :], gain_ref[3:4, :]
    sum_ref[...] = jnp.zeros(sum_ref.shape, F32)

    def valid_of(i, rows):
        row = lax.broadcasted_iota(jnp.int32, (rows, 1), 0) + i * rows
        return (row < length).astype(F32)

    def span(i, rows):
        return pl.ds(pl.multiple_of(i * rows, rows), rows)

    def count(row, values):
        sum_ref[row : row + 1, :] += jnp.sum(values, axis=0, keepdims=True)

    def unit(i):
        return pl.ds(pl.multiple_of(i * step, 128), step)

    def weight(ref, lanes):
        return ref[:, :, :, :, :, lanes].reshape(wide, -1)

    def project(i, carry):
        rows = span(i, TALL)
        acc_ref[rows, :] = mm(ctx_ref[rows, :], outw_ref[...], NT)
        return carry

    lax.fori_loop(0, slot // TALL, project, 0)

    def norm_one(i, carry):
        rows = span(i, ROWS)
        valid = valid_of(i, ROWS)
        attn, x = acc_ref[rows, :], x_ref[rows, :].astype(F32)
        count(4, valid * x * x)
        count(5, valid * attn * attn)
        total = x + attn
        res_ref[rows, :] = total
        normal, _ = norm_parts(total)
        hid_ref[rows, :] = (normal * gain_one + bias_one).astype(BF)
        return carry

    lax.fori_loop(0, slot // ROWS, norm_one, 0)

    def expand(i, carry):
        lanes = unit(i)
        for block in range(slot // TALL):
            rows = slice(block * TALL, (block + 1) * TALL)
            pre = mm(hid_ref[rows, :], inw_ref[:, lanes])
            below = 0.5 * (1.0 + lax.erf(pre * 0.5**0.5))
            act_ref[rows, lanes] = (pre * below).astype(BF)
            slope = below + pre * jnp.exp(-0.5 * pre * pre) * (2.0 * jnp.pi) ** -0.5
            slope_ref[rows, lanes] = slope.astype(BF)
        return carry

    lax.fori_loop(0, TURNS, expand, 0)
    both(late, 1)
    both(late, 2)

    def contract(i, carry):
        rows = span(i, 512)
        acc_ref[rows, :] = mm(act_ref[rows, :], weight(downw_ref, slice(None)), NT)
        return carry

    lax.fori_loop(0, slot // 512, contract, 0)

    def norm_two(i, carry):
        rows = span(i, ROWS)
        valid = valid_of(i, ROWS)
        ffn = acc_ref[rows, :]
        count(6, valid * ffn * ffn)
        normal, inverse = norm_parts(hid_ref[rows, :].astype(F32) + ffn)
        out_ref[rows, :] = (normal * gain_two + bias_two).astype(BF)
        grad = cot_ref[rows, :].astype(F32) * valid
        count(2, grad * normal)
        count(3, grad)
        back = norm_grad(grad, gain_two, normal, inverse)
        acc_ref[rows, :] = back
        dlow_ref[rows, :] = back.astype(BF)
        return carry

    lax.fori_loop(0, slot // ROWS, norm_two, 0)
    turn_ref[...] = jnp.transpose(dlow_ref[...])

    def down_grad(i, carry):
        lanes = unit(i)
        value = mm(turn_ref[...], act_ref[:, lanes]).astype(BF)
        gdown_ref[:, :, :, :, :, lanes] = value.reshape(gdown_ref.shape[:-1] + (step,))
        return carry

    lax.fori_loop(0, TURNS, down_grad, 0)
    both(down, 0)
    turn_ref[...] = jnp.transpose(hid_ref[...])

    def back_grad(i, carry):
        lanes = unit(i)
        weights = weight(downw_ref, lanes)
        for block in range(slot // TALL):
            rows = slice(block * TALL, (block + 1) * TALL)
            pre = mm(dlow_ref[rows, :], weights) * slope_ref[rows, lanes].astype(F32)
            slope_ref[rows, lanes] = pre.astype(BF)
        gin_ref[:, lanes] = mm(turn_ref[...], slope_ref[:, lanes]).astype(BF)
        return carry

    lax.fori_loop(0, TURNS // 2, back_grad, 0)
    both(down, 1)
    lax.fori_loop(TURNS // 2, TURNS, back_grad, 0)

    def narrow(i, carry):
        rows = span(i, 512)
        acc_ref[rows, :] += mm(slope_ref[rows, :], inw_ref[...], NT)
        return carry

    lax.fori_loop(0, slot // 512, narrow, 0)
    both(down, 2)

    def norm_one_back(i, carry):
        rows = span(i, ROWS)
        grad = acc_ref[rows, :]
        normal, inverse = norm_parts(res_ref[rows, :])
        count(0, grad * normal)
        count(1, grad)
        back = norm_grad(grad, gain_one, normal, inverse)
        res_ref[rows, :] = back
        dlow_ref[rows, :] = back.astype(BF)
        return carry

    lax.fori_loop(0, slot // ROWS, norm_one_back, 0)
    turn_ref[...] = jnp.transpose(dlow_ref[...])
    for block in range(3):
        rows = slice(block * wide // 3, (block + 1) * wide // 3)
        gout_ref[rows, :] = mm(turn_ref[rows, :], ctx_ref[...]).astype(BF)

    def reach(i, carry):
        rows = span(i, TALL)
        dctx_ref[rows, :] = mm(dlow_ref[rows, :], outw_ref[...]).astype(BF)
        return carry

    lax.fori_loop(0, slot // TALL, reach, 0)
    ends_ref[...] = jnp.zeros(ends_ref.shape, F32)
    tiles = wide // 128
    for n in range(4):
        for tile in range(tiles):
            ends_ref[n * tiles + tile : n * tiles + tile + 1, :] = sum_ref[n : n + 1, tile * 128 : (tile + 1) * 128]
    lane = lax.broadcasted_iota(jnp.int32, (1, 128), 1)
    line = jnp.where(lane == 3, jnp.minimum(length, slot).astype(F32), 0.0)
    for n in range(3):
        line = jnp.where(lane == n, jnp.sum(sum_ref[4 + n : 5 + n, :], axis=1, keepdims=True), line)
    ends_ref[STATS : STATS + 1, :] = line
    both(down, 3)


def mid_call(length, ctx, x, cot, outw, inw, part, gains):
    slot, wide = x.shape
    units = inw.shape[1]
    rows = part.shape[-2]
    shape = jax.ShapeDtypeStruct
    whole = (2, 2, 2, 2, rows, units)
    n = len(DOWN_GATHERS)
    return pl.pallas_call(
        partial(mid_kernel, slot, wide),
        out_shape=(
            shape((slot, wide), BF),
            shape((slot, wide), F32),
            shape((slot, wide), BF),
            shape((wide, units), BF),
            shape((wide, wide), BF),
            shape((2, 2, rows, units // 2), BF),
            shape((40, 128), F32),
        ),
        in_specs=[SM] + [VM] * 5 + [ANY, VM],
        out_specs=[VM] * 7,
        scratch_shapes=[
            pltpu.VMEM(whole, BF),
            pltpu.VMEM((slot, wide), BF),
            pltpu.VMEM((wide, slot), BF),
            pltpu.VMEM((slot, units), BF),
            pltpu.VMEM((slot, units), BF),
            pltpu.VMEM((slot, wide), F32),
            pltpu.VMEM((slot, wide), BF),
            pltpu.VMEM(whole, BF),
            pltpu.VMEM((8, wide), F32),
        ]
        + all_scatter_scratch(DOWN_SCATTERS, rows)[:-3]
        + [
            pltpu.SemaphoreType.DMA((4 * n,)),
            pltpu.SemaphoreType.DMA((4 * n,)),
            pltpu.SemaphoreType.DMA((n, 2)),
        ]
        + all_scatter_scratch(DOWN_SCATTERS, rows)[-3:],
        compiler_params=pltpu.CompilerParams(
            vmem_limit_bytes=67043328, collective_id=4, has_side_effects=True
        ),
        name="middle",
    )(length, ctx, x, cot, outw, inw, part, gains)


D = 768
BOTH = ("tensor", "dp")


def rows_sum(left_op, right_op):
    return lax.dot_general(left_op, right_op, (TN, ((), ())), preferred_element_type=F32)


def cols_sum(left_op, right_op):
    return lax.dot_general(left_op, right_op, (NT, ((), ())), preferred_element_type=F32)


def dense(left_op, right_op):
    return jnp.dot(left_op, right_op, preferred_element_type=F32)


def norm_back(grad, gain, normal, inverse):
    return (
        norm_grad(grad, gain, normal, inverse),
        jnp.sum(grad * normal, axis=0),
        jnp.sum(grad, axis=0),
    )


def gather_plain(pieces):
    sizes = lax.axis_size("tensor"), lax.axis_size("dp")
    out = []
    for piece in pieces:
        joined = lax.all_gather(piece, BOTH, axis=0, tiled=True)
        joined = joined.reshape(sizes[0], sizes[1] * piece.shape[0], piece.shape[1])
        out.append(joined.transpose(1, 0, 2).reshape(joined.shape[1], -1))
    return out


def scatter_plain(fulls):
    parts = lax.axis_size("tensor")
    out = []
    for full in fulls:
        stacked = full.reshape(full.shape[0], parts, -1).transpose(1, 0, 2).reshape(-1, full.shape[1] // parts)
        out.append(lax.psum_scatter(stacked, BOTH, scatter_dimension=0, tiled=True).astype(F32))
    return out


def per_device(own, x_in, lengths, cotangent, w_query, w_key, w_value, w_out, w_in, w_down,
               conv_weight, ln1_gain, ln1_bias, ln2_gain, ln2_bias):
    tensor_index = lax.axis_index("tensor")
    slot = x_in.shape[0]
    parts = lax.axis_size("tensor")
    length = lengths

    later = (w_out.T, w_in, w_down.T)
    few, own_heads, count = ln1_gain.shape[0], conv_weight.shape[0], conv_weight.shape[1]

    def rows_of(array, rows):
        return jnp.pad(array, ((0, rows - array.shape[0]), (0, 128 - array.shape[1])))

    vectors = jnp.stack([ln1_gain, ln1_bias, ln2_gain, ln2_bias])
    block = jnp.concatenate(
        [rows_of(vectors, TAPS_AT), rows_of(conv_weight, FLIP_AT - TAPS_AT),
         rows_of(conv_weight[:, ::-1], BLOCK - FLIP_AT)],
        axis=0,
    )
    if own:
        wholes, saved = attn_fwd(
            length, x_in, parts, own, (w_query, w_key, w_value, block) + later
        )
        qkv_w, blocks, out_w, in_w = (w.reshape(-1, w.shape[-1]) for w in wholes[:4])
        taps = blocks
        blocks = blocks.reshape(lax.axis_size("dp"), BLOCK, parts, 128)
    else:
        qkv_w, out_w, in_w, down_w = gather_plain(
            (jnp.concatenate([w_query, w_key, w_value], axis=1),) + later
        )
        blocks = lax.all_gather(block, ("dp", "tensor"), axis=0)
        blocks = blocks.reshape(-1, parts, BLOCK, 128).transpose(0, 2, 1, 3)
        taps = blocks[0].reshape(BLOCK, parts * 128)
        _, saved = attn_fwd(length, x_in, parts, own, (qkv_w, taps))
    gains = blocks[:, :4, :, :few].transpose(1, 0, 2, 3).reshape(4, D)
    gain_one, bias_one, gain_two, bias_two = gains[0], gains[1], gains[2], gains[3]
    ctx, saved = saved[0], saved[1:]

    if own:
        d_ctx, d_res1, output, grad_in, grad_out, quarter, ends = mid_call(
            length, ctx, x_in, cotangent, out_w, in_w, wholes[4], jnp.pad(gains, ((0, 4), (0, 0)))
        )
        fulls = [grad_out, grad_in]
    else:
        quarter = None
        tokens = x_in.astype(F32)
        mine = lax.dynamic_slice_in_dim(lengths, tensor_index, 1)
        valid = (jnp.arange(slot, dtype=jnp.int32) < mine[0]).astype(F32)[:, None]
        attn_branch = cols_sum(ctx, out_w)
        normal_one, inverse_one = norm_parts(tokens + attn_branch)
        hidden = (normal_one * gain_one + bias_one).astype(BF)
        pre = dense(hidden, in_w)
        below = 0.5 * (1.0 + lax.erf(pre * 0.5**0.5))
        act = (pre * below).astype(BF)
        slope = (below + pre * jnp.exp(-0.5 * pre * pre) * (2.0 * jnp.pi) ** -0.5).astype(BF)
        ffn_branch = cols_sum(act, down_w)
        normal_two, inverse_two = norm_parts(hidden.astype(F32) + ffn_branch)
        output = (normal_two * gain_two + bias_two).astype(BF)
        grad_result = cotangent.astype(F32) * valid
        d_res2, grad_gain_two, grad_bias_two = norm_back(grad_result, gain_two, normal_two, inverse_two)
        d_ffn = d_res2.astype(BF)
        grad_down = rows_sum(d_ffn, act)
        d_pre = (dense(d_ffn, down_w) * slope.astype(F32)).astype(BF)
        grad_in = rows_sum(hidden, d_pre)
        d_hidden = cols_sum(d_pre, in_w) + d_res2
        d_res1, grad_gain_one, grad_bias_one = norm_back(d_hidden, gain_one, normal_one, inverse_one)
        d_attn = d_res1.astype(BF)
        grad_out = rows_sum(d_attn, ctx)
        d_ctx = dense(d_attn, out_w).astype(BF)
        fulls = [grad_out.astype(BF), grad_in.astype(BF), grad_down.astype(BF)]

        def total(branch):
            return jnp.sum(valid * branch * branch)

        sums = jnp.stack([total(tokens), total(attn_branch), total(ffn_branch), jnp.sum(valid)])
        ends = jnp.concatenate(
            [
                jnp.stack([grad_gain_one, grad_bias_one, grad_gain_two, grad_bias_two]).reshape(24, 128),
                jnp.zeros((12, 128), F32),
                jnp.pad(sums[None], ((0, 3), (0, 124))),
            ],
            axis=0,
        )
    grads = attn_bwd(length, d_ctx, saved, taps, x_in.T, qkv_w, d_res1, ends, parts, own, fulls, quarter)
    input_grad, summed = grads[-2:]
    if own:
        weight_grads = (*grads[2:5], grads[0].T, grads[1], grads[5].T)
        stats = summed[STATS + 1, :3]
    else:
        early, (late,) = scatter_plain(fulls), scatter_plain([grads[0]])
        width = late.shape[1] // 3
        weight_grads = (
            late[:, :width], late[:, width : 2 * width], late[:, 2 * width :],
            early[0].T, early[1], early[2].T,
        )
        summed = lax.psum(summed, ("dp", "tensor"))
        stats = jnp.sqrt(summed[STATS, :3] / (summed[STATS, 3] * D))
    share = D // lax.axis_size(("dp", "tensor"))
    start_at = lax.axis_index(("dp", "tensor")) * share
    vectors = lax.dynamic_slice_in_dim(summed[:24].reshape(4, D), start_at, share, 1)
    conv_grad = lax.dynamic_slice_in_dim(summed, 24 + tensor_index * own_heads, own_heads, 0)[:, :count]
    return (
        output, input_grad, *weight_grads,
        conv_grad, vectors[0], vectors[1], vectors[2], vectors[3], stats,
    )


def solution(mesh):
    own = mesh.shape["dp"] == 16 and mesh.shape["tensor"] == 2
    rows, both = P(("dp", "tensor"), None), P(("dp", "tensor"))
    split, crossed = P("dp", "tensor"), P("tensor", "dp")
    return jax.shard_map(
        partial(per_device, own),
        mesh=mesh,
        in_specs=(rows, P("dp"), rows, split, split, split, crossed, split, crossed,
                  P("tensor", None), both, both, both, both),
        out_specs=(rows, rows, split, split, split, crossed, split, crossed,
                   P("tensor", None), both, both, both, both, P()),
        check_vma=False,
    )
```

```python
from functools import partial

import jax
import jax.numpy as jnp
from jax import lax
from jax.experimental import pallas as pl
from jax.experimental.pallas import tpu as pltpu
from jax.sharding import PartitionSpec as P

ANY = pl.BlockSpec(memory_space=pl.ANY)
F32, BF = jnp.float32, jnp.bfloat16
NN, NT, TN = ((1,), (0,)), ((1,), (1,)), ((0,), (0,))
MARKS = 64
HEAD = 64
PACK = 4
WIDE = PACK * HEAD
TAPS = 33
EDGE = TAPS // 2
ROWS = 128
TALL = 256
TAPS_AT, FLIP_AT, BLOCK = 8, 16, 24
STATS = 36
WINDOW = ROWS + 2 * EDGE
STEPS = 6
KEPT = 4


def mm(a, b, dims=NN):
    return lax.dot_general(a, b, (dims, ((), ())), preferred_element_type=F32)


def halves(a):
    high = a.astype(BF)
    return high, (a - high.astype(F32)).astype(BF)


def mm3(a, b, dims=NN):
    (ah, al), (bh, bl) = a, b
    return mm(ah, bh, dims) + (mm(ah, bl, dims) + mm(al, bh, dims))


def mm3f(a, b, dims=NN):
    return mm3(halves(a), halves(b), dims)


def grid_of(shape):
    return (
        lax.broadcasted_iota(jnp.int32, shape, 0),
        lax.broadcasted_iota(jnp.int32, shape, 1),
    )


def block_mask():
    row, col = grid_of((WIDE, WIDE))
    return row // HEAD == col // HEAD


def eye():
    row, col = grid_of((WIDE, WIDE))
    return (row == col).astype(F32)


def spread(packed, mask):
    full = jnp.concatenate([packed] * PACK, axis=0)
    return jnp.where(mask, full, jnp.zeros_like(full))


def gather_up(full):
    return sum(full[i * MARKS : (i + 1) * MARKS] for i in range(PACK))


def segment_reduce(a, fill, op):
    lane = lax.broadcasted_iota(jnp.int32, (a.shape[0], 128), 1) < HEAD
    parts = []
    for tile in range(a.shape[1] // 128):
        piece = a[:, tile * 128 : (tile + 1) * 128]
        low = op(jnp.where(lane, piece, fill), axis=1, keepdims=True)
        high = op(jnp.where(lane, fill, piece), axis=1, keepdims=True)
        parts.append(jnp.where(lane, low, high))
    return jnp.concatenate(parts, axis=1)


def average_matrix():
    row, col = grid_of((TALL // 16, TALL))
    return jnp.where(row == col // 16, 1.0 / 16, 0.0).astype(BF)


def average_back():
    row, col = grid_of((ROWS, ROWS // 16))
    return jnp.where(row // 16 == col, 1.0 / 16, 0.0).astype(BF)


def lanes_of(group):
    return slice(group * WIDE, (group + 1) * WIDE)


def put(ref, rows, which, wide, parts, start, value):
    share = wide // parts
    for tile in range(0, value.shape[1], 128):
        lane = start + tile
        at = (3 * (lane // share) + which) * share + lane % share
        ref[rows, at : at + 128] = value[:, tile : tile + 128]


def lhs(a):
    return jnp.concatenate(halves(a), axis=1)


def rhs(b):
    high, low = halves(b)
    return jnp.concatenate(
        [
            jnp.concatenate([high, low], axis=1),
            jnp.concatenate([high, jnp.zeros_like(high)], axis=1),
        ],
        axis=0,
    )


def pair_mm(left, right):
    out = mm(left, right)
    return out[:, :128] + out[:, 128:]


def fold(full):
    return full[:MARKS] + full[MARKS:]


def unfold(packed, mask):
    full = jnp.concatenate([packed, packed], axis=0)
    return jnp.where(mask, full, 0.0)


def pair_lanes(pair):
    return slice(pair * 128, (pair + 1) * 128)


def pair_consts():
    row, col = grid_of((128, 128))
    return row // HEAD == col // HEAD, (row == col).astype(F32)


def toeplitz(taps_ref, first, own_heads, group):
    parts = []
    for i in range(PACK):
        half, head = divmod(group * PACK + i, own_heads)
        line = taps_ref[first + head : first + head + 1, half * 128 : (half + 1) * 128]
        line = jnp.concatenate([line, jnp.zeros_like(line)], axis=1)
        line = jnp.broadcast_to(line, (ROWS, 256))
        parts.append(pltpu.roll(line, 0, 1, stride=1, stride_axis=0)[:, :WINDOW])
    return jnp.concatenate(parts, axis=0).astype(BF)


def diagonal_lanes(stacked):
    col = lax.broadcasted_iota(jnp.int32, (ROWS, WIDE), 1) // HEAD
    out = stacked[:ROWS]
    for i in range(1, PACK):
        out = jnp.where(col == i, stacked[i * ROWS : (i + 1) * ROWS], out)
    return out


def attn_fwd_kernel(slot, groups, parts, own, *refs):
    len_ref, x_ref = refs[:2]
    if own:
        shards, outs, refs = refs[2:9], refs[9:14], refs[14:]
        weight, taps_ref = outs[0], outs[1].at[0, 0, 0, 0]
    else:
        weight, taps_ref, refs = refs[2], refs[3], refs[4:]
    ctx_ref, *far, small_ref, far_chain = refs[:8]
    z_ref, k2_ref, s_ref, top_ref, t_ref = refs[8:13]
    near = refs[13:19]
    qh_ref, kh_ref, vp_ref, k1_ref, k3_ref, chain_ref = near
    leave = {
        name: pltpu.make_async_copy(here, there, refs[19].at[n])
        for n, (name, here, there) in enumerate(
            zip(("qh", "kh", "vp", "k1", "k3", "chain"), near, (*far, far_chain))
        )
    }
    refs = refs[:13] + refs[20:]
    moves = []
    if own:
        place = Place()
        greet(place)
        moves = gather_parts(place, GATHERS, shards, outs, *refs[13:])

    def advance(name):
        for which, stage in GATHER_AT.get(name, ()) if own else ():
            for part, wave in zip(moves, GATHER_WAVES):
                if wave == which:
                    part.run(stage)

    advance("start")
    count = slot // ROWS
    scale = HEAD ** -0.25
    length = len_ref[lax.axis_index("tensor")] if len_ref.shape[0] > 1 else len_ref[0]
    avg = average_matrix()
    wide = groups * WIDE
    share = wide // parts
    own_heads = share // HEAD
    vp_ref[0:EDGE, :] = jnp.zeros((EDGE, wide), BF)
    vp_ref[slot + EDGE : slot + 2 * EDGE, :] = jnp.zeros((EDGE, wide), BF)

    def columns(start, width):
        if own:
            return weight[:, :, :, :, :, start : start + width].reshape(-1, width)
        return weight[:, start : start + width]

    def valid_of(i, rows):
        row = lax.broadcasted_iota(jnp.int32, (rows, 1), 0) + i * rows
        return (row < length).astype(F32)

    def load(i, carry):
        rows = pl.ds(pl.multiple_of(i * TALL, TALL), TALL)
        few = pl.ds(pl.multiple_of(i * (TALL // 16), TALL // 16), TALL // 16)
        factor = valid_of(i, TALL) * scale
        for p in range(parts):
            both = mm(x_ref[rows, :], columns(3 * p * share, 2 * share)) * factor
            at = slice(p * share, (p + 1) * share)
            high, low = halves(both)
            qh_ref[rows, at] = high[:, :share]
            kh_ref[rows, at] = high[:, share:]
            means = mm(avg, high) + mm(avg, low)
            small_ref[0, few, at] = means[:, :share]
            small_ref[1, few, at] = means[:, share:]
        return carry

    lax.fori_loop(0, slot // TALL, load, 0)
    leave["qh"].start()
    leave["kh"].start()
    advance("load")
    mask = block_mask()
    pmask, one = pair_consts()
    pairs = 2 * groups

    for j in range(pairs):
        at = pair_lanes(j)
        ql, kl = unfold(small_ref[0, :, at], pmask), unfold(small_ref[1, :, at], pmask)
        a2 = jnp.where(pmask, mm3f(ql, kl, NT), -1e30)
        e2 = jnp.where(pmask, jnp.exp(a2 - jnp.max(a2, axis=1, keepdims=True)), 0.0)
        k2 = e2 / jnp.sum(e2, axis=1, keepdims=True)
        top = segment_reduce(jnp.sum(k2, axis=0, keepdims=True), -1e30, jnp.max)
        k2_ref[j] = lhs(k2)
        small_ref[2, :, at] = fold(k2)
        z_ref[j] = jnp.transpose(k2) / top

    def newton(step, carry):
        every = range(pairs)
        z = [z_ref[j] for j in every]
        p = [pair_mm(k2_ref[j], rhs(z[j])) for j in every]
        left = [lhs(p[j]) for j in every]
        t2 = [15.0 * one - pair_mm(left[j], rhs(7.0 * one - p[j])) for j in every]
        t3 = [13.0 * one - pair_mm(left[j], rhs(t2[j])) for j in every]
        new = [0.25 * pair_mm(lhs(z[j]), rhs(t3[j])) for j in every]
        for j in every:
            for n, value in enumerate((z, p, t2, t3)):
                chain_ref[step, n, :, pair_lanes(j)] = fold(value[j])
            z_ref[j] = new[j]
        return carry

    lax.fori_loop(0, STEPS // 2, newton, 0)
    advance("newton0")
    lax.fori_loop(STEPS // 2, STEPS, newton, 0)
    leave["chain"].start()
    advance("newton1")

    for g in range(groups):
        at = lanes_of(g)
        ql = spread(small_ref[0, :, at], mask).astype(BF)
        top_ref[...] = jnp.full(top_ref.shape, -jnp.inf, F32)

        def scores(i, carry):
            rows = pl.ds(pl.multiple_of(i * ROWS, ROWS), ROWS)
            row = lax.broadcasted_iota(jnp.int32, (ROWS, 1), 0) + i * ROWS
            a3 = jnp.where(row < length, mm(kh_ref[rows, at], ql, NT), -1e9)
            s_ref[rows, :] = a3
            top_ref[0:1, :] = jnp.maximum(top_ref[0:1, :], jnp.max(a3, axis=0, keepdims=True))
            return carry

        lax.fori_loop(0, count, scores, 0)
        peak = top_ref[0:1, :]
        top_ref[0:1, :] = jnp.zeros((1, WIDE), F32)

        def powers(i, carry):
            rows = pl.ds(pl.multiple_of(i * ROWS, ROWS), ROWS)
            e3 = jnp.exp(s_ref[rows, :] - peak)
            s_ref[rows, :] = e3
            top_ref[0:1, :] += jnp.sum(e3, axis=0, keepdims=True)
            return carry

        lax.fori_loop(0, count, powers, 0)
        inverse = 1.0 / top_ref[0:1, :]

        def weigh(i, carry):
            rows = pl.ds(pl.multiple_of(i * ROWS, ROWS), ROWS)
            k3_ref[rows, at] = (s_ref[rows, :] * inverse).astype(BF)
            return carry

        lax.fori_loop(0, count, weigh, 0)
        advance(f"third{g}")

    leave["k3"].start()
    ones = mask.astype(F32).astype(BF)
    for g in range(groups):
        at = lanes_of(g)
        kl = spread(small_ref[1, :, at], mask).astype(BF)

        def first(i, carry):
            rows = pl.ds(pl.multiple_of(i * ROWS, ROWS), ROWS)
            a1 = mm(qh_ref[rows, at], kl, NT)
            e1 = jnp.exp(a1 - segment_reduce(a1, -jnp.inf, jnp.max)).astype(BF)
            k1_ref[rows, at] = (e1.astype(F32) / mm(e1, ones)).astype(BF)
            return carry

        lax.fori_loop(0, count, first, 0)
        advance(f"first{g}")

    leave["k1"].start()

    def load_values(i, carry):
        rows = pl.ds(pl.multiple_of(i * TALL + EDGE, EDGE), TALL)
        valid = valid_of(i, TALL)
        x = x_ref[pl.ds(pl.multiple_of(i * TALL, TALL), TALL), :]
        for p in range(parts):
            value = mm(x, columns((3 * p + 2) * share, share)) * valid
            vp_ref[rows, p * share : (p + 1) * share] = value.astype(BF)
        return carry

    lax.fori_loop(0, slot // TALL, load_values, 0)
    leave["vp"].start()

    for g in range(groups):
        at = lanes_of(g)
        b = mm(k3_ref[:, at], vp_ref[EDGE : slot + EDGE, at], TN)
        b = jnp.where(mask, b, 0.0)
        for sub in range(2):
            j, inner = 2 * g + sub, pair_lanes(sub)
            z, piece = z_ref[j], b[inner, inner]
            small_ref[3, :, pair_lanes(j)] = fold(piece)
            small_ref[4, :, pair_lanes(j)] = fold(mm3f(z, piece))
            small_ref[5, :, pair_lanes(j)] = fold(z)
        t_ref[...] = toeplitz(taps_ref, TAPS_AT, own_heads, g)
        cb = spread(small_ref[4, :, at], mask).astype(BF)

        def mix(i, carry):
            rows = pl.ds(pl.multiple_of(i * ROWS, ROWS), ROWS)
            window = vp_ref[pl.ds(pl.multiple_of(i * ROWS, ROWS), WINDOW), at]
            ctx_ref[rows, at] = (
                mm(k1_ref[rows, at], cb) + diagonal_lanes(mm(t_ref[...], window))
            ).astype(BF)
            return carry

        lax.fori_loop(0, count, mix, 0)
        advance(f"mix{g}")
    advance("end")
    for copy in leave.values():
        copy.wait()


def attn_bwd_kernel(slot, groups, parts, own, *refs):
    (len_ref, g_ref, qh_ref, kh_ref, vp_ref, k1_ref, k3_ref, small_ref, chain_ref, taps_ref,
     xt_ref, w_ref, dres_ref, block_ref) = refs[:14]
    if own:
        fulls, left_refs, refs = refs[14:16], refs[16:18], refs[18:]
        outs, down_out, refs = refs[:5], refs[5], refs[6:]
    else:
        outs, refs = (refs[14],), refs[15:]
    late_ref = {}
    for n, (name, ref) in enumerate(
        (("chain", chain_ref), ("xt", xt_ref), ("w", w_ref), ("dres", dres_ref))
    ):
        late_ref[name] = pltpu.make_async_copy(ref, refs[2 + n], refs[6].at[n])
    chain_ref, xt_ref, w_ref, dres_ref = refs[2:6]
    dx_ref, sum_ref = refs[:2]
    refs = refs[:2] + refs[7:]
    (dqkv_ref, gp_ref, da1_ref, da3_ref, dk_ref, dz_ref, k2_ref,
     dql_ref, dkl_ref, t_ref, acc_ref) = refs[2:13]
    todo = {}
    wide_of = groups * WIDE
    if own:
        grad_ref, totals, landed = refs[13:16]
        place = Place()
        greet(place)
        scatters = scatter_parts(place, SCATTERS, fulls + (grad_ref,), outs, refs[26:])
        base = SUM_COPIES * len(SCATTERS)
        total = Total(place, totals.at[0], sum_ref, totals, landed, refs[-3], refs[-2], base, wide_of)
        tails = [
            ScatterEnd(place, left_refs[n], down_out, lane, order, refs[16 + 5 * n : 21 + 5 * n],
                       refs[-3], refs[-2], base + 5 + 3 * n)
            for n, (_, lane, _, order) in enumerate(DOWN_SCATTERS)
        ]
        todo = SCATTER_AT
    else:
        grad_ref = outs[0]
        totals = sum_ref

    def advance(name):
        for which, stage in todo.get(name, ()):
            if which == "t":
                total.run(stage)
            elif which == "d":
                for tail in tails:
                    tail.run(stage)
            else:
                for part, wave in zip(scatters, SCATTER_WAVES):
                    if wave == which:
                        part.run(stage)

    advance("start")
    for copy in late_ref.values():
        copy.start()
    count = slot // ROWS
    marks = ROWS // 16
    scale = HEAD ** -0.25
    length = len_ref[lax.axis_index("tensor")] if len_ref.shape[0] > 1 else len_ref[0]
    wide = groups * WIDE
    share = wide // parts
    own_heads = share // HEAD
    pairs = 2 * groups
    mask = block_mask()
    pmask, one = pair_consts()
    ones = mask.astype(F32).astype(BF)
    gp_ref[0:EDGE, :] = jnp.zeros((EDGE, wide), BF)
    gp_ref[slot + EDGE : slot + 2 * EDGE, :] = jnp.zeros((EDGE, wide), BF)
    gp_ref[EDGE : slot + EDGE, :] = g_ref[...]
    col = lax.broadcasted_iota(jnp.int32, (ROWS, WIDE), 1) // HEAD
    up, across = grid_of((ROWS, ROWS))
    flip = jnp.where(up + across == ROWS - 1, 1.0, 0.0).astype(BF)
    taps_lane = lax.broadcasted_iota(jnp.int32, (1, 128), 1) < TAPS

    def totals_row(row):
        return (0, slice(row, row + 1)) if own else slice(row, row + 1)

    if own:
        totals[0] = block_ref[...]
    else:
        sum_ref[...] = block_ref[...]

    for g in range(groups):
        at = lanes_of(g)
        cb = spread(small_ref[4, :, at], mask).astype(BF)

        def first(i, carry):
            rows = pl.ds(pl.multiple_of(i * ROWS, ROWS), ROWS)
            k1 = k1_ref[rows, at].astype(F32)
            dk1 = mm(g_ref[rows, at], cb, NT)
            high, low = halves(dk1 * k1)
            da1_ref[rows, at] = (k1 * (dk1 - (mm(high, ones) + mm(low, ones)))).astype(BF)
            return carry

        lax.fori_loop(0, count, first, 0)
        advance(f"first{g}")
        dc = jnp.where(mask, mm(k1_ref[:, at], g_ref[:, at], TN), 0.0)
        dkl_ref[:, at] = gather_up(jnp.where(mask, mm(da1_ref[:, at], qh_ref[:, at], TN), 0.0))
        many = jnp.ones((8, 128), BF)
        totals_of = []
        for sub in range(2):
            j, inner = 2 * g + sub, pair_lanes(sub)
            b, z = (unfold(small_ref[n, :, pair_lanes(j)], pmask) for n in (3, 5))
            piece = halves(dc[inner, inner])
            dz_ref[j] = mm3(halves(b), piece, NT)
            db = mm3(halves(z), piece, TN)
            dql_ref[:, pair_lanes(j)] = fold(db)
            high, low = halves(db * b)
            totals_of.append((mm(many, high, NT) + mm(many, low, NT))[0:1, :])
        peak = jnp.concatenate(totals_of, axis=1)
        dbb = spread(dql_ref[:, at], mask).astype(BF)
        t_ref[...] = toeplitz(taps_ref, FLIP_AT, own_heads, g)
        acc_ref[...] = jnp.zeros(acc_ref.shape, F32)

        def second(i, carry):
            rows = pl.ds(pl.multiple_of(i * ROWS, ROWS), ROWS)
            row = lax.broadcasted_iota(jnp.int32, (ROWS, 1), 0) + i * ROWS
            valid = (row < length).astype(F32)
            k3 = k3_ref[rows, at]
            vh = vp_ref[pl.ds(pl.multiple_of(i * ROWS + EDGE, EDGE), ROWS), at]
            dk3 = mm(vh, dbb, NT)
            da3_ref[rows, at] = (k3.astype(F32) * (dk3 - peak)).astype(BF)
            window = pl.ds(pl.multiple_of(i * ROWS, ROWS), WINDOW)
            dv = mm(k3, dbb) + diagonal_lanes(mm(t_ref[...], gp_ref[window, at]))
            put(dqkv_ref, rows, 2, wide, parts, g * WIDE, (dv * valid).astype(BF))
            grad = g_ref[rows, at]
            split = jnp.concatenate(
                [jnp.where(col == h, grad, jnp.zeros_like(grad)) for h in range(PACK)], axis=0
            )
            acc_ref[:, :WINDOW] += mm(split, vp_ref[window, at], NT)
            return carry

        lax.fori_loop(0, count, second, 0)
        for h in range(PACK):
            high, low = halves(acc_ref[h * ROWS : (h + 1) * ROWS, :])
            turned = pltpu.roll(mm(flip, high) + mm(flip, low), 0, 1, stride=1, stride_axis=0)
            line = pltpu.roll(jnp.sum(turned, axis=0, keepdims=True), 129, 1)[:, :128]
            totals[totals_row(24 + g * PACK + h)] = jnp.where(taps_lane, line, 0.0)
        dql_ref[:, at] = gather_up(jnp.where(mask, mm(da3_ref[:, at], kh_ref[:, at], TN), 0.0))
        advance(f"second{g}")

    def weight_grad(start, width):
        size = xt_ref.shape[0] // 4

        def block_grad(block, carry):
            rows = pl.ds(pl.multiple_of(block * size, 64), size)
            for p in range(parts):
                lanes = slice(3 * p * share + start, 3 * p * share + start + width)
                here = mm(xt_ref[rows, :], dqkv_ref[:, lanes]).astype(BF)
                if own:
                    four = here.reshape(2, 2, grad_ref.shape[-2], width)
                    grad_ref[block // 2, block % 2, :, :, :, lanes] = four
                else:
                    grad_ref[rows, lanes] = here
            return carry

        lax.fori_loop(0, 4, block_grad, 0)

    late_ref["xt"].wait()
    weight_grad(2 * share, share)
    advance("values")
    late_ref["chain"].wait()
    for j in range(pairs):
        dk_ref[j] = jnp.zeros((128, 128), F32)
        k2_ref[j] = unfold(small_ref[2, :, pair_lanes(j)], pmask)

    def newton(back, carry):
        step = STEPS - 1 - back
        every = range(pairs)
        z, p, t2, t3 = (
            [unfold(chain_ref[step, n, :, pair_lanes(j)], pmask) for j in every] for n in range(KEPT)
        )
        dz = [0.25 * dz_ref[j] for j in every]
        dt3 = [pair_mm(lhs(dz[j]), rhs(z[j])) for j in every]
        dt2 = [-pair_mm(lhs(dt3[j]), rhs(p[j])) for j in every]
        dp = [pair_mm(lhs(dt2[j]), rhs(p[j])) - pair_mm(lhs(t2[j]), rhs(dt3[j])) for j in every]
        dp = [dp[j] - pair_mm(lhs(7.0 * one - p[j]), rhs(dt2[j])) for j in every]
        for j in every:
            dk_ref[j] += pair_mm(lhs(z[j]), rhs(dp[j]))
        new = [pair_mm(lhs(t3[j]), rhs(dz[j])) + pair_mm(lhs(dp[j]), rhs(k2_ref[j])) for j in every]
        for j in every:
            dz_ref[j] = new[j]
        return carry

    for third_of in range(3):
        lax.fori_loop(third_of * STEPS // 3, (third_of + 1) * STEPS // 3, newton, 0)
        advance(f"newton{third_of}")

    for j in range(pairs):
        at = pair_lanes(j)
        k2 = k2_ref[j]
        sums = jnp.sum(k2, axis=0, keepdims=True)
        top = segment_reduce(sums, -1e30, jnp.max)
        hit = (sums == top).astype(F32)
        ties = segment_reduce(hit, 0.0, jnp.sum)
        dz0 = dz_ref[j]
        dtop = -segment_reduce(jnp.sum(dz0 * k2, axis=0, keepdims=True), 0.0, jnp.sum) / (top * top)
        dk2 = jnp.where(pmask, jnp.transpose(dk_ref[j]) + dz0 / top + hit * (dtop / ties), 0.0)
        da2 = halves(k2 * (dk2 - jnp.sum(dk2 * k2, axis=1, keepdims=True)))
        qls, kls = (halves(unfold(small_ref[n, :, at], pmask)) for n in (0, 1))
        dql_ref[:, at] += fold(mm3(da2, kls))
        dkl_ref[:, at] += fold(mm3(da2, qls, TN))
    back = average_back()

    for g in range(groups):
        at = lanes_of(g)
        qlb, klb = (spread(small_ref[n, :, at].astype(BF), mask) for n in (0, 1))

        def third(i, carry):
            rows = pl.ds(pl.multiple_of(i * ROWS, ROWS), ROWS)
            few = pl.ds(pl.multiple_of(i * marks, marks), marks)
            row = lax.broadcasted_iota(jnp.int32, (ROWS, 1), 0) + i * ROWS
            valid = jnp.where(row < length, scale, 0.0)
            dq = mm(da1_ref[rows, at], klb) + mm(back, dql_ref[few, at].astype(BF))
            dk = mm(da3_ref[rows, at], qlb) + mm(back, dkl_ref[few, at].astype(BF))
            put(dqkv_ref, rows, 0, wide, parts, g * WIDE, (dq * valid).astype(BF))
            put(dqkv_ref, rows, 1, wide, parts, g * WIDE, (dk * valid).astype(BF))
            return carry

        lax.fori_loop(0, count, third, 0)
        advance(f"third{g}")

    weight_grad(0, share)
    advance("queries")
    weight_grad(share, share)
    advance("keys")
    late_ref["w"].wait()
    late_ref["dres"].wait()

    def input_rows(i, carry):
        rows = pl.ds(pl.multiple_of(i * TALL, TALL), TALL)
        dx_ref[rows, :] = (dres_ref[rows, :] + mm(dqkv_ref[rows, :], w_ref[...], NT)).astype(BF)
        return carry

    for half in range(2):
        turns = slot // TALL // 2
        lax.fori_loop(half * turns, (half + 1) * turns, input_rows, 0)
        advance(f"input{half}")
    advance("end")


VM = pl.BlockSpec(memory_space=pltpu.VMEM)
SM = pl.BlockSpec(memory_space=pltpu.SMEM)
LIMIT = 60 * 1024 * 1024


def attn_fwd(length, x, parts, own, weights):
    slot, wide = x.shape
    groups = wide // WIDE
    shape = jax.ShapeDtypeStruct
    talks = dict(collective_id=1, has_side_effects=True) if own else {}
    gathered = gather_shapes(weights[0].shape[0], wide, 2 * weights[-1].shape[1]) if own else ()
    outs = pl.pallas_call(
        partial(attn_fwd_kernel, slot, groups, parts, own),
        out_shape=gathered
        + (
            shape((slot, wide), BF),
            shape((slot, wide), BF),
            shape((slot, wide), BF),
            shape((slot + 2 * EDGE, wide), BF),
            shape((slot, wide), BF),
            shape((slot, wide), BF),
            shape((6, MARKS, wide), F32),
            shape((STEPS, KEPT, MARKS, wide), F32),
        ),
        in_specs=[SM, VM] + [VM] * len(weights),
        out_specs=([VM, VM, ANY, ANY, ANY] if own else []) + [VM] + [ANY] * 5 + [VM, ANY],
        scratch_shapes=[
            pltpu.VMEM((2 * groups, 128, 128), F32),
            pltpu.VMEM((2 * groups, 128, 256), BF),
            pltpu.VMEM((slot, WIDE), F32),
            pltpu.VMEM((8, WIDE), F32),
            pltpu.VMEM((PACK * ROWS, WINDOW), BF),
            pltpu.VMEM((slot, wide), BF),
            pltpu.VMEM((slot, wide), BF),
            pltpu.VMEM((slot + 2 * EDGE, wide), BF),
            pltpu.VMEM((slot, wide), BF),
            pltpu.VMEM((slot, wide), BF),
            pltpu.VMEM((STEPS, KEPT, MARKS, wide), F32),
            pltpu.SemaphoreType.DMA((6,)),
        ]
        + (gather_scratch(GATHERS) if own else []),
        compiler_params=pltpu.CompilerParams(vmem_limit_bytes=LIMIT, **talks),
        name="attn_fwd",
    )(length, x, *weights)
    return outs[: len(gathered)], outs[len(gathered) :]


def attn_bwd(length, g, saved, taps, xt, weight, dres, block, parts, own, fulls, left=()):
    slot, wide = g.shape
    groups = wide // WIDE
    shape = jax.ShapeDtypeStruct
    talks = dict(collective_id=2, has_side_effects=True) if own else {}
    ends = (shape((slot, wide), BF), shape(block.shape, F32))
    if own:
        rows = fulls[0].shape[0] // 16
        fulls = [f.reshape(2, 2, 2, 2, rows, f.shape[1]) for f in fulls]
        width = 2 * left[0].shape[-1]
        outs = (shape((rows, wide // 2), F32), shape((rows, width), F32))
        outs += (shape((rows, wide // 2), F32),) * 3 + (shape((rows, width), F32),)
        extra = [
            pltpu.VMEM((2, 2, 2, 2, rows, 3 * wide), BF),
            pltpu.VMEM((6,) + block.shape, F32),
            pltpu.VMEM((5,) + block.shape, F32),
        ] + 2 * end_scratch(rows, width // 2) + all_scatter_scratch(SCATTERS, rows, 11)
    else:
        fulls, extra = [], []
        outs = (shape((wide, 3 * wide), BF),)
    return pl.pallas_call(
        partial(attn_bwd_kernel, slot, groups, parts, own),
        out_shape=outs + ends,
        in_specs=[SM] + [VM] * 7 + [ANY, VM, ANY, ANY, ANY, VM] + [ANY] * len(fulls) + [VM] * len(left),
        out_specs=[VM] * (len(outs) + 2),
        scratch_shapes=[
            pltpu.VMEM(saved[-1].shape, F32),
            pltpu.VMEM(xt.shape, BF),
            pltpu.VMEM(weight.shape, BF),
            pltpu.VMEM(dres.shape, F32),
            pltpu.SemaphoreType.DMA((4,)),
            pltpu.VMEM((slot, 3 * wide), BF),
            pltpu.VMEM((slot + 2 * EDGE, wide), BF),
            pltpu.VMEM((slot, wide), BF),
            pltpu.VMEM((slot, wide), BF),
            pltpu.VMEM((2 * groups, 128, 128), F32),
            pltpu.VMEM((2 * groups, 128, 128), F32),
            pltpu.VMEM((2 * groups, 128, 128), F32),
            pltpu.VMEM((MARKS, wide), F32),
            pltpu.VMEM((MARKS, wide), F32),
            pltpu.VMEM((PACK * ROWS, WINDOW), BF),
            pltpu.VMEM((PACK * ROWS, 256), F32),
        ]
        + extra,
        compiler_params=pltpu.CompilerParams(vmem_limit_bytes=67043328, **talks),
        name="attn_bwd",
    )(length, g, *saved, taps, xt, weight, dres, block, *fulls, *left)
MESH = pl.DeviceIdType.MESH
WAYS = ("zh", "zl", "y", "x", "c")
COPIES = 11
STAGES = 6


class Place:
    def __init__(self):
        dp = lax.axis_index("dp")
        self.x = lax.axis_index("tensor")
        self.zh, self.zl = dp // 8, (dp // 4) % 2
        self.y, self.c = (dp // 2) % 2, dp % 2

    def at(self, way):
        spot = {w: getattr(self, w) for w in WAYS}
        spot[way] = 1 - spot[way]
        return {
            "dp": spot["zh"] * 8 + spot["zl"] * 4 + spot["y"] * 2 + spot["c"],
            "tensor": spot["x"],
        }


def greet(place):
    barrier = pltpu.get_barrier_semaphore()
    for way in WAYS:
        pl.semaphore_signal(barrier, inc=1, device_id=place.at(way), device_id_type=MESH)
    pl.semaphore_wait(barrier, len(WAYS))


class Mover:
    def __init__(self, place, send, recv, base):
        self.place, self.send, self.recv, self.base = place, send, recv, base
        self.started = []

    def copy(self, index, src, dst, way):
        return pltpu.make_async_remote_copy(
            src_ref=src, dst_ref=dst,
            send_sem=self.send.at[self.base + index], recv_sem=self.recv.at[self.base + index],
            device_id=self.place.at(way), device_id_type=MESH,
        )

    def push(self, index, src, dst, way):
        copy = self.copy(index, src, dst, way)
        copy.start()
        self.started.append(copy)

    def arrive(self, index, ref, way):
        self.copy(index, ref, ref, way).wait_recv()

    def drain(self):
        for copy in self.started:
            copy.wait_send()


class Gather(Mover):
    def __init__(self, place, shard, whole, lane, width, order, send, recv, base, local, last=4):
        super().__init__(place, send, recv, base)
        self.last = last
        self.shard, self.whole, self.local = shard, whole, local
        self.lane, self.width, self.order = lane, width, order

    def view(self, zh, zl, y, c, x):
        half = self.whole.shape[-1] // 2
        lanes = pl.ds(pl.multiple_of(x * half + self.lane, 128), self.width)
        return self.whole.at[zh, zl, y, c, :, lanes]

    def steps(self, c):
        p, every = self.place, slice(None)
        yield "zh", [self.view(p.zh, p.zl, p.y, c, p.x)], [self.view(1 - p.zh, p.zl, p.y, c, p.x)]
        yield "zl", [self.view(every, p.zl, p.y, c, p.x)], [self.view(every, 1 - p.zl, p.y, c, p.x)]
        if self.order == "yx":
            yield "y", [self.view(every, every, p.y, c, p.x)], [self.view(every, every, 1 - p.y, c, p.x)]
            yield "x", [self.view(every, every, every, c, p.x)], [self.view(every, every, every, c, 1 - p.x)]
        else:
            yield "x", [self.view(every, every, p.y, c, p.x)], [self.view(every, every, p.y, c, 1 - p.x)]
            yield (
                "y",
                [self.view(every, every, p.y, c, x) for x in (0, 1)],
                [self.view(every, every, 1 - p.y, c, x) for x in (0, 1)],
            )

    def run(self, stage):
        p = self.place
        here = self.view(p.zh, p.zl, p.y, p.c, p.x)
        if stage == 0:
            self.mine, self.other = list(self.steps(p.c)), list(self.steps(1 - p.c))
            self.push(0, self.shard, here, "zh")
            self.push(5, self.shard, here, "c")
            self.own = pltpu.make_async_copy(self.shard, here, self.local)
            self.own.start()
        elif stage <= self.last:
            way, _, landed = self.mine[stage - 1]
            for i, ref in enumerate(landed):
                self.arrive(stage - 1 + i, ref, way)
            if stage == 1:
                self.own.wait()
            if stage < self.last:
                way, outgoing, _ = self.mine[stage]
                for i, ref in enumerate(outgoing):
                    self.push(stage + i, ref, ref, way)
            for i, ref in enumerate(landed):
                self.push(5 + stage + i, ref, ref, "c")
        elif stage == self.last + 1:
            self.arrive(5, self.view(p.zh, p.zl, p.y, 1 - p.c, p.x), "c")
            for k in range(self.last):
                for i, ref in enumerate(self.other[k][2]):
                    self.arrive(6 + k + i, ref, "c")
            self.drain()


class GatherEnd(Gather):
    def __init__(self, place, early, whole, lane, width, order, send, recv, base, local):
        Mover.__init__(self, place, send, recv, base)
        self.early, self.whole, self.local = early, whole, local
        self.lane, self.width, self.order = lane, width, order

    def halves_of(self, c):
        p, every = self.place, slice(None)
        if self.order == "yx":
            return "x", [(every, every, every, c, p.x)], [(every, every, every, c, 1 - p.x)]
        return (
            "y",
            [(every, every, p.y, c, x) for x in (0, 1)],
            [(every, every, 1 - p.y, c, x) for x in (0, 1)],
        )

    def old(self, spot):
        now, self.whole = self.whole, self.early
        ref = self.view(*spot)
        self.whole = now
        return ref

    def run(self, stage):
        p, every = self.place, slice(None)
        way, sent, landed = self.halves_of(p.c)
        if stage == 0:
            for i, spot in enumerate(sent):
                self.push(i, self.old(spot), self.view(*spot), way)
            self.loads = []
            if self.order == "yx":
                spots = [(every, every, every, every, p.x)]
            else:
                spots = [(every, every, p.y, every, x) for x in (0, 1)]
            for i, spot in enumerate(spots):
                load = pltpu.make_async_copy(self.old(spot), self.view(*spot), self.local.at[i])
                load.start()
                self.loads.append(load)
        elif stage == 1:
            for i, spot in enumerate(landed):
                self.arrive(i, self.view(*spot), way)
                self.push(2 + i, self.view(*spot), self.view(*spot), "c")
        else:
            for i, spot in enumerate(self.halves_of(1 - p.c)[2]):
                self.arrive(2 + i, self.view(*spot), "c")
            for load in self.loads:
                load.wait()
            self.drain()


class Scatter(Mover):
    def __init__(self, place, full, lane, width, order, out, bufs, send, recv, base, local):
        super().__init__(place, send, recv, base)
        self.full, self.lane, self.width, self.order = full, lane, width, order
        self.out, self.local = out, local
        self.sums, self.in_c, self.in_1, self.in_2, self.in_l, self.in_h = bufs

    def lanes(self, x):
        half = self.full.shape[-1] // 2
        return pl.ds(x * half + self.lane, self.width)

    def add(self, target, landed):
        lead = landed.shape[:-2]
        total = 1
        for n in lead:
            total *= n
        flat_dims = lead

        def one(i, carry):
            index = []
            for n in reversed(flat_dims):
                index.append(i % n)
                i = i // n
            index = tuple(reversed(index))
            target[index] = target[index] + landed[index]
            return carry

        if total == 1:
            one(0, 0)
        else:
            lax.fori_loop(0, total, one, 0)

    def run(self, stage):
        p, every = self.place, slice(None)
        if stage == 0:
            self.loads = []
            for x in (0, 1):
                self.push(x, self.full.at[:, :, :, 1 - p.c, :, self.lanes(x)], self.in_c.at[x], "c")
                load = pltpu.make_async_copy(
                    self.full.at[:, :, :, p.c, :, self.lanes(x)], self.sums.at[x], self.local.at[x]
                )
                load.start()
                self.loads.append(load)
            return
        if stage == 1:
            for x in (0, 1):
                self.arrive(x, self.in_c.at[x], "c")
                self.loads[x].wait()
            self.add(self.sums, self.in_c)
            if self.order == "xy":
                self.push(2, self.sums.at[1 - p.x], self.in_1.at[...], "x")
            else:
                for x in (0, 1):
                    self.push(2 + x, self.sums.at[x, :, :, 1 - p.y], self.in_1.at[x], "y")
        elif stage == 2:
            if self.order == "xy":
                self.arrive(2, self.in_1, "x")
                self.add(self.sums.at[p.x], self.in_1)
                self.push(4, self.sums.at[p.x, :, :, 1 - p.y], self.in_2, "y")
            else:
                for x in (0, 1):
                    self.arrive(2 + x, self.in_1.at[x], "y")
                    self.add(self.sums.at[x, :, :, p.y], self.in_1.at[x])
                self.push(4, self.sums.at[1 - p.x, :, :, p.y], self.in_2, "x")
        elif stage == 3:
            self.arrive(4, self.in_2, "y" if self.order == "xy" else "x")
            self.add(self.sums.at[p.x, :, :, p.y], self.in_2)
            self.push(5, self.sums.at[p.x, :, 1 - p.zl, p.y], self.in_l, "zl")
        elif stage == 4:
            self.arrive(5, self.in_l, "zl")
            self.add(self.sums.at[p.x, :, p.zl, p.y], self.in_l)
            self.push(6, self.sums.at[p.x, 1 - p.zh, p.zl, p.y], self.in_h, "zh")
        else:
            self.arrive(6, self.in_h, "zh")
            self.store(
                self.sums[p.x, p.zh, p.zl, p.y].astype(F32) + self.in_h[...].astype(F32)
            )
            self.drain()

    def store(self, value):
        ref, first = self.out
        ref[:, first : first + self.width] = value


class ScatterStart(Scatter):
    def run(self, stage):
        if stage < 2:
            super().run(stage)
            return
        p = self.place
        for k in (0, 1):
            if self.order == "xy":
                if k == 0:
                    self.arrive(2, self.in_1, "x")
                here, index = self.sums, lambda a, b, k=k: (p.x, a, b, k)
                there = lambda a, b, k=k: (a, b, k)
            else:
                self.arrive(2 + k, self.in_1.at[k], "y")
                here, index = self.sums, lambda a, b, k=k: (k, a, b, p.y)
                there = lambda a, b, k=k: (k, a, b)
            for a in (0, 1):
                for b in (0, 1):
                    self.out[k, a, b] = here[index(a, b)] + self.in_1[there(a, b)]
        self.drain()


class ScatterEnd(Mover):
    def __init__(self, place, left, out, lane, order, bufs, send, recv, base):
        super().__init__(place, send, recv, base)
        self.left, self.out, self.lane = left, out, lane
        self.way = "y" if order == "xy" else "x"
        self.in_2, self.in_l, self.in_h, self.quarter, self.sums = bufs

    def run(self, stage):
        p = self.place
        mine = getattr(p, self.way)
        if stage == 0:
            self.push(0, self.left.at[1 - mine], self.in_2, self.way)
        elif stage == 1:
            self.arrive(0, self.in_2, self.way)
            for a in (0, 1):
                for b in (0, 1):
                    self.quarter[a, b] = self.left[mine, a, b] + self.in_2[a, b]
            self.push(1, self.quarter.at[:, 1 - p.zl], self.in_l, "zl")
        elif stage == 2:
            self.arrive(1, self.in_l, "zl")
            for a in (0, 1):
                self.sums[a] = self.quarter[a, p.zl] + self.in_l[a]
            self.push(2, self.sums.at[1 - p.zh], self.in_h, "zh")
        else:
            self.arrive(2, self.in_h, "zh")
            width = self.in_h.shape[-1]
            self.out[:, self.lane : self.lane + width] = (
                self.sums[p.zh].astype(F32) + self.in_h[...].astype(F32)
            )
            self.drain()


def end_scratch(rows, width):
    return [
        pltpu.VMEM((2, 2, rows, width), BF),
        pltpu.VMEM((2, rows, width), BF),
        pltpu.VMEM((rows, width), BF),
        pltpu.VMEM((2, 2, rows, width), BF),
        pltpu.VMEM((2, rows, width), BF),
    ]


def scatter_scratch(rows, width, order):
    first = (2, 2, 2) if order == "xy" else (2, 2, 2)
    return [
        pltpu.VMEM((2, 2, 2, 2, rows, width), BF),
        pltpu.VMEM((2, 2, 2, 2, rows, width), BF),
        pltpu.VMEM(first + (rows, width), BF),
        pltpu.VMEM((2, 2, rows, width), BF),
        pltpu.VMEM((2, rows, width), BF),
        pltpu.VMEM((rows, width), BF),
    ]


class Total(Mover):
    def __init__(self, place, block, out, sums, landed, send, recv, base, features):
        super().__init__(place, send, recv, base)
        self.features = features
        self.block, self.out, self.sums, self.landed = block, out, sums, landed

    def run(self, stage):
        if stage > 0:
            self.arrive(stage - 1, self.landed.at[stage - 1], WAYS[stage - 1])
            self.sums[stage] = self.sums[stage - 1] + self.landed[stage - 1]
        if stage < 5:
            self.push(stage, self.sums.at[stage], self.landed.at[stage], WAYS[stage])
        else:
            final = self.sums[5]
            self.out[...] = final
            squares = final[STATS : STATS + 1, :]
            self.out[STATS + 1 : STATS + 2, :] = jnp.sqrt(squares / (squares[:, 3:4] * self.features))
            self.drain()


GATHERS = (
    (0, 0, 384, "yx", 0, 0), (0, 384, 384, "xy", 1, 0), (1, 0, 128, "yx", 3, 0),
    (0, 768, 256, "yx", 2, 0), (0, 1024, 128, "xy", 2, 256),
    (3, 0, 384, "yx", 5, 0), (3, 384, 384, "xy", 5, 384),
    (3, 768, 384, "yx", 5, 768), (3, 1152, 384, "xy", 5, 1152),
    (2, 0, 256, "yx", 4, 0), (2, 256, 128, "xy", 4, 256),
    (4, 0, 768, "yx", 6, 0), (4, 768, 768, "xy", 6, 768),
)
GATHER_WAVES = "qqqvvaabbbbdd"
GATHER_LAST = (4,) * 11 + (3, 3)
GATHER_AT = {
    "start": (("q", 0), ("q", 1), ("q", 2), ("v", 0), ("q", 3), ("v", 1), ("a", 0), ("v", 2),
              ("a", 1), ("q", 4), ("b", 0), ("q", 5), ("a", 2)),
    "load": (("v", 3), ("a", 3), ("b", 1), ("d", 0)),
    "newton1": (("v", 4), ("b", 2)),
    "third2": (("v", 5), ("a", 4), ("d", 1)),
    "first1": (("b", 3),),
    "first2": (("a", 5),),
    "mix0": (("d", 2),),
    "end": (("b", 4), ("d", 3), ("b", 5), ("d", 4)),
}
DOWN_GATHERS = GATHERS[-2:]
DOWN_SCATTERS = ((0, 0, 768, "xy"), (0, 768, 768, "yx"))
SCATTERS = (
    (1, 0, 768, "xy", 1, 0), (1, 768, 768, "yx", 1, 768),
    (0, 0, 256, "xy", 0, 0), (0, 256, 128, "yx", 0, 256),
    (2, 768, 256, "xy", 4, 0), (2, 1024, 128, "yx", 4, 256),
    (2, 0, 256, "yx", 2, 0), (2, 256, 128, "xy", 2, 256),
    (2, 384, 256, "xy", 3, 0), (2, 640, 128, "yx", 3, 256),
)
SCATTER_WAVES = "aaaavvqqkk"
SCATTER_AT = {
    "start": (("a", 0), ("d", 0)),
    "second0": (("d", 1), ("a", 1)),
    "second1": (("d", 2),),
    "second2": (("t", 0), ("d", 3)),
    "values": (("v", 0), ("t", 1)),
    "newton0": (("t", 2),),
    "newton1": (("t", 3),),
    "newton2": (("a", 2), ("v", 1), ("t", 4)),
    "third1": (("t", 5),),
    "queries": (("q", 0), ("a", 3)),
    "keys": (("k", 0), ("q", 1), ("v", 2)),
    "input0": (("k", 1), ("v", 3), ("q", 2), ("a", 4)),
    "input1": (("k", 2), ("v", 4), ("q", 3), ("k", 3)),
    "end": (("v", 5), ("q", 4), ("k", 4), ("a", 5), ("q", 5), ("k", 5)),
}


def gather_parts(place, cuts, shards, wholes, send, recv, local):
    parts = []
    for n, (i, lane, width, order, source, first) in enumerate(cuts):
        shard = shards[source].at[:, pl.ds(first, width)]
        parts.append(Gather(place, shard, wholes[i], lane, width, order, send, recv, COPIES * n,
                            local.at[n], GATHER_LAST[n]))
    return parts


def gather_scratch(cuts):
    n = len(cuts)
    return [
        pltpu.SemaphoreType.DMA((COPIES * n,)),
        pltpu.SemaphoreType.DMA((COPIES * n,)),
        pltpu.SemaphoreType.DMA((n,)),
    ]


def gather_shapes(rows, wide, units):
    whole = (2, 2, 2, 2)
    return (
        jax.ShapeDtypeStruct(whole + (rows, 3 * wide), BF),
        jax.ShapeDtypeStruct(whole + (BLOCK, 256), F32),
        jax.ShapeDtypeStruct(whole + (rows, wide), BF),
        jax.ShapeDtypeStruct(whole + (rows, units), BF),
        jax.ShapeDtypeStruct(whole + (rows, units), BF),
    )


SUM_COPIES = 7


def scatter_parts(place, cuts, fulls, outs, refs):
    send, recv, local = refs[-3:]
    return [
        Scatter(place, fulls[i], lane, width, order, (outs[n_out], first),
                refs[6 * n : 6 * n + 6], send, recv, SUM_COPIES * n, local.at[n])
        for n, (i, lane, width, order, n_out, first) in enumerate(cuts)
    ]


def all_scatter_scratch(cuts, rows, extra=0):
    out = []
    for _, _, width, order, *_ in cuts:
        out += scatter_scratch(rows, width, order)
    n = len(cuts)
    return out + [
        pltpu.SemaphoreType.DMA((SUM_COPIES * n + extra,)),
        pltpu.SemaphoreType.DMA((SUM_COPIES * n + extra,)),
        pltpu.SemaphoreType.DMA((n, 2)),
    ]


def norm_parts(values):
    centre = values - jnp.mean(values, axis=-1, keepdims=True)
    spread_of = jnp.mean(centre * centre, axis=-1, keepdims=True)
    inverse = lax.rsqrt(spread_of + 1e-05)
    return centre * inverse, inverse


def norm_grad(grad, gain, normal, inverse):
    scaled = grad * gain
    lean = jnp.mean(scaled, axis=-1, keepdims=True)
    along = jnp.mean(scaled * normal, axis=-1, keepdims=True)
    return inverse * (scaled - lean - normal * along)


TURNS = 12


def mid_kernel(slot, wide, *refs):
    (len_ref, ctx_ref, x_ref, far_cot, outw_ref, far_inw, partial_ref, gain_ref,
     dctx_ref, res_ref, far_out, far_gin, gout_ref, left_a, left_b, ends_ref,
     downw_ref, hid_ref, turn_ref, act_ref, slope_ref, acc_ref, dlow_ref, gdown_ref, sum_ref) = refs[:25]
    cot_ref, inw_ref, out_ref, gin_ref, copies = refs[25:30]
    get_inw = pltpu.make_async_copy(far_inw, inw_ref, copies.at[0])
    get_cot = pltpu.make_async_copy(far_cot, cot_ref, copies.at[1])
    put_out = pltpu.make_async_copy(out_ref, far_out, copies.at[2])
    put_gin = pltpu.make_async_copy(gin_ref, far_gin, copies.at[3])
    refs = refs[:24] + refs[30:]
    place = Place()
    greet(place)
    gsend, grecv, glocal = refs[-3 - 3 : -3]
    late = [
        GatherEnd(place, partial_ref, downw_ref, lane, width, order, gsend, grecv, 4 * n, glocal.at[n])
        for n, (_, lane, width, order, *_) in enumerate(DOWN_GATHERS)
    ]
    down = [
        ScatterStart(place, gdown_ref, lane, width, order, (left_a, left_b)[n],
                     refs[24 + 6 * n : 30 + 6 * n], refs[-3], refs[-2], SUM_COPIES * n, refs[-1].at[n])
        for n, (_, lane, width, order) in enumerate(DOWN_SCATTERS)
    ]

    def both(parts, stage):
        for part in parts:
            part.run(stage)

    both(late, 0)
    get_inw.start()
    get_cot.start()
    hidden_units = act_ref.shape[1]
    step = hidden_units // TURNS
    length = len_ref[lax.axis_index("tensor")]
    gain_one, bias_one = gain_ref[0:1, :], gain_ref[1:2, :]
    gain_two, bias_two = gain_ref[2:3, :], gain_ref[3:4, :]
    sum_ref[...] = jnp.zeros(sum_ref.shape, F32)

    def valid_of(i, rows):
        row = lax.broadcasted_iota(jnp.int32, (rows, 1), 0) + i * rows
        return (row < length).astype(F32)

    def span(i, rows):
        return pl.ds(pl.multiple_of(i * rows, rows), rows)

    def count(row, values):
        sum_ref[row : row + 1, :] += jnp.sum(values, axis=0, keepdims=True)

    def unit(i):
        return pl.ds(pl.multiple_of(i * step, 128), step)

    def weight(ref, lanes):
        return ref[:, :, :, :, :, lanes].reshape(wide, -1)

    def project(i, carry):
        rows = span(i, TALL)
        acc_ref[rows, :] = mm(ctx_ref[rows, :], outw_ref[...], NT)
        return carry

    lax.fori_loop(0, slot // TALL, project, 0)

    def norm_one(i, carry):
        rows = span(i, ROWS)
        valid = valid_of(i, ROWS)
        attn, x = acc_ref[rows, :], x_ref[rows, :].astype(F32)
        count(4, valid * x * x)
        count(5, valid * attn * attn)
        total = x + attn
        res_ref[rows, :] = total
        normal, _ = norm_parts(total)
        hid_ref[rows, :] = (normal * gain_one + bias_one).astype(BF)
        return carry

    lax.fori_loop(0, slot // ROWS, norm_one, 0)

    def expand(i, carry):
        lanes = unit(i)
        for block in range(slot // TALL):
            rows = slice(block * TALL, (block + 1) * TALL)
            pre = mm(hid_ref[rows, :], inw_ref[:, lanes])
            below = 0.5 * (1.0 + lax.erf(pre * 0.5**0.5))
            act_ref[rows, lanes] = (pre * below).astype(BF)
            slope = below + pre * jnp.exp(-0.5 * pre * pre) * (2.0 * jnp.pi) ** -0.5
            slope_ref[rows, lanes] = slope.astype(BF)
        return carry

    get_inw.wait()
    lax.fori_loop(0, TURNS, expand, 0)
    both(late, 1)
    both(late, 2)

    def contract(i, carry):
        rows = span(i, 512)
        acc_ref[rows, :] = mm(act_ref[rows, :], weight(downw_ref, slice(None)), NT)
        return carry

    lax.fori_loop(0, slot // 512, contract, 0)

    def norm_two(i, carry):
        rows = span(i, ROWS)
        valid = valid_of(i, ROWS)
        ffn = acc_ref[rows, :]
        count(6, valid * ffn * ffn)
        normal, inverse = norm_parts(hid_ref[rows, :].astype(F32) + ffn)
        out_ref[rows, :] = (normal * gain_two + bias_two).astype(BF)
        grad = cot_ref[rows, :].astype(F32) * valid
        count(2, grad * normal)
        count(3, grad)
        back = norm_grad(grad, gain_two, normal, inverse)
        acc_ref[rows, :] = back
        dlow_ref[rows, :] = back.astype(BF)
        return carry

    get_cot.wait()
    lax.fori_loop(0, slot // ROWS, norm_two, 0)
    put_out.start()
    turn_ref[...] = jnp.transpose(dlow_ref[...])

    def down_grad(i, carry):
        each = TURNS // 4
        block = i // TURNS
        i = (i % TURNS) // each * 2 * each + i % each + block * each
        lanes = unit(i)
        value = mm(turn_ref[...], act_ref[:, lanes]).astype(BF)
        gdown_ref[:, :, :, :, :, lanes] = value.reshape(gdown_ref.shape[:-1] + (step,))
        return carry

    lax.fori_loop(0, TURNS // 2, down_grad, 0)
    down[0].run(0)
    lax.fori_loop(TURNS, TURNS + TURNS // 2, down_grad, 0)
    down[1].run(0)
    turn_ref[...] = jnp.transpose(hid_ref[...])

    def back_grad(i, carry):
        lanes = unit(i)
        weights = weight(downw_ref, lanes)
        for block in range(slot // TALL):
            rows = slice(block * TALL, (block + 1) * TALL)
            pre = mm(dlow_ref[rows, :], weights) * slope_ref[rows, lanes].astype(F32)
            slope_ref[rows, lanes] = pre.astype(BF)
        gin_ref[:, lanes] = mm(turn_ref[...], slope_ref[:, lanes]).astype(BF)
        return carry

    lax.fori_loop(0, TURNS // 4, back_grad, 0)
    down[0].run(1)
    lax.fori_loop(TURNS // 4, TURNS // 2, back_grad, 0)
    down[1].run(1)
    lax.fori_loop(TURNS // 2, TURNS, back_grad, 0)
    put_gin.start()

    def narrow(i, carry):
        rows = span(i, 512)
        acc_ref[rows, :] += mm(slope_ref[rows, :], inw_ref[...], NT)
        return carry

    lax.fori_loop(0, slot // 512, narrow, 0)

    def norm_one_back(i, carry):
        rows = span(i, ROWS)
        grad = acc_ref[rows, :]
        normal, inverse = norm_parts(res_ref[rows, :])
        count(0, grad * normal)
        count(1, grad)
        back = norm_grad(grad, gain_one, normal, inverse)
        res_ref[rows, :] = back
        dlow_ref[rows, :] = back.astype(BF)
        return carry

    lax.fori_loop(0, slot // ROWS, norm_one_back, 0)
    turn_ref[...] = jnp.transpose(dlow_ref[...])

    def out_grad(i, carry):
        rows = span(i, TALL)
        gout_ref[rows, :] = mm(turn_ref[rows, :], ctx_ref[...]).astype(BF)
        return carry

    lax.fori_loop(0, wide // TALL, out_grad, 0)

    def reach(i, carry):
        rows = span(i, TALL)
        dctx_ref[rows, :] = mm(dlow_ref[rows, :], outw_ref[...]).astype(BF)
        return carry

    lax.fori_loop(0, slot // TALL, reach, 0)
    ends_ref[...] = jnp.zeros(ends_ref.shape, F32)
    tiles = wide // 128
    for n in range(4):
        for tile in range(tiles):
            ends_ref[n * tiles + tile : n * tiles + tile + 1, :] = sum_ref[n : n + 1, tile * 128 : (tile + 1) * 128]
    lane = lax.broadcasted_iota(jnp.int32, (1, 128), 1)
    line = jnp.where(lane == 3, jnp.minimum(length, slot).astype(F32), 0.0)
    for n in range(3):
        line = jnp.where(lane == n, jnp.sum(sum_ref[4 + n : 5 + n, :], axis=1, keepdims=True), line)
    ends_ref[STATS : STATS + 1, :] = line
    both(down, 2)
    put_out.wait()
    put_gin.wait()


def mid_call(length, ctx, x, cot, outw, inw, part, gains):
    slot, wide = x.shape
    units = inw.shape[1]
    rows = part.shape[-2]
    shape = jax.ShapeDtypeStruct
    whole = (2, 2, 2, 2, rows, units)
    n = len(DOWN_GATHERS)
    return pl.pallas_call(
        partial(mid_kernel, slot, wide),
        out_shape=(
            shape((slot, wide), BF),
            shape((slot, wide), F32),
            shape((slot, wide), BF),
            shape((wide, units), BF),
            shape((wide, wide), BF),
            shape((2, 2, 2, rows, units // 4), BF),
            shape((2, 2, 2, rows, units // 4), BF),
            shape((40, 128), F32),
        ),
        in_specs=[SM, VM, VM, ANY, VM, ANY, ANY, VM],
        out_specs=[VM, VM, ANY, ANY, VM, VM, VM, VM],
        scratch_shapes=[
            pltpu.VMEM(whole, BF),
            pltpu.VMEM((slot, wide), BF),
            pltpu.VMEM((wide, slot), BF),
            pltpu.VMEM((slot, units), BF),
            pltpu.VMEM((slot, units), BF),
            pltpu.VMEM((slot, wide), F32),
            pltpu.VMEM((slot, wide), BF),
            pltpu.VMEM(whole, BF),
            pltpu.VMEM((8, wide), F32),
            pltpu.VMEM((slot, wide), BF),
            pltpu.VMEM(inw.shape, BF),
            pltpu.VMEM((slot, wide), BF),
            pltpu.VMEM((wide, units), BF),
            pltpu.SemaphoreType.DMA((4,)),
        ]
        + all_scatter_scratch(DOWN_SCATTERS, rows)[:-3]
        + [
            pltpu.SemaphoreType.DMA((4 * n,)),
            pltpu.SemaphoreType.DMA((4 * n,)),
            pltpu.SemaphoreType.DMA((n, 2)),
        ]
        + all_scatter_scratch(DOWN_SCATTERS, rows)[-3:],
        compiler_params=pltpu.CompilerParams(
            vmem_limit_bytes=67043328, collective_id=4, has_side_effects=True
        ),
        name="middle",
    )(length, ctx, x, cot, outw, inw, part, gains)


D = 768
BOTH = ("tensor", "dp")


def rows_sum(left_op, right_op):
    return lax.dot_general(left_op, right_op, (TN, ((), ())), preferred_element_type=F32)


def cols_sum(left_op, right_op):
    return lax.dot_general(left_op, right_op, (NT, ((), ())), preferred_element_type=F32)


def dense(left_op, right_op):
    return jnp.dot(left_op, right_op, preferred_element_type=F32)


def norm_back(grad, gain, normal, inverse):
    return (
        norm_grad(grad, gain, normal, inverse),
        jnp.sum(grad * normal, axis=0),
        jnp.sum(grad, axis=0),
    )


def gather_plain(pieces):
    sizes = lax.axis_size("tensor"), lax.axis_size("dp")
    out = []
    for piece in pieces:
        joined = lax.all_gather(piece, BOTH, axis=0, tiled=True)
        joined = joined.reshape(sizes[0], sizes[1] * piece.shape[0], piece.shape[1])
        out.append(joined.transpose(1, 0, 2).reshape(joined.shape[1], -1))
    return out


def scatter_plain(fulls):
    parts = lax.axis_size("tensor")
    out = []
    for full in fulls:
        stacked = full.reshape(full.shape[0], parts, -1).transpose(1, 0, 2).reshape(-1, full.shape[1] // parts)
        out.append(lax.psum_scatter(stacked, BOTH, scatter_dimension=0, tiled=True).astype(F32))
    return out


def per_device(own, x_in, lengths, cotangent, w_query, w_key, w_value, w_out, w_in, w_down,
               conv_weight, ln1_gain, ln1_bias, ln2_gain, ln2_bias):
    tensor_index = lax.axis_index("tensor")
    slot = x_in.shape[0]
    parts = lax.axis_size("tensor")
    length = lengths

    later = (w_out.T, w_in, w_down.T)
    few, own_heads, count = ln1_gain.shape[0], conv_weight.shape[0], conv_weight.shape[1]

    def rows_of(array, rows):
        return jnp.pad(array, ((0, rows - array.shape[0]), (0, 128 - array.shape[1])))

    vectors = jnp.stack([ln1_gain, ln1_bias, ln2_gain, ln2_bias])
    block = jnp.concatenate(
        [rows_of(vectors, TAPS_AT), rows_of(conv_weight, FLIP_AT - TAPS_AT),
         rows_of(conv_weight[:, ::-1], BLOCK - FLIP_AT)],
        axis=0,
    )
    if own:
        wholes, saved = attn_fwd(
            length, x_in, parts, own, (w_query, w_key, w_value, block) + later
        )
        qkv_w, blocks, out_w, in_w = (w.reshape(-1, w.shape[-1]) for w in wholes[:4])
        taps = blocks
        blocks = blocks.reshape(lax.axis_size("dp"), BLOCK, parts, 128)
    else:
        qkv_w, out_w, in_w, down_w = gather_plain(
            (jnp.concatenate([w_query, w_key, w_value], axis=1),) + later
        )
        blocks = lax.all_gather(block, ("dp", "tensor"), axis=0)
        blocks = blocks.reshape(-1, parts, BLOCK, 128).transpose(0, 2, 1, 3)
        taps = blocks[0].reshape(BLOCK, parts * 128)
        _, saved = attn_fwd(length, x_in, parts, own, (qkv_w, taps))
    gains = blocks[:, :4, :, :few].transpose(1, 0, 2, 3).reshape(4, D)
    gain_one, bias_one, gain_two, bias_two = gains[0], gains[1], gains[2], gains[3]
    ctx, saved = saved[0], saved[1:]

    if own:
        d_ctx, d_res1, output, grad_in, grad_out, *left, ends = mid_call(
            length, ctx, x_in, cotangent, out_w, in_w, wholes[4], jnp.pad(gains, ((0, 4), (0, 0)))
        )
        fulls = [grad_out, grad_in]
    else:
        left = ()
        tokens = x_in.astype(F32)
        mine = lax.dynamic_slice_in_dim(lengths, tensor_index, 1)
        valid = (jnp.arange(slot, dtype=jnp.int32) < mine[0]).astype(F32)[:, None]
        attn_branch = cols_sum(ctx, out_w)
        normal_one, inverse_one = norm_parts(tokens + attn_branch)
        hidden = (normal_one * gain_one + bias_one).astype(BF)
        pre = dense(hidden, in_w)
        below = 0.5 * (1.0 + lax.erf(pre * 0.5**0.5))
        act = (pre * below).astype(BF)
        slope = (below + pre * jnp.exp(-0.5 * pre * pre) * (2.0 * jnp.pi) ** -0.5).astype(BF)
        ffn_branch = cols_sum(act, down_w)
        normal_two, inverse_two = norm_parts(hidden.astype(F32) + ffn_branch)
        output = (normal_two * gain_two + bias_two).astype(BF)
        grad_result = cotangent.astype(F32) * valid
        d_res2, grad_gain_two, grad_bias_two = norm_back(grad_result, gain_two, normal_two, inverse_two)
        d_ffn = d_res2.astype(BF)
        grad_down = rows_sum(d_ffn, act)
        d_pre = (dense(d_ffn, down_w) * slope.astype(F32)).astype(BF)
        grad_in = rows_sum(hidden, d_pre)
        d_hidden = cols_sum(d_pre, in_w) + d_res2
        d_res1, grad_gain_one, grad_bias_one = norm_back(d_hidden, gain_one, normal_one, inverse_one)
        d_attn = d_res1.astype(BF)
        grad_out = rows_sum(d_attn, ctx)
        d_ctx = dense(d_attn, out_w).astype(BF)
        fulls = [grad_out.astype(BF), grad_in.astype(BF), grad_down.astype(BF)]

        def total(branch):
            return jnp.sum(valid * branch * branch)

        sums = jnp.stack([total(tokens), total(attn_branch), total(ffn_branch), jnp.sum(valid)])
        ends = jnp.concatenate(
            [
                jnp.stack([grad_gain_one, grad_bias_one, grad_gain_two, grad_bias_two]).reshape(24, 128),
                jnp.zeros((12, 128), F32),
                jnp.pad(sums[None], ((0, 3), (0, 124))),
            ],
            axis=0,
        )
    grads = attn_bwd(length, d_ctx, saved, taps, x_in.T, qkv_w, d_res1, ends, parts, own, fulls, left)
    input_grad, summed = grads[-2:]
    if own:
        weight_grads = (*grads[2:5], grads[0].T, grads[1], grads[5].T)
        stats = summed[STATS + 1, :3]
    else:
        early, (late,) = scatter_plain(fulls), scatter_plain([grads[0]])
        width = late.shape[1] // 3
        weight_grads = (
            late[:, :width], late[:, width : 2 * width], late[:, 2 * width :],
            early[0].T, early[1], early[2].T,
        )
        summed = lax.psum(summed, ("dp", "tensor"))
        stats = jnp.sqrt(summed[STATS, :3] / (summed[STATS, 3] * D))
    share = D // lax.axis_size(("dp", "tensor"))
    start_at = lax.axis_index(("dp", "tensor")) * share
    vectors = lax.dynamic_slice_in_dim(summed[:24].reshape(4, D), start_at, share, 1)
    conv_grad = lax.dynamic_slice_in_dim(summed, 24 + tensor_index * own_heads, own_heads, 0)[:, :count]
    return (
        output, input_grad, *weight_grads,
        conv_grad, vectors[0], vectors[1], vectors[2], vectors[3], stats,
    )


def solution(mesh):
    own = mesh.shape["dp"] == 16 and mesh.shape["tensor"] == 2
    rows, both = P(("dp", "tensor"), None), P(("dp", "tensor"))
    split, crossed = P("dp", "tensor"), P("tensor", "dp")
    return jax.shard_map(
        partial(per_device, own),
        mesh=mesh,
        in_specs=(rows, P("dp"), rows, split, split, split, crossed, split, crossed,
                  P("tensor", None), both, both, both, both),
        out_specs=(rows, rows, split, split, split, crossed, split, crossed,
                   P("tensor", None), both, both, both, both, P()),
        check_vma=False,
    )
```

```python
from functools import partial

import jax
import jax.numpy as jnp
from jax import lax
from jax.experimental import pallas as pl
from jax.experimental.pallas import tpu as pltpu
from jax.sharding import PartitionSpec as P

ANY = pl.BlockSpec(memory_space=pl.ANY)
F32, BF = jnp.float32, jnp.bfloat16
NN, NT, TN = ((1,), (0,)), ((1,), (1,)), ((0,), (0,))
MARKS = 64
HEAD = 64
PACK = 4
WIDE = PACK * HEAD
TAPS = 33
EDGE = TAPS // 2
ROWS = 128
TALL = 256
TAPS_AT, FLIP_AT, BLOCK = 8, 16, 24
STATS = 36
WINDOW = ROWS + 2 * EDGE
STEPS = 6
KEPT = 4


def mm(a, b, dims=NN):
    return lax.dot_general(a, b, (dims, ((), ())), preferred_element_type=F32)


def halves(a):
    high = a.astype(BF)
    return high, (a - high.astype(F32)).astype(BF)


def mm3(a, b, dims=NN):
    (ah, al), (bh, bl) = a, b
    return mm(ah, bh, dims) + (mm(ah, bl, dims) + mm(al, bh, dims))


def mm3f(a, b, dims=NN):
    return mm3(halves(a), halves(b), dims)


def grid_of(shape):
    return (
        lax.broadcasted_iota(jnp.int32, shape, 0),
        lax.broadcasted_iota(jnp.int32, shape, 1),
    )


def block_mask():
    row, col = grid_of((WIDE, WIDE))
    return row // HEAD == col // HEAD


def eye():
    row, col = grid_of((WIDE, WIDE))
    return (row == col).astype(F32)


def spread(packed, mask):
    full = jnp.concatenate([packed] * PACK, axis=0)
    return jnp.where(mask, full, jnp.zeros_like(full))


def gather_up(full):
    return sum(full[i * MARKS : (i + 1) * MARKS] for i in range(PACK))


def segment_reduce(a, fill, op):
    lane = lax.broadcasted_iota(jnp.int32, (a.shape[0], 128), 1) < HEAD
    parts = []
    for tile in range(a.shape[1] // 128):
        piece = a[:, tile * 128 : (tile + 1) * 128]
        low = op(jnp.where(lane, piece, fill), axis=1, keepdims=True)
        high = op(jnp.where(lane, fill, piece), axis=1, keepdims=True)
        parts.append(jnp.where(lane, low, high))
    return jnp.concatenate(parts, axis=1)


def average_matrix():
    row, col = grid_of((TALL // 16, TALL))
    return jnp.where(row == col // 16, 1.0 / 16, 0.0).astype(BF)


def average_back():
    row, col = grid_of((ROWS, ROWS // 16))
    return jnp.where(row // 16 == col, 1.0 / 16, 0.0).astype(BF)


def lanes_of(group):
    return slice(group * WIDE, (group + 1) * WIDE)


def put(ref, rows, which, wide, parts, start, value):
    share = wide // parts
    for tile in range(0, value.shape[1], 128):
        lane = start + tile
        at = (3 * (lane // share) + which) * share + lane % share
        ref[rows, at : at + 128] = value[:, tile : tile + 128]


def lhs(a):
    return jnp.concatenate(halves(a), axis=1)


def rhs(b):
    high, low = halves(b)
    return jnp.concatenate(
        [
            jnp.concatenate([high, low], axis=1),
            jnp.concatenate([high, jnp.zeros_like(high)], axis=1),
        ],
        axis=0,
    )


def pair_mm(left, right):
    out = mm(left, right)
    return out[:, :128] + out[:, 128:]


def fold(full):
    return full[:MARKS] + full[MARKS:]


def unfold(packed, mask):
    full = jnp.concatenate([packed, packed], axis=0)
    return jnp.where(mask, full, 0.0)


def pair_lanes(pair):
    return slice(pair * 128, (pair + 1) * 128)


def pair_consts():
    row, col = grid_of((128, 128))
    return row // HEAD == col // HEAD, (row == col).astype(F32)


def toeplitz(taps_ref, first, own_heads, group):
    parts = []
    for i in range(PACK):
        half, head = divmod(group * PACK + i, own_heads)
        line = taps_ref[first + head : first + head + 1, half * 128 : (half + 1) * 128]
        line = jnp.concatenate([line, jnp.zeros_like(line)], axis=1)
        line = jnp.broadcast_to(line, (ROWS, 256))
        parts.append(pltpu.roll(line, 0, 1, stride=1, stride_axis=0)[:, :WINDOW])
    return jnp.concatenate(parts, axis=0).astype(BF)


def diagonal_lanes(stacked):
    col = lax.broadcasted_iota(jnp.int32, (ROWS, WIDE), 1) // HEAD
    out = stacked[:ROWS]
    for i in range(1, PACK):
        out = jnp.where(col == i, stacked[i * ROWS : (i + 1) * ROWS], out)
    return out


def attn_fwd_kernel(slot, groups, parts, own, *refs):
    len_ref, x_ref = refs[:2]
    if own:
        shards, outs, refs = refs[2:9], refs[9:14], refs[14:]
        weight, taps_ref = outs[0], outs[1].at[0, 0, 0, 0]
    else:
        weight, taps_ref, refs = refs[2], refs[3], refs[4:]
    ctx_ref, *far, small_ref, far_chain = refs[:8]
    z_ref, k2_ref, s_ref, top_ref, t_ref = refs[8:13]
    near = refs[13:19]
    qh_ref, kh_ref, vp_ref, k1_ref, k3_ref, chain_ref = near
    leave = {
        name: pltpu.make_async_copy(here, there, refs[19].at[n])
        for n, (name, here, there) in enumerate(
            zip(("qh", "kh", "vp", "k1", "k3", "chain"), near, (*far, far_chain))
        )
    }
    refs = refs[:13] + refs[20:]
    moves = []
    if own:
        place = Place()
        greet(place)
        moves = gather_parts(place, GATHERS, shards, outs, *refs[13:])

    def advance(name):
        for which, stage in GATHER_AT.get(name, ()) if own else ():
            for part, wave in zip(moves, GATHER_WAVES):
                if wave == which:
                    part.run(stage)

    advance("start")
    count = slot // ROWS
    scale = HEAD ** -0.25
    length = len_ref[lax.axis_index("tensor")] if len_ref.shape[0] > 1 else len_ref[0]
    avg = average_matrix()
    wide = groups * WIDE
    share = wide // parts
    own_heads = share // HEAD
    vp_ref[0:EDGE, :] = jnp.zeros((EDGE, wide), BF)
    vp_ref[slot + EDGE : slot + 2 * EDGE, :] = jnp.zeros((EDGE, wide), BF)

    def columns(start, width):
        if own:
            return weight[:, :, :, :, :, start : start + width].reshape(-1, width)
        return weight[:, start : start + width]

    def valid_of(i, rows):
        row = lax.broadcasted_iota(jnp.int32, (rows, 1), 0) + i * rows
        return (row < length).astype(F32)

    def load(i, carry):
        rows = pl.ds(pl.multiple_of(i * TALL, TALL), TALL)
        few = pl.ds(pl.multiple_of(i * (TALL // 16), TALL // 16), TALL // 16)
        factor = valid_of(i, TALL) * scale
        for p in range(parts):
            both = mm(x_ref[rows, :], columns(3 * p * share, 2 * share)) * factor
            at = slice(p * share, (p + 1) * share)
            high, low = halves(both)
            qh_ref[rows, at] = high[:, :share]
            kh_ref[rows, at] = high[:, share:]
            means = mm(avg, high) + mm(avg, low)
            small_ref[0, few, at] = means[:, :share]
            small_ref[1, few, at] = means[:, share:]
        return carry

    lax.fori_loop(0, slot // TALL, load, 0)
    leave["qh"].start()
    leave["kh"].start()
    advance("load")
    mask = block_mask()
    pmask, one = pair_consts()
    pairs = 2 * groups

    for j in range(pairs):
        at = pair_lanes(j)
        ql, kl = unfold(small_ref[0, :, at], pmask), unfold(small_ref[1, :, at], pmask)
        a2 = jnp.where(pmask, mm3f(ql, kl, NT), -1e30)
        e2 = jnp.where(pmask, jnp.exp(a2 - jnp.max(a2, axis=1, keepdims=True)), 0.0)
        k2 = e2 / jnp.sum(e2, axis=1, keepdims=True)
        top = segment_reduce(jnp.sum(k2, axis=0, keepdims=True), -1e30, jnp.max)
        k2_ref[j] = lhs(k2)
        small_ref[2, :, at] = fold(k2)
        z_ref[j] = jnp.transpose(k2) / top

    def newton(step, carry):
        every = range(pairs)
        z = [z_ref[j] for j in every]
        p = [pair_mm(k2_ref[j], rhs(z[j])) for j in every]
        left = [lhs(p[j]) for j in every]
        t2 = [15.0 * one - pair_mm(left[j], rhs(7.0 * one - p[j])) for j in every]
        t3 = [13.0 * one - pair_mm(left[j], rhs(t2[j])) for j in every]
        new = [0.25 * pair_mm(lhs(z[j]), rhs(t3[j])) for j in every]
        for j in every:
            for n, value in enumerate((z, p, t2, t3)):
                chain_ref[step, n, :, pair_lanes(j)] = fold(value[j])
            z_ref[j] = new[j]
        return carry

    lax.fori_loop(0, STEPS // 2, newton, 0)
    advance("newton0")
    lax.fori_loop(STEPS // 2, STEPS, newton, 0)
    leave["chain"].start()
    advance("newton1")

    for g in range(groups):
        at = lanes_of(g)
        ql = spread(small_ref[0, :, at], mask).astype(BF)
        top_ref[...] = jnp.full(top_ref.shape, -jnp.inf, F32)

        def scores(i, carry):
            rows = pl.ds(pl.multiple_of(i * ROWS, ROWS), ROWS)
            row = lax.broadcasted_iota(jnp.int32, (ROWS, 1), 0) + i * ROWS
            a3 = jnp.where(row < length, mm(kh_ref[rows, at], ql, NT), -1e9)
            s_ref[rows, :] = a3
            top_ref[0:1, :] = jnp.maximum(top_ref[0:1, :], jnp.max(a3, axis=0, keepdims=True))
            return carry

        lax.fori_loop(0, count, scores, 0)
        peak = top_ref[0:1, :]
        top_ref[0:1, :] = jnp.zeros((1, WIDE), F32)

        def powers(i, carry):
            rows = pl.ds(pl.multiple_of(i * ROWS, ROWS), ROWS)
            e3 = jnp.exp(s_ref[rows, :] - peak)
            s_ref[rows, :] = e3
            top_ref[0:1, :] += jnp.sum(e3, axis=0, keepdims=True)
            return carry

        lax.fori_loop(0, count, powers, 0)
        inverse = 1.0 / top_ref[0:1, :]

        def weigh(i, carry):
            rows = pl.ds(pl.multiple_of(i * ROWS, ROWS), ROWS)
            k3_ref[rows, at] = (s_ref[rows, :] * inverse).astype(BF)
            return carry

        lax.fori_loop(0, count, weigh, 0)
        advance(f"third{g}")

    leave["k3"].start()
    ones = mask.astype(F32).astype(BF)
    for g in range(groups):
        at = lanes_of(g)
        kl = spread(small_ref[1, :, at], mask).astype(BF)

        def first(i, carry):
            rows = pl.ds(pl.multiple_of(i * ROWS, ROWS), ROWS)
            a1 = mm(qh_ref[rows, at], kl, NT)
            e1 = jnp.exp(a1 - segment_reduce(a1, -jnp.inf, jnp.max)).astype(BF)
            k1_ref[rows, at] = (e1.astype(F32) / mm(e1, ones)).astype(BF)
            return carry

        lax.fori_loop(0, count, first, 0)
        advance(f"first{g}")

    leave["k1"].start()

    def load_values(i, carry):
        rows = pl.ds(pl.multiple_of(i * TALL + EDGE, EDGE), TALL)
        valid = valid_of(i, TALL)
        x = x_ref[pl.ds(pl.multiple_of(i * TALL, TALL), TALL), :]
        for p in range(parts):
            value = mm(x, columns((3 * p + 2) * share, share)) * valid
            vp_ref[rows, p * share : (p + 1) * share] = value.astype(BF)
        return carry

    lax.fori_loop(0, slot // TALL, load_values, 0)
    leave["vp"].start()

    for g in range(groups):
        at = lanes_of(g)
        b = mm(k3_ref[:, at], vp_ref[EDGE : slot + EDGE, at], TN)
        b = jnp.where(mask, b, 0.0)
        for sub in range(2):
            j, inner = 2 * g + sub, pair_lanes(sub)
            z, piece = z_ref[j], b[inner, inner]
            small_ref[3, :, pair_lanes(j)] = fold(piece)
            small_ref[4, :, pair_lanes(j)] = fold(mm3f(z, piece))
            small_ref[5, :, pair_lanes(j)] = fold(z)
        t_ref[...] = toeplitz(taps_ref, TAPS_AT, own_heads, g)
        cb = spread(small_ref[4, :, at], mask).astype(BF)

        def mix(i, carry):
            rows = pl.ds(pl.multiple_of(i * ROWS, ROWS), ROWS)
            window = vp_ref[pl.ds(pl.multiple_of(i * ROWS, ROWS), WINDOW), at]
            ctx_ref[rows, at] = (
                mm(k1_ref[rows, at], cb) + diagonal_lanes(mm(t_ref[...], window))
            ).astype(BF)
            return carry

        lax.fori_loop(0, count, mix, 0)
        advance(f"mix{g}")
    advance("end")
    for copy in leave.values():
        copy.wait()


def attn_bwd_kernel(slot, groups, parts, own, *refs):
    (len_ref, g_ref, qh_ref, kh_ref, vp_ref, k1_ref, k3_ref, small_ref, chain_ref, taps_ref,
     xt_ref, w_ref, dres_ref, block_ref) = refs[:14]
    if own:
        fulls, left_refs, refs = refs[14:16], refs[16:18], refs[18:]
        outs, down_out, refs = refs[:5], refs[5], refs[6:]
    else:
        outs, refs = (refs[14],), refs[15:]
    late_ref = {}
    for n, (name, ref) in enumerate(
        (("chain", chain_ref), ("xt", xt_ref), ("w", w_ref), ("dres", dres_ref))
    ):
        late_ref[name] = pltpu.make_async_copy(ref, refs[0 if name == "xt" else 2 + n], refs[6].at[n])
    chain_ref, xt_ref, w_ref, dres_ref = refs[2:6]
    dx_ref, sum_ref = refs[:2]
    refs = refs[:2] + refs[7:]
    (dqkv_ref, gp_ref, da1_ref, da3_ref, dk_ref, dz_ref, k2_ref,
     dql_ref, dkl_ref, t_ref, acc_ref) = refs[2:13]
    todo = {}
    wide_of = groups * WIDE
    if own:
        grad_ref, totals, landed = refs[13:16]
        place = Place()
        greet(place)
        scatters = scatter_parts(place, SCATTERS, fulls + (grad_ref,), outs, refs[26:])
        base = SUM_COPIES * len(SCATTERS)
        total = Total(place, totals.at[0], sum_ref, totals, landed, refs[-3], refs[-2], base, wide_of)
        tails = [
            ScatterEnd(place, left_refs[n], down_out, lane, order, refs[16 + 5 * n : 21 + 5 * n],
                       refs[-3], refs[-2], base + 5 + 3 * n)
            for n, (_, lane, _, order) in enumerate(DOWN_SCATTERS)
        ]
        todo = SCATTER_AT
    else:
        grad_ref = outs[0]
        totals = sum_ref

    def advance(name):
        for which, stage in todo.get(name, ()):
            if which == "t":
                total.run(stage)
            elif which == "d":
                for tail in tails:
                    tail.run(stage)
            else:
                for part, wave in zip(scatters, SCATTER_WAVES):
                    if wave == which:
                        part.run(stage)

    advance("start")
    for copy in late_ref.values():
        copy.start()
    count = slot // ROWS
    marks = ROWS // 16
    scale = HEAD ** -0.25
    length = len_ref[lax.axis_index("tensor")] if len_ref.shape[0] > 1 else len_ref[0]
    wide = groups * WIDE
    share = wide // parts
    own_heads = share // HEAD
    pairs = 2 * groups
    mask = block_mask()
    pmask, one = pair_consts()
    ones = mask.astype(F32).astype(BF)
    gp_ref[0:EDGE, :] = jnp.zeros((EDGE, wide), BF)
    gp_ref[slot + EDGE : slot + 2 * EDGE, :] = jnp.zeros((EDGE, wide), BF)
    gp_ref[EDGE : slot + EDGE, :] = g_ref[...]
    col = lax.broadcasted_iota(jnp.int32, (ROWS, WIDE), 1) // HEAD
    up, across = grid_of((ROWS, ROWS))
    flip = jnp.where(up + across == ROWS - 1, 1.0, 0.0).astype(BF)
    taps_lane = lax.broadcasted_iota(jnp.int32, (1, 128), 1) < TAPS

    def totals_row(row):
        return (0, slice(row, row + 1)) if own else slice(row, row + 1)

    if own:
        totals[0] = block_ref[...]
    else:
        sum_ref[...] = block_ref[...]

    for g in range(groups):
        at = lanes_of(g)
        cb = spread(small_ref[4, :, at], mask).astype(BF)

        def first(i, carry):
            rows = pl.ds(pl.multiple_of(i * ROWS, ROWS), ROWS)
            k1 = k1_ref[rows, at].astype(F32)
            dk1 = mm(g_ref[rows, at], cb, NT)
            high, low = halves(dk1 * k1)
            da1_ref[rows, at] = (k1 * (dk1 - (mm(high, ones) + mm(low, ones)))).astype(BF)
            return carry

        lax.fori_loop(0, count, first, 0)
        advance(f"first{g}")
        dc = jnp.where(mask, mm(k1_ref[:, at], g_ref[:, at], TN), 0.0)
        dkl_ref[:, at] = gather_up(jnp.where(mask, mm(da1_ref[:, at], qh_ref[:, at], TN), 0.0))
        many = jnp.ones((8, 128), BF)
        totals_of = []
        for sub in range(2):
            j, inner = 2 * g + sub, pair_lanes(sub)
            b, z = (unfold(small_ref[n, :, pair_lanes(j)], pmask) for n in (3, 5))
            piece = halves(dc[inner, inner])
            dz_ref[j] = mm3(halves(b), piece, NT)
            db = mm3(halves(z), piece, TN)
            dql_ref[:, pair_lanes(j)] = fold(db)
            high, low = halves(db * b)
            totals_of.append((mm(many, high, NT) + mm(many, low, NT))[0:1, :])
        peak = jnp.concatenate(totals_of, axis=1)
        dbb = spread(dql_ref[:, at], mask).astype(BF)
        t_ref[...] = toeplitz(taps_ref, FLIP_AT, own_heads, g)
        acc_ref[...] = jnp.zeros(acc_ref.shape, F32)

        def second(i, carry):
            rows = pl.ds(pl.multiple_of(i * ROWS, ROWS), ROWS)
            row = lax.broadcasted_iota(jnp.int32, (ROWS, 1), 0) + i * ROWS
            valid = (row < length).astype(F32)
            k3 = k3_ref[rows, at]
            vh = vp_ref[pl.ds(pl.multiple_of(i * ROWS + EDGE, EDGE), ROWS), at]
            dk3 = mm(vh, dbb, NT)
            da3_ref[rows, at] = (k3.astype(F32) * (dk3 - peak)).astype(BF)
            window = pl.ds(pl.multiple_of(i * ROWS, ROWS), WINDOW)
            dv = mm(k3, dbb) + diagonal_lanes(mm(t_ref[...], gp_ref[window, at]))
            put(dqkv_ref, rows, 2, wide, parts, g * WIDE, (dv * valid).astype(BF))
            grad = g_ref[rows, at]
            split = jnp.concatenate(
                [jnp.where(col == h, grad, jnp.zeros_like(grad)) for h in range(PACK)], axis=0
            )
            acc_ref[:, :WINDOW] += mm(split, vp_ref[window, at], NT)
            return carry

        lax.fori_loop(0, count, second, 0)
        for h in range(PACK):
            high, low = halves(acc_ref[h * ROWS : (h + 1) * ROWS, :])
            turned = pltpu.roll(mm(flip, high) + mm(flip, low), 0, 1, stride=1, stride_axis=0)
            line = pltpu.roll(jnp.sum(turned, axis=0, keepdims=True), 129, 1)[:, :128]
            totals[totals_row(24 + g * PACK + h)] = jnp.where(taps_lane, line, 0.0)
        dql_ref[:, at] = gather_up(jnp.where(mask, mm(da3_ref[:, at], kh_ref[:, at], TN), 0.0))
        advance(f"second{g}")

    def weight_grad(start, width):
        size = xt_ref.shape[0] // 4

        def block_grad(block, carry):
            rows = pl.ds(pl.multiple_of(block * size, 64), size)
            for p in range(parts):
                lanes = slice(3 * p * share + start, 3 * p * share + start + width)
                here = mm(xt_ref[rows, :], dqkv_ref[:, lanes]).astype(BF)
                if own:
                    four = here.reshape(2, 2, grad_ref.shape[-2], width)
                    grad_ref[block // 2, block % 2, :, :, :, lanes] = four
                else:
                    grad_ref[rows, lanes] = here
            return carry

        lax.fori_loop(0, 4, block_grad, 0)

    late_ref["xt"].wait()
    xt_ref[...] = jnp.transpose(dx_ref[...])
    weight_grad(2 * share, share)
    advance("values")
    late_ref["chain"].wait()
    for j in range(pairs):
        dk_ref[j] = jnp.zeros((128, 128), F32)
        k2_ref[j] = unfold(small_ref[2, :, pair_lanes(j)], pmask)

    def newton(back, carry):
        step = STEPS - 1 - back
        every = range(pairs)
        z, p, t2, t3 = (
            [unfold(chain_ref[step, n, :, pair_lanes(j)], pmask) for j in every] for n in range(KEPT)
        )
        dz = [0.25 * dz_ref[j] for j in every]
        dt3 = [pair_mm(lhs(dz[j]), rhs(z[j])) for j in every]
        dt2 = [-pair_mm(lhs(dt3[j]), rhs(p[j])) for j in every]
        dp = [pair_mm(lhs(dt2[j]), rhs(p[j])) - pair_mm(lhs(t2[j]), rhs(dt3[j])) for j in every]
        dp = [dp[j] - pair_mm(lhs(7.0 * one - p[j]), rhs(dt2[j])) for j in every]
        for j in every:
            dk_ref[j] += pair_mm(lhs(z[j]), rhs(dp[j]))
        new = [pair_mm(lhs(t3[j]), rhs(dz[j])) + pair_mm(lhs(dp[j]), rhs(k2_ref[j])) for j in every]
        for j in every:
            dz_ref[j] = new[j]
        return carry

    for third_of in range(3):
        lax.fori_loop(third_of * STEPS // 3, (third_of + 1) * STEPS // 3, newton, 0)
        advance(f"newton{third_of}")

    for j in range(pairs):
        at = pair_lanes(j)
        k2 = k2_ref[j]
        sums = jnp.sum(k2, axis=0, keepdims=True)
        top = segment_reduce(sums, -1e30, jnp.max)
        hit = (sums == top).astype(F32)
        ties = segment_reduce(hit, 0.0, jnp.sum)
        dz0 = dz_ref[j]
        dtop = -segment_reduce(jnp.sum(dz0 * k2, axis=0, keepdims=True), 0.0, jnp.sum) / (top * top)
        dk2 = jnp.where(pmask, jnp.transpose(dk_ref[j]) + dz0 / top + hit * (dtop / ties), 0.0)
        da2 = halves(k2 * (dk2 - jnp.sum(dk2 * k2, axis=1, keepdims=True)))
        qls, kls = (halves(unfold(small_ref[n, :, at], pmask)) for n in (0, 1))
        dql_ref[:, at] += fold(mm3(da2, kls))
        dkl_ref[:, at] += fold(mm3(da2, qls, TN))
    back = average_back()

    for g in range(groups):
        at = lanes_of(g)
        qlb, klb = (spread(small_ref[n, :, at].astype(BF), mask) for n in (0, 1))

        def third(i, carry):
            rows = pl.ds(pl.multiple_of(i * ROWS, ROWS), ROWS)
            few = pl.ds(pl.multiple_of(i * marks, marks), marks)
            row = lax.broadcasted_iota(jnp.int32, (ROWS, 1), 0) + i * ROWS
            valid = jnp.where(row < length, scale, 0.0)
            dq = mm(da1_ref[rows, at], klb) + mm(back, dql_ref[few, at].astype(BF))
            dk = mm(da3_ref[rows, at], qlb) + mm(back, dkl_ref[few, at].astype(BF))
            put(dqkv_ref, rows, 0, wide, parts, g * WIDE, (dq * valid).astype(BF))
            put(dqkv_ref, rows, 1, wide, parts, g * WIDE, (dk * valid).astype(BF))
            return carry

        lax.fori_loop(0, count, third, 0)
        advance(f"third{g}")

    weight_grad(0, share)
    advance("queries")
    weight_grad(share, share)
    advance("keys")
    late_ref["w"].wait()
    late_ref["dres"].wait()

    def input_rows(i, carry):
        rows = pl.ds(pl.multiple_of(i * TALL, TALL), TALL)
        dx_ref[rows, :] = (dres_ref[rows, :] + mm(dqkv_ref[rows, :], w_ref[...], NT)).astype(BF)
        return carry

    for half in range(2):
        turns = slot // TALL // 2
        lax.fori_loop(half * turns, (half + 1) * turns, input_rows, 0)
        advance(f"input{half}")
    advance("end")


VM = pl.BlockSpec(memory_space=pltpu.VMEM)
SM = pl.BlockSpec(memory_space=pltpu.SMEM)
LIMIT = 60 * 1024 * 1024


def attn_fwd(length, x, parts, own, weights):
    slot, wide = x.shape
    groups = wide // WIDE
    shape = jax.ShapeDtypeStruct
    talks = dict(collective_id=1, has_side_effects=True) if own else {}
    gathered = gather_shapes(weights[0].shape[0], wide, 2 * weights[-1].shape[1]) if own else ()
    outs = pl.pallas_call(
        partial(attn_fwd_kernel, slot, groups, parts, own),
        out_shape=gathered
        + (
            shape((slot, wide), BF),
            shape((slot, wide), BF),
            shape((slot, wide), BF),
            shape((slot + 2 * EDGE, wide), BF),
            shape((slot, wide), BF),
            shape((slot, wide), BF),
            shape((6, MARKS, wide), F32),
            shape((STEPS, KEPT, MARKS, wide), F32),
        ),
        in_specs=[SM, VM] + [VM] * len(weights),
        out_specs=([VM, VM, ANY, ANY, ANY] if own else []) + [VM] + [ANY] * 5 + [VM, ANY],
        scratch_shapes=[
            pltpu.VMEM((2 * groups, 128, 128), F32),
            pltpu.VMEM((2 * groups, 128, 256), BF),
            pltpu.VMEM((slot, WIDE), F32),
            pltpu.VMEM((8, WIDE), F32),
            pltpu.VMEM((PACK * ROWS, WINDOW), BF),
            pltpu.VMEM((slot, wide), BF),
            pltpu.VMEM((slot, wide), BF),
            pltpu.VMEM((slot + 2 * EDGE, wide), BF),
            pltpu.VMEM((slot, wide), BF),
            pltpu.VMEM((slot, wide), BF),
            pltpu.VMEM((STEPS, KEPT, MARKS, wide), F32),
            pltpu.SemaphoreType.DMA((6,)),
        ]
        + (gather_scratch(GATHERS) if own else []),
        compiler_params=pltpu.CompilerParams(vmem_limit_bytes=LIMIT, **talks),
        name="attn_fwd",
    )(length, x, *weights)
    return outs[: len(gathered)], outs[len(gathered) :]


def attn_bwd(length, g, saved, taps, x, weight, dres, block, parts, own, fulls, left=()):
    slot, wide = g.shape
    groups = wide // WIDE
    shape = jax.ShapeDtypeStruct
    talks = dict(collective_id=2, has_side_effects=True) if own else {}
    ends = (shape((slot, wide), BF), shape(block.shape, F32))
    if own:
        rows = fulls[0].shape[0] // 16
        fulls = [f.reshape(2, 2, 2, 2, rows, f.shape[1]) for f in fulls]
        width = 2 * left[0].shape[-1]
        outs = (shape((rows, wide // 2), F32), shape((rows, width), F32))
        outs += (shape((rows, wide // 2), F32),) * 3 + (shape((rows, width), F32),)
        extra = [
            pltpu.VMEM((2, 2, 2, 2, rows, 3 * wide), BF),
            pltpu.VMEM((6,) + block.shape, F32),
            pltpu.VMEM((5,) + block.shape, F32),
        ] + 2 * end_scratch(rows, width // 2) + all_scatter_scratch(SCATTERS, rows, 11)
    else:
        fulls, extra = [], []
        outs = (shape((wide, 3 * wide), BF),)
    return pl.pallas_call(
        partial(attn_bwd_kernel, slot, groups, parts, own),
        out_shape=outs + ends,
        in_specs=[SM] + [VM] * 7 + [ANY, VM, ANY, ANY, ANY, VM] + [ANY] * len(fulls) + [VM] * len(left),
        out_specs=[VM] * (len(outs) + 2),
        scratch_shapes=[
            pltpu.VMEM(saved[-1].shape, F32),
            pltpu.VMEM((wide, slot), BF),
            pltpu.VMEM(weight.shape, BF),
            pltpu.VMEM(dres.shape, F32),
            pltpu.SemaphoreType.DMA((4,)),
            pltpu.VMEM((slot, 3 * wide), BF),
            pltpu.VMEM((slot + 2 * EDGE, wide), BF),
            pltpu.VMEM((slot, wide), BF),
            pltpu.VMEM((slot, wide), BF),
            pltpu.VMEM((2 * groups, 128, 128), F32),
            pltpu.VMEM((2 * groups, 128, 128), F32),
            pltpu.VMEM((2 * groups, 128, 128), F32),
            pltpu.VMEM((MARKS, wide), F32),
            pltpu.VMEM((MARKS, wide), F32),
            pltpu.VMEM((PACK * ROWS, WINDOW), BF),
            pltpu.VMEM((PACK * ROWS, 256), F32),
        ]
        + extra,
        compiler_params=pltpu.CompilerParams(vmem_limit_bytes=67043328, **talks),
        name="attn_bwd",
    )(length, g, *saved, taps, x, weight, dres, block, *fulls, *left)
MESH = pl.DeviceIdType.MESH
WAYS = ("zh", "zl", "y", "x", "c")
COPIES = 11
STAGES = 6


class Place:
    def __init__(self):
        dp = lax.axis_index("dp")
        self.x = lax.axis_index("tensor")
        self.zh, self.zl = dp // 8, (dp // 4) % 2
        self.y, self.c = (dp // 2) % 2, dp % 2

    def at(self, way):
        spot = {w: getattr(self, w) for w in WAYS}
        spot[way] = 1 - spot[way]
        return {
            "dp": spot["zh"] * 8 + spot["zl"] * 4 + spot["y"] * 2 + spot["c"],
            "tensor": spot["x"],
        }


def greet(place):
    barrier = pltpu.get_barrier_semaphore()
    for way in WAYS:
        pl.semaphore_signal(barrier, inc=1, device_id=place.at(way), device_id_type=MESH)
    pl.semaphore_wait(barrier, len(WAYS))


class Mover:
    def __init__(self, place, send, recv, base):
        self.place, self.send, self.recv, self.base = place, send, recv, base
        self.started = []

    def copy(self, index, src, dst, way):
        return pltpu.make_async_remote_copy(
            src_ref=src, dst_ref=dst,
            send_sem=self.send.at[self.base + index], recv_sem=self.recv.at[self.base + index],
            device_id=self.place.at(way), device_id_type=MESH,
        )

    def push(self, index, src, dst, way):
        copy = self.copy(index, src, dst, way)
        copy.start()
        self.started.append(copy)

    def arrive(self, index, ref, way):
        self.copy(index, ref, ref, way).wait_recv()

    def drain(self):
        for copy in self.started:
            copy.wait_send()


class Gather(Mover):
    def __init__(self, place, shard, whole, lane, width, order, send, recv, base, local, last=4):
        super().__init__(place, send, recv, base)
        self.last = last
        self.shard, self.whole, self.local = shard, whole, local
        self.lane, self.width, self.order = lane, width, order

    def view(self, zh, zl, y, c, x):
        half = self.whole.shape[-1] // 2
        lanes = pl.ds(pl.multiple_of(x * half + self.lane, 128), self.width)
        return self.whole.at[zh, zl, y, c, :, lanes]

    def steps(self, c):
        p, every = self.place, slice(None)
        yield "zh", [self.view(p.zh, p.zl, p.y, c, p.x)], [self.view(1 - p.zh, p.zl, p.y, c, p.x)]
        yield "zl", [self.view(every, p.zl, p.y, c, p.x)], [self.view(every, 1 - p.zl, p.y, c, p.x)]
        if self.order == "yx":
            yield "y", [self.view(every, every, p.y, c, p.x)], [self.view(every, every, 1 - p.y, c, p.x)]
            yield "x", [self.view(every, every, every, c, p.x)], [self.view(every, every, every, c, 1 - p.x)]
        else:
            yield "x", [self.view(every, every, p.y, c, p.x)], [self.view(every, every, p.y, c, 1 - p.x)]
            yield (
                "y",
                [self.view(every, every, p.y, c, x) for x in (0, 1)],
                [self.view(every, every, 1 - p.y, c, x) for x in (0, 1)],
            )

    def run(self, stage):
        p = self.place
        here = self.view(p.zh, p.zl, p.y, p.c, p.x)
        if stage == 0:
            self.mine, self.other = list(self.steps(p.c)), list(self.steps(1 - p.c))
            self.push(0, self.shard, here, "zh")
            self.push(5, self.shard, here, "c")
            self.own = pltpu.make_async_copy(self.shard, here, self.local)
            self.own.start()
        elif stage <= self.last:
            way, _, landed = self.mine[stage - 1]
            for i, ref in enumerate(landed):
                self.arrive(stage - 1 + i, ref, way)
            if stage == 1:
                self.own.wait()
            if stage < self.last:
                way, outgoing, _ = self.mine[stage]
                for i, ref in enumerate(outgoing):
                    self.push(stage + i, ref, ref, way)
            for i, ref in enumerate(landed):
                self.push(5 + stage + i, ref, ref, "c")
        elif stage == self.last + 1:
            self.arrive(5, self.view(p.zh, p.zl, p.y, 1 - p.c, p.x), "c")
            for k in range(self.last):
                for i, ref in enumerate(self.other[k][2]):
                    self.arrive(6 + k + i, ref, "c")
            self.drain()


class GatherEnd(Gather):
    def __init__(self, place, early, whole, lane, width, order, send, recv, base, local):
        Mover.__init__(self, place, send, recv, base)
        self.early, self.whole, self.local = early, whole, local
        self.lane, self.width, self.order = lane, width, order

    def halves_of(self, c):
        p, every = self.place, slice(None)
        if self.order == "yx":
            return "x", [(every, every, every, c, p.x)], [(every, every, every, c, 1 - p.x)]
        return (
            "y",
            [(every, every, p.y, c, x) for x in (0, 1)],
            [(every, every, 1 - p.y, c, x) for x in (0, 1)],
        )

    def old(self, spot):
        now, self.whole = self.whole, self.early
        ref = self.view(*spot)
        self.whole = now
        return ref

    def run(self, stage):
        p, every = self.place, slice(None)
        way, sent, landed = self.halves_of(p.c)
        if stage == 0:
            for i, spot in enumerate(sent):
                self.push(i, self.old(spot), self.view(*spot), way)
            self.loads = []
            if self.order == "yx":
                spots = [(every, every, every, every, p.x)]
            else:
                spots = [(every, every, p.y, every, x) for x in (0, 1)]
            for i, spot in enumerate(spots):
                load = pltpu.make_async_copy(self.old(spot), self.view(*spot), self.local.at[i])
                load.start()
                self.loads.append(load)
        elif stage == 1:
            for i, spot in enumerate(landed):
                self.arrive(i, self.view(*spot), way)
                self.push(2 + i, self.view(*spot), self.view(*spot), "c")
        else:
            for i, spot in enumerate(self.halves_of(1 - p.c)[2]):
                self.arrive(2 + i, self.view(*spot), "c")
            for load in self.loads:
                load.wait()
            self.drain()


class Scatter(Mover):
    def __init__(self, place, full, lane, width, order, out, bufs, send, recv, base, local):
        super().__init__(place, send, recv, base)
        self.full, self.lane, self.width, self.order = full, lane, width, order
        self.out, self.local = out, local
        self.sums, self.in_c, self.in_1, self.in_2, self.in_l, self.in_h = bufs

    def lanes(self, x):
        half = self.full.shape[-1] // 2
        return pl.ds(x * half + self.lane, self.width)

    def add(self, target, landed):
        lead = landed.shape[:-2]
        total = 1
        for n in lead:
            total *= n
        flat_dims = lead

        def one(i, carry):
            index = []
            for n in reversed(flat_dims):
                index.append(i % n)
                i = i // n
            index = tuple(reversed(index))
            target[index] = target[index] + landed[index]
            return carry

        if total == 1:
            one(0, 0)
        else:
            lax.fori_loop(0, total, one, 0)

    def run(self, stage):
        p, every = self.place, slice(None)
        if stage == 0:
            self.loads = []
            for x in (0, 1):
                self.push(x, self.full.at[:, :, :, 1 - p.c, :, self.lanes(x)], self.in_c.at[x], "c")
                load = pltpu.make_async_copy(
                    self.full.at[:, :, :, p.c, :, self.lanes(x)], self.sums.at[x], self.local.at[x]
                )
                load.start()
                self.loads.append(load)
            return
        if stage == 1:
            for x in (0, 1):
                self.arrive(x, self.in_c.at[x], "c")
                self.loads[x].wait()
            self.add(self.sums, self.in_c)
            if self.order == "xy":
                self.push(2, self.sums.at[1 - p.x], self.in_1.at[...], "x")
            else:
                for x in (0, 1):
                    self.push(2 + x, self.sums.at[x, :, :, 1 - p.y], self.in_1.at[x], "y")
        elif stage == 2:
            if self.order == "xy":
                self.arrive(2, self.in_1, "x")
                self.add(self.sums.at[p.x], self.in_1)
                self.push(4, self.sums.at[p.x, :, :, 1 - p.y], self.in_2, "y")
            else:
                for x in (0, 1):
                    self.arrive(2 + x, self.in_1.at[x], "y")
                    self.add(self.sums.at[x, :, :, p.y], self.in_1.at[x])
                self.push(4, self.sums.at[1 - p.x, :, :, p.y], self.in_2, "x")
        elif stage == 3:
            self.arrive(4, self.in_2, "y" if self.order == "xy" else "x")
            self.add(self.sums.at[p.x, :, :, p.y], self.in_2)
            self.push(5, self.sums.at[p.x, :, 1 - p.zl, p.y], self.in_l, "zl")
        elif stage == 4:
            self.arrive(5, self.in_l, "zl")
            self.add(self.sums.at[p.x, :, p.zl, p.y], self.in_l)
            self.push(6, self.sums.at[p.x, 1 - p.zh, p.zl, p.y], self.in_h, "zh")
        else:
            self.arrive(6, self.in_h, "zh")
            self.store(
                self.sums[p.x, p.zh, p.zl, p.y].astype(F32) + self.in_h[...].astype(F32)
            )
            self.drain()

    def store(self, value):
        ref, first = self.out
        ref[:, first : first + self.width] = value


class ScatterStart(Scatter):
    def run(self, stage):
        if stage < 2:
            super().run(stage)
            return
        p = self.place
        for k in (0, 1):
            if self.order == "xy":
                if k == 0:
                    self.arrive(2, self.in_1, "x")
                here, index = self.sums, lambda a, b, k=k: (p.x, a, b, k)
                there = lambda a, b, k=k: (a, b, k)
            else:
                self.arrive(2 + k, self.in_1.at[k], "y")
                here, index = self.sums, lambda a, b, k=k: (k, a, b, p.y)
                there = lambda a, b, k=k: (k, a, b)
            for a in (0, 1):
                for b in (0, 1):
                    self.out[k, a, b] = here[index(a, b)] + self.in_1[there(a, b)]
        self.drain()


class ScatterEnd(Mover):
    def __init__(self, place, left, out, lane, order, bufs, send, recv, base):
        super().__init__(place, send, recv, base)
        self.left, self.out, self.lane = left, out, lane
        self.way = "y" if order == "xy" else "x"
        self.in_2, self.in_l, self.in_h, self.quarter, self.sums = bufs

    def run(self, stage):
        p = self.place
        mine = getattr(p, self.way)
        if stage == 0:
            self.push(0, self.left.at[1 - mine], self.in_2, self.way)
        elif stage == 1:
            self.arrive(0, self.in_2, self.way)
            for a in (0, 1):
                for b in (0, 1):
                    self.quarter[a, b] = self.left[mine, a, b] + self.in_2[a, b]
            self.push(1, self.quarter.at[:, 1 - p.zl], self.in_l, "zl")
        elif stage == 2:
            self.arrive(1, self.in_l, "zl")
            for a in (0, 1):
                self.sums[a] = self.quarter[a, p.zl] + self.in_l[a]
            self.push(2, self.sums.at[1 - p.zh], self.in_h, "zh")
        else:
            self.arrive(2, self.in_h, "zh")
            width = self.in_h.shape[-1]
            self.out[:, self.lane : self.lane + width] = (
                self.sums[p.zh].astype(F32) + self.in_h[...].astype(F32)
            )
            self.drain()


def end_scratch(rows, width):
    return [
        pltpu.VMEM((2, 2, rows, width), BF),
        pltpu.VMEM((2, rows, width), BF),
        pltpu.VMEM((rows, width), BF),
        pltpu.VMEM((2, 2, rows, width), BF),
        pltpu.VMEM((2, rows, width), BF),
    ]


def scatter_scratch(rows, width, order):
    first = (2, 2, 2) if order == "xy" else (2, 2, 2)
    return [
        pltpu.VMEM((2, 2, 2, 2, rows, width), BF),
        pltpu.VMEM((2, 2, 2, 2, rows, width), BF),
        pltpu.VMEM(first + (rows, width), BF),
        pltpu.VMEM((2, 2, rows, width), BF),
        pltpu.VMEM((2, rows, width), BF),
        pltpu.VMEM((rows, width), BF),
    ]


class Total(Mover):
    def __init__(self, place, block, out, sums, landed, send, recv, base, features):
        super().__init__(place, send, recv, base)
        self.features = features
        self.block, self.out, self.sums, self.landed = block, out, sums, landed

    def run(self, stage):
        if stage > 0:
            self.arrive(stage - 1, self.landed.at[stage - 1], WAYS[stage - 1])
            self.sums[stage] = self.sums[stage - 1] + self.landed[stage - 1]
        if stage < 5:
            self.push(stage, self.sums.at[stage], self.landed.at[stage], WAYS[stage])
        else:
            final = self.sums[5]
            self.out[...] = final
            squares = final[STATS : STATS + 1, :]
            self.out[STATS + 1 : STATS + 2, :] = jnp.sqrt(squares / (squares[:, 3:4] * self.features))
            self.drain()


GATHERS = (
    (0, 0, 384, "yx", 0, 0), (0, 384, 384, "xy", 1, 0), (1, 0, 128, "yx", 3, 0),
    (0, 768, 256, "yx", 2, 0), (0, 1024, 128, "xy", 2, 256),
    (3, 0, 384, "yx", 5, 0), (3, 384, 384, "xy", 5, 384),
    (3, 768, 384, "yx", 5, 768), (3, 1152, 384, "xy", 5, 1152),
    (2, 0, 256, "yx", 4, 0), (2, 256, 128, "xy", 4, 256),
    (4, 0, 768, "yx", 6, 0), (4, 768, 768, "xy", 6, 768),
)
GATHER_WAVES = "qqqvvaabbbbdd"
GATHER_LAST = (4,) * 11 + (3, 3)
GATHER_AT = {
    "start": (("q", 0), ("q", 1), ("q", 2), ("v", 0), ("q", 3), ("v", 1), ("a", 0), ("v", 2),
              ("a", 1), ("q", 4), ("b", 0), ("q", 5), ("a", 2)),
    "load": (("v", 3), ("a", 3), ("b", 1), ("d", 0)),
    "newton1": (("v", 4), ("b", 2)),
    "third2": (("v", 5), ("a", 4), ("d", 1)),
    "first1": (("b", 3),),
    "first2": (("a", 5),),
    "mix0": (("d", 2),),
    "end": (("b", 4), ("d", 3), ("b", 5), ("d", 4)),
}
DOWN_GATHERS = GATHERS[-2:]
DOWN_SCATTERS = ((0, 0, 768, "xy"), (0, 768, 768, "yx"))
SCATTERS = (
    (1, 0, 768, "xy", 1, 0), (1, 768, 768, "yx", 1, 768),
    (0, 0, 256, "xy", 0, 0), (0, 256, 128, "yx", 0, 256),
    (2, 768, 256, "xy", 4, 0), (2, 1024, 128, "yx", 4, 256),
    (2, 0, 256, "yx", 2, 0), (2, 256, 128, "xy", 2, 256),
    (2, 384, 256, "xy", 3, 0), (2, 640, 128, "yx", 3, 256),
)
SCATTER_WAVES = "aaaavvqqkk"
SCATTER_AT = {
    "start": (("a", 0), ("d", 0)),
    "second0": (("d", 1), ("a", 1)),
    "second1": (("d", 2),),
    "second2": (("t", 0), ("d", 3)),
    "values": (("v", 0), ("t", 1)),
    "newton0": (("t", 2),),
    "newton1": (("t", 3),),
    "newton2": (("a", 2), ("v", 1), ("t", 4)),
    "third1": (("t", 5),),
    "queries": (("q", 0), ("a", 3)),
    "keys": (("k", 0), ("q", 1), ("v", 2)),
    "input0": (("k", 1), ("v", 3), ("q", 2), ("a", 4)),
    "input1": (("k", 2), ("v", 4), ("q", 3), ("k", 3)),
    "end": (("v", 5), ("q", 4), ("k", 4), ("a", 5), ("q", 5), ("k", 5)),
}


def gather_parts(place, cuts, shards, wholes, send, recv, local):
    parts = []
    for n, (i, lane, width, order, source, first) in enumerate(cuts):
        shard = shards[source].at[:, pl.ds(first, width)]
        parts.append(Gather(place, shard, wholes[i], lane, width, order, send, recv, COPIES * n,
                            local.at[n], GATHER_LAST[n]))
    return parts


def gather_scratch(cuts):
    n = len(cuts)
    return [
        pltpu.SemaphoreType.DMA((COPIES * n,)),
        pltpu.SemaphoreType.DMA((COPIES * n,)),
        pltpu.SemaphoreType.DMA((n,)),
    ]


def gather_shapes(rows, wide, units):
    whole = (2, 2, 2, 2)
    return (
        jax.ShapeDtypeStruct(whole + (rows, 3 * wide), BF),
        jax.ShapeDtypeStruct(whole + (BLOCK, 256), F32),
        jax.ShapeDtypeStruct(whole + (rows, wide), BF),
        jax.ShapeDtypeStruct(whole + (rows, units), BF),
        jax.ShapeDtypeStruct(whole + (rows, units), BF),
    )


SUM_COPIES = 7


def scatter_parts(place, cuts, fulls, outs, refs):
    send, recv, local = refs[-3:]
    return [
        Scatter(place, fulls[i], lane, width, order, (outs[n_out], first),
                refs[6 * n : 6 * n + 6], send, recv, SUM_COPIES * n, local.at[n])
        for n, (i, lane, width, order, n_out, first) in enumerate(cuts)
    ]


def all_scatter_scratch(cuts, rows, extra=0):
    out = []
    for _, _, width, order, *_ in cuts:
        out += scatter_scratch(rows, width, order)
    n = len(cuts)
    return out + [
        pltpu.SemaphoreType.DMA((SUM_COPIES * n + extra,)),
        pltpu.SemaphoreType.DMA((SUM_COPIES * n + extra,)),
        pltpu.SemaphoreType.DMA((n, 2)),
    ]


def norm_parts(values):
    centre = values - jnp.mean(values, axis=-1, keepdims=True)
    spread_of = jnp.mean(centre * centre, axis=-1, keepdims=True)
    inverse = lax.rsqrt(spread_of + 1e-05)
    return centre * inverse, inverse


def norm_grad(grad, gain, normal, inverse):
    scaled = grad * gain
    lean = jnp.mean(scaled, axis=-1, keepdims=True)
    along = jnp.mean(scaled * normal, axis=-1, keepdims=True)
    return inverse * (scaled - lean - normal * along)


TURNS = 12


def mid_kernel(slot, wide, *refs):
    (len_ref, ctx_ref, x_ref, far_cot, outw_ref, far_inw, partial_ref, gain_ref,
     dctx_ref, res_ref, far_out, far_gin, gout_ref, left_a, left_b, ends_ref,
     downw_ref, hid_ref, turn_ref, act_ref, slope_ref, acc_ref, dlow_ref, gdown_ref, sum_ref) = refs[:25]
    cot_ref, inw_ref, out_ref, gin_ref, copies = refs[25:30]
    get_inw = pltpu.make_async_copy(far_inw, inw_ref, copies.at[0])
    get_cot = pltpu.make_async_copy(far_cot, cot_ref, copies.at[1])
    put_out = pltpu.make_async_copy(out_ref, far_out, copies.at[2])
    put_gin = pltpu.make_async_copy(gin_ref, far_gin, copies.at[3])
    refs = refs[:24] + refs[30:]
    place = Place()
    greet(place)
    gsend, grecv, glocal = refs[-3 - 3 : -3]
    late = [
        GatherEnd(place, partial_ref, downw_ref, lane, width, order, gsend, grecv, 4 * n, glocal.at[n])
        for n, (_, lane, width, order, *_) in enumerate(DOWN_GATHERS)
    ]
    down = [
        ScatterStart(place, gdown_ref, lane, width, order, (left_a, left_b)[n],
                     refs[24 + 6 * n : 30 + 6 * n], refs[-3], refs[-2], SUM_COPIES * n, refs[-1].at[n])
        for n, (_, lane, width, order) in enumerate(DOWN_SCATTERS)
    ]

    def both(parts, stage):
        for part in parts:
            part.run(stage)

    both(late, 0)
    get_inw.start()
    get_cot.start()
    hidden_units = act_ref.shape[1]
    step = hidden_units // TURNS
    length = len_ref[lax.axis_index("tensor")]
    gain_one, bias_one = gain_ref[0:1, :], gain_ref[1:2, :]
    gain_two, bias_two = gain_ref[2:3, :], gain_ref[3:4, :]
    sum_ref[...] = jnp.zeros(sum_ref.shape, F32)

    def valid_of(i, rows):
        row = lax.broadcasted_iota(jnp.int32, (rows, 1), 0) + i * rows
        return (row < length).astype(F32)

    def span(i, rows):
        return pl.ds(pl.multiple_of(i * rows, rows), rows)

    def count(row, values):
        sum_ref[row : row + 1, :] += jnp.sum(values, axis=0, keepdims=True)

    def unit(i):
        return pl.ds(pl.multiple_of(i * step, 128), step)

    def weight(ref, lanes):
        return ref[:, :, :, :, :, lanes].reshape(wide, -1)

    def project(i, carry):
        rows = span(i, TALL)
        acc_ref[rows, :] = mm(ctx_ref[rows, :], outw_ref[...], NT)
        return carry

    lax.fori_loop(0, slot // TALL, project, 0)

    def norm_one(i, carry):
        rows = span(i, ROWS)
        valid = valid_of(i, ROWS)
        attn, x = acc_ref[rows, :], x_ref[rows, :].astype(F32)
        count(4, valid * x * x)
        count(5, valid * attn * attn)
        total = x + attn
        res_ref[rows, :] = total
        normal, _ = norm_parts(total)
        hid_ref[rows, :] = (normal * gain_one + bias_one).astype(BF)
        return carry

    lax.fori_loop(0, slot // ROWS, norm_one, 0)

    def expand(i, carry):
        lanes = unit(i)
        for block in range(slot // TALL):
            rows = slice(block * TALL, (block + 1) * TALL)
            pre = mm(hid_ref[rows, :], inw_ref[:, lanes])
            below = 0.5 * (1.0 + lax.erf(pre * 0.5**0.5))
            act_ref[rows, lanes] = (pre * below).astype(BF)
            slope = below + pre * jnp.exp(-0.5 * pre * pre) * (2.0 * jnp.pi) ** -0.5
            slope_ref[rows, lanes] = slope.astype(BF)
        return carry

    get_inw.wait()
    lax.fori_loop(0, TURNS * 3 // 4, expand, 0)
    both(late, 1)
    lax.fori_loop(TURNS * 3 // 4, TURNS, expand, 0)
    both(late, 2)

    def contract(i, carry):
        rows = span(i, 512)
        acc_ref[rows, :] = mm(act_ref[rows, :], weight(downw_ref, slice(None)), NT)
        return carry

    lax.fori_loop(0, slot // 512, contract, 0)

    def norm_two(i, carry):
        rows = span(i, ROWS)
        valid = valid_of(i, ROWS)
        ffn = acc_ref[rows, :]
        count(6, valid * ffn * ffn)
        normal, inverse = norm_parts(hid_ref[rows, :].astype(F32) + ffn)
        out_ref[rows, :] = (normal * gain_two + bias_two).astype(BF)
        grad = cot_ref[rows, :].astype(F32) * valid
        count(2, grad * normal)
        count(3, grad)
        back = norm_grad(grad, gain_two, normal, inverse)
        acc_ref[rows, :] = back
        dlow_ref[rows, :] = back.astype(BF)
        return carry

    get_cot.wait()
    lax.fori_loop(0, slot // ROWS, norm_two, 0)
    put_out.start()
    turn_ref[...] = jnp.transpose(dlow_ref[...])

    def down_grad(i, carry):
        each = TURNS // 4
        block = i // TURNS
        i = (i % TURNS) // each * 2 * each + i % each + block * each
        lanes = unit(i)
        value = mm(turn_ref[...], act_ref[:, lanes]).astype(BF)
        gdown_ref[:, :, :, :, :, lanes] = value.reshape(gdown_ref.shape[:-1] + (step,))
        return carry

    lax.fori_loop(0, TURNS // 2, down_grad, 0)
    down[0].run(0)
    lax.fori_loop(TURNS, TURNS + TURNS // 2, down_grad, 0)
    down[1].run(0)
    down[0].run(1)
    turn_ref[...] = jnp.transpose(hid_ref[...])

    def back_grad(i, carry):
        lanes = unit(i)
        weights = weight(downw_ref, lanes)
        for block in range(slot // TALL):
            rows = slice(block * TALL, (block + 1) * TALL)
            pre = mm(dlow_ref[rows, :], weights) * slope_ref[rows, lanes].astype(F32)
            slope_ref[rows, lanes] = pre.astype(BF)
        gin_ref[:, lanes] = mm(turn_ref[...], slope_ref[:, lanes]).astype(BF)
        return carry

    lax.fori_loop(0, TURNS // 4, back_grad, 0)
    down[1].run(1)
    lax.fori_loop(TURNS // 4, TURNS, back_grad, 0)
    put_gin.start()

    def narrow(i, carry):
        rows = span(i, 512)
        acc_ref[rows, :] += mm(slope_ref[rows, :], inw_ref[...], NT)
        return carry

    lax.fori_loop(0, slot // 512, narrow, 0)

    def norm_one_back(i, carry):
        rows = span(i, ROWS)
        grad = acc_ref[rows, :]
        normal, inverse = norm_parts(res_ref[rows, :])
        count(0, grad * normal)
        count(1, grad)
        back = norm_grad(grad, gain_one, normal, inverse)
        res_ref[rows, :] = back
        dlow_ref[rows, :] = back.astype(BF)
        return carry

    lax.fori_loop(0, slot // ROWS, norm_one_back, 0)
    turn_ref[...] = jnp.transpose(dlow_ref[...])

    def out_grad(i, carry):
        rows = span(i, TALL)
        gout_ref[rows, :] = mm(turn_ref[rows, :], ctx_ref[...]).astype(BF)
        return carry

    lax.fori_loop(0, wide // TALL, out_grad, 0)

    def reach(i, carry):
        rows = span(i, TALL)
        dctx_ref[rows, :] = mm(dlow_ref[rows, :], outw_ref[...]).astype(BF)
        return carry

    lax.fori_loop(0, slot // TALL, reach, 0)
    ends_ref[...] = jnp.zeros(ends_ref.shape, F32)
    tiles = wide // 128
    for n in range(4):
        for tile in range(tiles):
            ends_ref[n * tiles + tile : n * tiles + tile + 1, :] = sum_ref[n : n + 1, tile * 128 : (tile + 1) * 128]
    lane = lax.broadcasted_iota(jnp.int32, (1, 128), 1)
    line = jnp.where(lane == 3, jnp.minimum(length, slot).astype(F32), 0.0)
    for n in range(3):
        line = jnp.where(lane == n, jnp.sum(sum_ref[4 + n : 5 + n, :], axis=1, keepdims=True), line)
    ends_ref[STATS : STATS + 1, :] = line
    both(down, 2)
    put_out.wait()
    put_gin.wait()


def mid_call(length, ctx, x, cot, outw, inw, part, gains):
    slot, wide = x.shape
    units = inw.shape[1]
    rows = part.shape[-2]
    shape = jax.ShapeDtypeStruct
    whole = (2, 2, 2, 2, rows, units)
    n = len(DOWN_GATHERS)
    return pl.pallas_call(
        partial(mid_kernel, slot, wide),
        out_shape=(
            shape((slot, wide), BF),
            shape((slot, wide), F32),
            shape((slot, wide), BF),
            shape((wide, units), BF),
            shape((wide, wide), BF),
            shape((2, 2, 2, rows, units // 4), BF),
            shape((2, 2, 2, rows, units // 4), BF),
            shape((40, 128), F32),
        ),
        in_specs=[SM, VM, VM, ANY, VM, ANY, ANY, VM],
        out_specs=[VM, VM, ANY, ANY, VM, VM, VM, VM],
        scratch_shapes=[
            pltpu.VMEM(whole, BF),
            pltpu.VMEM((slot, wide), BF),
            pltpu.VMEM((wide, slot), BF),
            pltpu.VMEM((slot, units), BF),
            pltpu.VMEM((slot, units), BF),
            pltpu.VMEM((slot, wide), F32),
            pltpu.VMEM((slot, wide), BF),
            pltpu.VMEM(whole, BF),
            pltpu.VMEM((8, wide), F32),
            pltpu.VMEM((slot, wide), BF),
            pltpu.VMEM(inw.shape, BF),
            pltpu.VMEM((slot, wide), BF),
            pltpu.VMEM((wide, units), BF),
            pltpu.SemaphoreType.DMA((4,)),
        ]
        + all_scatter_scratch(DOWN_SCATTERS, rows)[:-3]
        + [
            pltpu.SemaphoreType.DMA((4 * n,)),
            pltpu.SemaphoreType.DMA((4 * n,)),
            pltpu.SemaphoreType.DMA((n, 2)),
        ]
        + all_scatter_scratch(DOWN_SCATTERS, rows)[-3:],
        compiler_params=pltpu.CompilerParams(
            vmem_limit_bytes=67043328, collective_id=4, has_side_effects=True
        ),
        name="middle",
    )(length, ctx, x, cot, outw, inw, part, gains)


D = 768
BOTH = ("tensor", "dp")


def rows_sum(left_op, right_op):
    return lax.dot_general(left_op, right_op, (TN, ((), ())), preferred_element_type=F32)


def cols_sum(left_op, right_op):
    return lax.dot_general(left_op, right_op, (NT, ((), ())), preferred_element_type=F32)


def dense(left_op, right_op):
    return jnp.dot(left_op, right_op, preferred_element_type=F32)


def norm_back(grad, gain, normal, inverse):
    return (
        norm_grad(grad, gain, normal, inverse),
        jnp.sum(grad * normal, axis=0),
        jnp.sum(grad, axis=0),
    )


def gather_plain(pieces):
    sizes = lax.axis_size("tensor"), lax.axis_size("dp")
    out = []
    for piece in pieces:
        joined = lax.all_gather(piece, BOTH, axis=0, tiled=True)
        joined = joined.reshape(sizes[0], sizes[1] * piece.shape[0], piece.shape[1])
        out.append(joined.transpose(1, 0, 2).reshape(joined.shape[1], -1))
    return out


def scatter_plain(fulls):
    parts = lax.axis_size("tensor")
    out = []
    for full in fulls:
        stacked = full.reshape(full.shape[0], parts, -1).transpose(1, 0, 2).reshape(-1, full.shape[1] // parts)
        out.append(lax.psum_scatter(stacked, BOTH, scatter_dimension=0, tiled=True).astype(F32))
    return out


def per_device(own, x_in, lengths, cotangent, w_query, w_key, w_value, w_out, w_in, w_down,
               conv_weight, ln1_gain, ln1_bias, ln2_gain, ln2_bias):
    tensor_index = lax.axis_index("tensor")
    slot = x_in.shape[0]
    parts = lax.axis_size("tensor")
    length = lengths

    later = (w_out.T, w_in, w_down.T)
    few, own_heads, count = ln1_gain.shape[0], conv_weight.shape[0], conv_weight.shape[1]

    def rows_of(array, rows):
        return jnp.pad(array, ((0, rows - array.shape[0]), (0, 128 - array.shape[1])))

    vectors = jnp.stack([ln1_gain, ln1_bias, ln2_gain, ln2_bias])
    block = jnp.concatenate(
        [rows_of(vectors, TAPS_AT), rows_of(conv_weight, FLIP_AT - TAPS_AT),
         rows_of(conv_weight[:, ::-1], BLOCK - FLIP_AT)],
        axis=0,
    )
    if own:
        wholes, saved = attn_fwd(
            length, x_in, parts, own, (w_query, w_key, w_value, block) + later
        )
        qkv_w, blocks, out_w, in_w = (w.reshape(-1, w.shape[-1]) for w in wholes[:4])
        taps = blocks
        blocks = blocks.reshape(lax.axis_size("dp"), BLOCK, parts, 128)
    else:
        qkv_w, out_w, in_w, down_w = gather_plain(
            (jnp.concatenate([w_query, w_key, w_value], axis=1),) + later
        )
        blocks = lax.all_gather(block, ("dp", "tensor"), axis=0)
        blocks = blocks.reshape(-1, parts, BLOCK, 128).transpose(0, 2, 1, 3)
        taps = blocks[0].reshape(BLOCK, parts * 128)
        _, saved = attn_fwd(length, x_in, parts, own, (qkv_w, taps))
    gains = blocks[:, :4, :, :few].transpose(1, 0, 2, 3).reshape(4, D)
    gain_one, bias_one, gain_two, bias_two = gains[0], gains[1], gains[2], gains[3]
    ctx, saved = saved[0], saved[1:]

    if own:
        d_ctx, d_res1, output, grad_in, grad_out, *left, ends = mid_call(
            length, ctx, x_in, cotangent, out_w, in_w, wholes[4], jnp.pad(gains, ((0, 4), (0, 0)))
        )
        fulls = [grad_out, grad_in]
    else:
        left = ()
        tokens = x_in.astype(F32)
        mine = lax.dynamic_slice_in_dim(lengths, tensor_index, 1)
        valid = (jnp.arange(slot, dtype=jnp.int32) < mine[0]).astype(F32)[:, None]
        attn_branch = cols_sum(ctx, out_w)
        normal_one, inverse_one = norm_parts(tokens + attn_branch)
        hidden = (normal_one * gain_one + bias_one).astype(BF)
        pre = dense(hidden, in_w)
        below = 0.5 * (1.0 + lax.erf(pre * 0.5**0.5))
        act = (pre * below).astype(BF)
        slope = (below + pre * jnp.exp(-0.5 * pre * pre) * (2.0 * jnp.pi) ** -0.5).astype(BF)
        ffn_branch = cols_sum(act, down_w)
        normal_two, inverse_two = norm_parts(hidden.astype(F32) + ffn_branch)
        output = (normal_two * gain_two + bias_two).astype(BF)
        grad_result = cotangent.astype(F32) * valid
        d_res2, grad_gain_two, grad_bias_two = norm_back(grad_result, gain_two, normal_two, inverse_two)
        d_ffn = d_res2.astype(BF)
        grad_down = rows_sum(d_ffn, act)
        d_pre = (dense(d_ffn, down_w) * slope.astype(F32)).astype(BF)
        grad_in = rows_sum(hidden, d_pre)
        d_hidden = cols_sum(d_pre, in_w) + d_res2
        d_res1, grad_gain_one, grad_bias_one = norm_back(d_hidden, gain_one, normal_one, inverse_one)
        d_attn = d_res1.astype(BF)
        grad_out = rows_sum(d_attn, ctx)
        d_ctx = dense(d_attn, out_w).astype(BF)
        fulls = [grad_out.astype(BF), grad_in.astype(BF), grad_down.astype(BF)]

        def total(branch):
            return jnp.sum(valid * branch * branch)

        sums = jnp.stack([total(tokens), total(attn_branch), total(ffn_branch), jnp.sum(valid)])
        ends = jnp.concatenate(
            [
                jnp.stack([grad_gain_one, grad_bias_one, grad_gain_two, grad_bias_two]).reshape(24, 128),
                jnp.zeros((12, 128), F32),
                jnp.pad(sums[None], ((0, 3), (0, 124))),
            ],
            axis=0,
        )
    grads = attn_bwd(length, d_ctx, saved, taps, x_in, qkv_w, d_res1, ends, parts, own, fulls, left)
    input_grad, summed = grads[-2:]
    if own:
        weight_grads = (*grads[2:5], grads[0].T, grads[1], grads[5].T)
        stats = summed[STATS + 1, :3]
    else:
        early, (late,) = scatter_plain(fulls), scatter_plain([grads[0]])
        width = late.shape[1] // 3
        weight_grads = (
            late[:, :width], late[:, width : 2 * width], late[:, 2 * width :],
            early[0].T, early[1], early[2].T,
        )
        summed = lax.psum(summed, ("dp", "tensor"))
        stats = jnp.sqrt(summed[STATS, :3] / (summed[STATS, 3] * D))
    share = D // lax.axis_size(("dp", "tensor"))
    start_at = lax.axis_index(("dp", "tensor")) * share
    vectors = lax.dynamic_slice_in_dim(summed[:24].reshape(4, D), start_at, share, 1)
    conv_grad = lax.dynamic_slice_in_dim(summed, 24 + tensor_index * own_heads, own_heads, 0)[:, :count]
    return (
        output, input_grad, *weight_grads,
        conv_grad, vectors[0], vectors[1], vectors[2], vectors[3], stats,
    )


def solution(mesh):
    own = mesh.shape["dp"] == 16 and mesh.shape["tensor"] == 2
    rows, both = P(("dp", "tensor"), None), P(("dp", "tensor"))
    split, crossed = P("dp", "tensor"), P("tensor", "dp")
    return jax.shard_map(
        partial(per_device, own),
        mesh=mesh,
        in_specs=(rows, P("dp"), rows, split, split, split, crossed, split, crossed,
                  P("tensor", None), both, both, both, both),
        out_specs=(rows, rows, split, split, split, crossed, split, crossed,
                   P("tensor", None), both, both, both, both, P()),
        check_vma=False,
    )
```
